32 devices in a mesh: dp: 16 (over z, y, core), tensor: 2 (over x).
Axes of the slice: x: 2, y: 2, z: 4, core: 2. Of those that a mesh axis runs over, the one named last changes fastest.
Arguments:
- patches: bfloat16 [37632, 768], P(('dp', 'tensor')), may hold values from -6 to 6
- gain_first: bfloat16 [768], replicated, may hold values from 0.099609375 to 1.8984375
- shift_first: bfloat16 [768], replicated, may hold values from -3 to 3
- attend_weight: bfloat16 [768, 2304], P(None, 'tensor'), may hold values from -0.21875 to 0.21875
- attend_bias: bfloat16 [24, 2, 32], P('tensor'), may hold values from -3 to 3
- offset_table: bfloat16 [24, 169], P('tensor'), may hold values from -5 to 5
- output_weight: bfloat16 [768, 768], P('tensor'), may hold values from -0.625 to 0.625
- output_bias: bfloat16 [768], replicated, may hold values from -3 to 3
- gain_second: bfloat16 [768], replicated, may hold values from 0.099609375 to 1.8984375
- shift_second: bfloat16 [768], replicated, may hold values from -3 to 3
- expand_weight: bfloat16 [768, 3072], P(None, 'tensor'), may hold values from -0.21875 to 0.21875
- expand_bias: bfloat16 [3072], P('tensor'), may hold values from -3 to 3
- reduce_weight: bfloat16 [3072, 768], P('tensor'), may hold values from -0.109375 to 0.109375
- reduce_bias: bfloat16 [768], replicated, may hold values from -3 to 3
- crop_counts: int32 [96], P('dp'), may hold values from 2 to 10, as said below
- cotangent: bfloat16 [37632, 768], P(('dp', 'tensor')), may hold values from -6 to 6
Outputs:
- result: bfloat16 [37632, 768], P(('dp', 'tensor'))
- input_grad: float32 [37632, 768], P(('dp', 'tensor'))
- gain_first_grad: float32 [768], P('tensor')
- shift_first_grad: float32 [768], P('tensor')
- attend_weight_grad: float32 [768, 2304], P(None, 'tensor')
- attend_bias_grad: float32 [24, 2, 32], P('tensor')
- offset_table_grad: float32 [24, 169], P('tensor')
- output_weight_grad: float32 [768, 768], P('tensor')
- output_bias_grad: float32 [768], P('tensor')
- gain_second_grad: float32 [768], P('tensor')
- shift_second_grad: float32 [768], P('tensor')
- expand_weight_grad: float32 [768, 3072], P(None, 'tensor')
- expand_bias_grad: float32 [3072], P('tensor')
- reduce_weight_grad: float32 [3072, 768], P('tensor')
- reduce_bias_grad: float32 [768], P('tensor')
The draws below stay inside these ranges and needn't reach their ends.
Inputs may be any that keep to these rules, and one draw needn't show every extreme that they name: `crop_counts`: in each index of dp the counts of its 6 images sum to exactly 36, so their 2 + count windows fill its 48 window slots in order.
All inputs are finite; a program needn't handle non-finite values.
Results may differ from the reference program's by a relative error of at most 0.02.
Values may be sent and summed in bfloat16 or wider, within the bound.
No kernel may reach another device: no remote copies, remote signals or barrier semaphores. Data moves between devices by JAX's collectives and lax.ppermute only.
A program may use at most 256 MiB of HBM per device.

```python
import jax
import jax.numpy as jnp
from jax import lax

D = 768
HEADS = 24
HEAD_DIM = 32
FF = 3072
IMG_DP = 6
ROWS = 37632
IMAGES = 96
N_DP = 16


def draw_crop_counts(key, part):
    groups = IMAGES // IMG_DP
    half = IMG_DP // 2
    first_key, second_key = jax.random.split(key)
    moves = jax.random.randint(first_key, (groups, half), -4, 5, dtype=jnp.int32)
    places = jnp.arange(half, dtype=jnp.int32)[None, :]
    moves = jnp.where(places == 0, 4, moves)
    values = jnp.concatenate([6 + moves, 6 - moves], axis=1)
    keys = jax.random.split(second_key, groups)
    order = jax.vmap(lambda k: jax.random.permutation(k, IMG_DP))(keys)
    values = jnp.take_along_axis(values, order.astype(jnp.int32), axis=1)
    return values.reshape(-1).astype(jnp.int32)


def block_levels(stream_key, dims, cuts, least, high):
    loudness, own = 1.0, jax.random.fold_in(stream_key, 6)
    for dim, shards_of in cuts:
        heights = jnp.exp(jax.random.uniform(jax.random.fold_in(own, dim), (shards_of,), jnp.float32, least / len(cuts), high / len(cuts)))
        loudness = loudness * jnp.repeat(heights, dims[dim] // shards_of).reshape([-1 if axis == dim else 1 for axis in range(len(dims))])
    return loudness


def scatter_about(rng, extent, deviation, reach, cuts=(), kind=jnp.bfloat16):
    result = deviation * jax.random.normal(rng, extent, jnp.float32)
    if cuts:
        result = result * block_levels(rng, extent, cuts, -0.22, 0.18)
    return jnp.clip(result, -reach, reach).astype(kind)


def setup_inputs(seed: int = 0) -> dict:
    streams_of = jax.random.split(jax.random.key(seed), 17)
    patches = scatter_about(streams_of[0], (ROWS, D), 1.0, 6.0, ((0, 32),))
    gain_first = jnp.clip(1.0 + 0.18 * jax.random.normal(streams_of[1], (D,), jnp.float32), 0.099609375, 1.8984375).astype(jnp.bfloat16)
    shift_first = scatter_about(streams_of[2], (D,), 0.5, 3.0)
    attend_weight = scatter_about(streams_of[3], (D, 3 * D), D ** -0.5, 0.21875, ((1, 2),))
    attend_bias = scatter_about(streams_of[4], (HEADS, 2, HEAD_DIM), 0.5, 3.0, ((0, 2),))
    offset_table = scatter_about(streams_of[5], (HEADS, 169), 1.0, 5.0, ((0, 2),))
    output_weight = scatter_about(streams_of[6], (D, D), (D // 8) ** -0.5, 0.625, ((0, 2),))
    output_bias = scatter_about(streams_of[7], (D,), 0.5, 3.0)
    gain_second = jnp.clip(1.0 + 0.18 * jax.random.normal(streams_of[8], (D,), jnp.float32), 0.099609375, 1.8984375).astype(jnp.bfloat16)
    shift_second = scatter_about(streams_of[9], (D,), 0.5, 3.0)
    expand_weight = scatter_about(streams_of[10], (D, FF), D ** -0.5, 0.21875, ((1, 2),))
    expand_bias = scatter_about(streams_of[11], (FF,), 0.5, 3.0, ((0, 2),))
    reduce_weight = scatter_about(streams_of[12], (FF, D), FF ** -0.5, 0.109375, ((0, 2),))
    reduce_bias = scatter_about(streams_of[13], (D,), 0.5, 3.0)
    crop_counts = draw_crop_counts(jax.random.fold_in(streams_of[16], 71), 0)
    cotangent = scatter_about(streams_of[15], (ROWS, D), 1.0, 6.0, ((0, 32),))
    return {"patches": patches, "gain_first": gain_first, "shift_first": shift_first, "attend_weight": attend_weight, "attend_bias": attend_bias, "offset_table": offset_table, "output_weight": output_weight, "output_bias": output_bias, "gain_second": gain_second, "shift_second": shift_second, "expand_weight": expand_weight, "expand_bias": expand_bias, "reduce_weight": reduce_weight, "reduce_bias": reduce_bias, "crop_counts": crop_counts, "cotangent": cotangent}


@jax.custom_vjp
def low(v):
    return lax.optimization_barrier(v.astype(jnp.bfloat16)).astype(jnp.float32)

@jax.custom_vjp
def low_back(v):
    return v

def low_keep(v):
    return (low(v), None)

def low_pass(kept, grad):
    return (grad,)

def back_keep(v):
    return (v, None)

def back_low(kept, grad):
    return (low(grad),)
low.defvjp(low_keep, low_pass)
low_back.defvjp(back_keep, back_low)
HIGH = lax.Precision.HIGHEST
EPSILON = 1e-05
MASKED = 30000.0
SIDE = 7

def window_live(counts, slots):
    totals = counts + 2
    ends = jnp.cumsum(totals, dtype=jnp.int32)
    starts = ends - totals
    places = jnp.arange(slots, dtype=jnp.int32)[:, None]
    inside = (places >= starts[None, :]) & (places < ends[None, :])
    offset = lax.optimization_barrier(jnp.sum(jnp.where(inside, places - starts[None, :], 0), axis=1, dtype=jnp.int32))
    present = jnp.any(inside, axis=1)
    spots = jnp.arange(SIDE * SIDE, dtype=jnp.int32)
    corner = (spots // SIDE < 3) & (spots % SIDE < 3)
    whole = present & (offset < 2)
    partial_win = present & (offset >= 2)
    alive = whole[:, None] | partial_win[:, None] & corner[None, :]
    return alive.astype(jnp.float32)

def offset_index():
    spots = jnp.arange(SIDE * SIDE, dtype=jnp.int32)
    row_of = spots // SIDE
    col_of = spots % SIDE
    return ((row_of[:, None] - row_of[None, :] + SIDE - 1) * (2 * SIDE - 1) + col_of[:, None] - col_of[None, :] + SIDE - 1).astype(jnp.int32)

def norm_rows(values, gain, shift):
    mean = lax.optimization_barrier(jnp.mean(values, axis=1, keepdims=True))
    centred = values - mean
    scale = lax.rsqrt(lax.optimization_barrier(jnp.mean(centred * centred, axis=1, keepdims=True)) + EPSILON)
    return centred * scale * gain + shift

def block_forward(rows, params, alive, index):
    gain_first, shift_first, attend_weight, attend_bias, offset_table, output_weight, output_bias, gain_second, shift_second, expand_weight, expand_bias, reduce_weight, reduce_bias = params
    windows = alive.shape[0]
    keep = alive.reshape(-1, 1)
    first = low(norm_rows(rows, gain_first, shift_first))
    blank = jnp.zeros_like(attend_bias[:, 0])
    bias_row = jnp.stack([attend_bias[:, 0], blank, attend_bias[:, 1]], axis=1).reshape(-1)
    packed = low_back(jnp.dot(first, attend_weight, precision=HIGH) + bias_row)
    packed = packed.reshape(windows, SIDE * SIDE, HEADS, 3, HEAD_DIM)
    query = low(packed[..., 0, :] * HEAD_DIM ** (-0.5))
    key = low(packed[..., 1, :])
    value = low(packed[..., 2, :])
    relative = offset_table[:, index]
    masking = (alive - 1.0) * MASKED
    scores = low_back(jnp.einsum('wihd,wjhd->whij', query, key, precision=HIGH) + relative[None] + masking[:, None, None, :])
    peak = lax.optimization_barrier(jnp.max(scores, axis=3, keepdims=True))
    expo = jnp.exp(scores - peak)
    probs = low(expo / lax.optimization_barrier(jnp.sum(expo, axis=3, keepdims=True)))
    mixed = low_back(low(jnp.einsum('whij,wjhd->wihd', probs, value, precision=HIGH)))
    mixed = mixed.reshape(windows * SIDE * SIDE, HEADS * HEAD_DIM)
    attended = low_back(jnp.dot(mixed, output_weight, precision=HIGH))
    middle = rows + keep * (attended + output_bias)
    second = low(norm_rows(middle, gain_second, shift_second))
    hidden_pre = low_back(jnp.dot(second, expand_weight, precision=HIGH) + expand_bias)
    hidden = low(jax.nn.gelu(hidden_pre, approximate=False))
    reduced = low_back(jnp.dot(hidden, reduce_weight, precision=HIGH))
    return middle + keep * (reduced + reduce_bias)

def reference(patches, gain_first, shift_first, attend_weight, attend_bias, offset_table, output_weight, output_bias, gain_second, shift_second, expand_weight, expand_bias, reduce_weight, reduce_bias, crop_counts, cotangent):
    params = tuple((p.astype(jnp.float32) for p in (gain_first, shift_first, attend_weight, attend_bias, offset_table, output_weight, output_bias, gain_second, shift_second, expand_weight, expand_bias, reduce_weight, reduce_bias)))
    live = jax.vmap(lambda c: window_live(c, 8 * IMG_DP))(crop_counts.reshape(N_DP, IMG_DP))
    live = live.reshape(-1, 8, SIDE * SIDE)
    index = offset_index()
    rows = patches.astype(jnp.float32).reshape(-1, 8 * SIDE * SIDE, D)
    grads_in = cotangent.astype(jnp.float32).reshape(-1, 8 * SIDE * SIDE, D)
    zeros = tuple((jnp.zeros_like(p) for p in params))

    def step(totals, args):
        block, grad, alive = args
        out, pull = jax.vjp(lambda r, p: block_forward(r, p, alive, index), block, params)
        row_grad, param_grads = pull(grad)
        return (tuple((a + b for a, b in zip(totals, param_grads))), (out.astype(jnp.bfloat16), row_grad))
    totals, (outs, row_grads) = lax.scan(step, zeros, (rows, grads_in, live))
    return (outs.reshape(ROWS, D), row_grads.reshape(ROWS, D), totals[0], totals[1], totals[2], totals[3], totals[4], totals[5], totals[6], totals[7], totals[8], totals[9], totals[10], totals[11], totals[12])
```

```python
from functools import partial

import jax
import jax.numpy as jnp
import numpy as np
from jax import lax
from jax.experimental import pallas as pl
from jax.experimental.pallas import tpu as pltpu
from jax.sharding import Mesh
from jax.sharding import PartitionSpec as P

HEAD_DIM = 32
EPSILON = 1e-05
MASKED = 30000.0
SIDE = 7
SLOTS = SIDE * SIDE
BLK = 128
GROUP = 4
GW = 3 * GROUP * HEAD_DIM
BF = jnp.bfloat16
F32 = jnp.float32
VMEM_LIMIT = 60 * 1024 * 1024


def dot(a, b):
    return jnp.dot(a, b, preferred_element_type=F32)


def dot_nt(a, b):
    return lax.dot_general(a, b, (((1,), (1,)), ((), ())), preferred_element_type=F32)


def dot_tn(a, b):
    return lax.dot_general(a, b, (((0,), (0,)), ((), ())), preferred_element_type=F32)


def kind_tables():
    slot = -np.ones((2, BLK), np.int64)
    owner = 100 + np.arange(BLK)[None].repeat(2, 0)
    nine = np.arange(9)
    nine = (nine // 3) * SIDE + nine % 3
    for w in range(2):
        slot[0, w * SLOTS : (w + 1) * SLOTS] = np.arange(SLOTS)
        owner[0, w * SLOTS : (w + 1) * SLOTS] = w
    for w in range(3):
        at = 2 * SLOTS + 9 * w
        slot[0, at : at + 9] = nine
        owner[0, at : at + 9] = 2 + w
    for w in range(14):
        slot[1, 9 * w : 9 * w + 9] = nine
        owner[1, 9 * w : 9 * w + 9] = w
    pick = (slot[:, :, None] == np.arange(64)[None, None, :]).astype(np.float32)
    same = owner[:, :, None] == owner[:, None, :]
    mask = np.where(same, 0.0, -1e30).astype(np.float32)
    return pick, mask


def group_perm():
    perm = np.zeros((GW, GW), np.float32)
    for h in range(GROUP):
        for p in range(3):
            for e in range(HEAD_DIM):
                perm[(h * 3 + p) * HEAD_DIM + e, (p * GROUP + h) * HEAD_DIM + e] = 1.0
    return perm


def offset_codes():
    spots = np.arange(SLOTS)
    r, c = spots // SIDE, spots % SIDE
    return (r[None, :] - r[:, None] + SIDE - 1) * (2 * SIDE - 1) + c[None, :] - c[:, None] + SIDE - 1


def row_map(counts, windows, first_window, bad, blocks):
    totals = counts + 2
    ends = jnp.cumsum(totals, dtype=jnp.int32)
    starts = ends - totals
    place = first_window + jnp.arange(windows, dtype=jnp.int32)
    inside = (place[:, None] >= starts[None]) & (place[:, None] < ends[None])
    offset = jnp.sum(jnp.where(inside, place[:, None] - starts[None], 0), axis=1)
    present = jnp.any(inside, axis=1)
    whole = present & (offset < 2)
    full = present & (whole | bad)
    part = present & ~full
    fr = jnp.cumsum(full.astype(jnp.int32)) - 1
    pr = jnp.cumsum(part.astype(jnp.int32)) - 1
    nfull = fr[-1] + 1
    npart = pr[-1] + 1
    n0 = (nfull + 1) // 2
    n1 = (jnp.maximum(npart - 3 * n0, 0) + 13) // 14
    r = np.arange(BLK)
    b = jnp.arange(blocks, dtype=jnp.int32)[:, None]
    is_full0 = jnp.asarray(r < 2 * SLOTS)[None]
    full_rank = 2 * b + jnp.asarray(np.minimum(r // SLOTS, 1), jnp.int32)[None]
    nine0 = np.clip(r - 2 * SLOTS, 0, 26)
    part_rank0 = 3 * b + jnp.asarray(nine0 // 9, jnp.int32)[None]
    pad0 = jnp.asarray(r >= 2 * SLOTS + 27)[None]
    nine1 = np.clip(r, 0, 125)
    part_rank1 = 3 * n0 + 14 * (b - n0) + jnp.asarray(nine1 // 9, jnp.int32)[None]
    pad1 = jnp.asarray(r >= 126)[None]
    corner = lambda s: (s % 9 // 3) * SIDE + s % 3
    kind0 = b < n0
    want_full = kind0 & is_full0
    rank = jnp.where(want_full, full_rank, jnp.where(kind0, part_rank0, part_rank1))
    slot = jnp.where(
        kind0,
        jnp.asarray(np.where(r < 2 * SLOTS, r % SLOTS, corner(nine0)), jnp.int32)[None],
        jnp.asarray(corner(nine1), jnp.int32)[None],
    )
    pad = jnp.where(kind0, pad0, pad1) | (b >= n0 + n1)
    win = jnp.arange(windows, dtype=jnp.int32)
    key = jnp.where(full, fr, jnp.where(part, pr + 1000, 100000))
    goal = jnp.where(want_full, rank, rank + 1000)
    goal = jnp.where(pad, -1, goal)
    hit = goal[:, :, None] == key[None, None, :]
    found = jnp.any(hit, axis=2)
    window = jnp.sum(jnp.where(hit, win[None, None], 0), axis=2)
    is_whole = jnp.any(hit & whole[None, None], axis=2)
    in_corner = (slot // SIDE < 3) & (slot % SIDE < 3)
    live = found & (is_whole | in_corner)
    index = jnp.where(found, window * SLOTS + slot, -1)
    return index.reshape(-1), live.reshape(-1), n0 + n1, n0


def norm_stats(x):
    mean = jnp.mean(x, axis=1, keepdims=True)
    c = x - mean
    scale = lax.rsqrt(jnp.mean(c * c, axis=1, keepdims=True) + EPSILON)
    return c * scale, scale


def norm_back(grad, normal, scale, gain):
    inner = grad * gain
    mean = jnp.mean(inner, axis=1, keepdims=True)
    proj = jnp.mean(inner * normal, axis=1, keepdims=True)
    return scale * (inner - mean - normal * proj)


def gather_kernel(meta, idx, live, patches, cot, g1, b1, xc, cotc, branch, first):
    rows = idx.shape[0]
    total = patches.shape[0]
    spots = lax.broadcasted_iota(jnp.int32, (BLK, total), 1)

    def one(b, carry):
        at = pl.ds(pl.multiple_of(b * BLK, BLK), BLK)
        pick = (spots == idx[at, :]).astype(F32).astype(BF)
        x = dot(pick, patches[...])
        up = dot(pick, cot[...])
        xc[at, :] = x.astype(BF)
        cotc[at, :] = up.astype(BF)
        branch[at, :] = (up * live[at, :]).astype(BF)
        n, _ = norm_stats(x)
        first[at, :] = (n * g1[...] + b1[...]).astype(BF)
        return carry

    lax.fori_loop(0, rows // BLK, one, 0)


def lane_head(shape, axis):
    return lax.broadcasted_iota(jnp.int32, shape, axis) // HEAD_DIM


def spread_rows(x):
    h = lane_head(x.shape, 1)
    zero = jnp.zeros_like(x)
    return jnp.concatenate([jnp.where(h == i, x, zero) for i in range(GROUP)], axis=0)


def spread_cols(xt):
    h = lane_head(xt.shape, 0)
    zero = jnp.zeros_like(xt)
    return jnp.concatenate([jnp.where(h == i, xt, zero) for i in range(GROUP)], axis=1)


def fold_rows(x):
    h = lane_head((BLK, BLK), 1)
    out = x[0:BLK]
    for i in range(1, GROUP):
        out = jnp.where(h == i, x[i * BLK : (i + 1) * BLK], out)
    return out


def attend_kernel(shards, meta, live, xc, first, perm, pick, mask, g2, b2, ob, *rest):
    n = shards
    w, bias, rel, w_out = (rest[i * n : (i + 1) * n] for i in range(4))
    qkv, probs, mixed, middle, second = rest[4 * n : 4 * n + 5]
    table, att = rest[4 * n + 5 :]
    rows = xc.shape[0]
    blocks = rows // BLK
    chunk = pl.program_id(0)
    per = w[0].shape[1] // GW
    groups = per * n

    @pl.when(chunk == 0)
    def _():
        for s in range(n):
            for kind in range(2):
                e = pick[kind]
                half = dot_nt(rel[s][...], e).astype(BF)
                for h in range(per * GROUP):
                    t = dot(e, half[h * 64 : (h + 1) * 64])
                    t = t + mask[kind].astype(F32)
                    table[kind, s * per + h // GROUP, (h % GROUP) * BLK : (h % GROUP + 1) * BLK, :] = t.astype(BF)

    for s in range(n):
        for g in range(per):
            c = slice(g * GW, (g + 1) * GW)
            v = dot(first[...], w[s][:, c]) + bias[s][:, c]
            col = lax.broadcasted_iota(jnp.int32, (1, GW), 1)
            scale = jnp.where(col // HEAD_DIM % 3 == 0, HEAD_DIM**-0.5, 1.0)
            v = (v * scale).astype(BF)
            at = s * per + g
            qkv[:, at * GW : (at + 1) * GW] = dot(v, perm[...]).astype(BF)

    n0 = meta[1]
    for g in range(groups):
        def one(b, carry):
            at = pl.ds(pl.multiple_of(b * BLK, BLK), BLK)
            kind = jnp.where(chunk * blocks + b < n0, 0, 1)
            base = g * GW
            q = qkv[at, base : base + BLK]
            k = qkv[at, base + BLK : base + 2 * BLK]
            v = qkv[at, base + 2 * BLK : base + 3 * BLK]
            st = dot_nt(spread_rows(k), q) + table[kind, g].astype(F32)
            dead = (live[at, :] - 1.0) * MASKED
            st = st.reshape(GROUP, BLK, BLK) + jnp.where(meta[3] > 0, dead, 0.0)[None]
            peak = jnp.max(st, axis=1, keepdims=True)
            e = jnp.exp(st - peak)
            p = (e * (1.0 / jnp.sum(e, axis=1, keepdims=True))).astype(BF)
            p = p.reshape(GROUP * BLK, BLK)
            probs[b, g] = p
            vt = v.astype(F32).T.astype(BF)
            mt = dot(spread_cols(vt), p)
            mixed[at, g * BLK : (g + 1) * BLK] = mt.T.astype(BF)
            return carry

        lax.fori_loop(0, blocks, one, 0)

    wide = per * BLK
    total = dot(mixed[:, 0:wide], w_out[0][...])
    for s in range(1, n):
        total = total + dot(mixed[:, s * wide : (s + 1) * wide], w_out[s][...])
    att[...] = total

    def tail(b, carry):
        at = pl.ds(pl.multiple_of(b * BLK, BLK), BLK)
        m = xc[at, :].astype(F32) + live[at, :] * (att[at, :] + ob[...])
        middle[at, :] = m
        nrm, _ = norm_stats(m)
        second[at, :] = (nrm * g2[...] + b2[...]).astype(BF)
        return carry

    lax.fori_loop(0, blocks, tail, 0)


def feed_kernel(tiles, carried, meta, second, branch, we, wr, be, *rest):
    if carried:
        red_in, sg_in = rest[:2]
        rest = rest[2:]
    dwe, dwr, dbe, red, sg = rest[:5]
    red_acc, sg_acc = rest[5:]
    t, c = pl.program_id(0), pl.program_id(1)
    u = dot(second[...], we[...]) + be[...]
    cdf = 0.5 * (1.0 + lax.erf(u * 0.7071067811865476))
    h = (u * cdf).astype(BF)
    slope = cdf + u * (jnp.exp(-0.5 * u * u) * 0.3989422804014327)
    pg = (dot_nt(branch[...], wr[...]) * slope).astype(BF)
    grad_r = dot_tn(h, branch[...])
    grad_e = dot_tn(second[...], pg)
    grad_b = jnp.sum(pg.astype(F32), axis=0, keepdims=True)
    red_t = dot(h, wr[...])
    sg_t = dot_nt(pg, we[...])

    @pl.when(c == 0)
    def _():
        dwr[...] = grad_r.astype(BF)
        dwe[...] = grad_e.astype(BF)
        dbe[...] = grad_b

    @pl.when(c > 0)
    def _():
        dwr[...] = (dwr[...].astype(F32) + grad_r).astype(BF)
        dwe[...] = (dwe[...].astype(F32) + grad_e).astype(BF)
        dbe[...] = dbe[...] + grad_b

    @pl.when(t == 0)
    def _():
        if carried:
            red_acc[c] = red_in[...] + red_t
            sg_acc[c] = sg_in[...] + sg_t
        else:
            red_acc[c] = red_t
            sg_acc[c] = sg_t

    @pl.when(t > 0)
    def _():
        red_acc[c] = red_acc[c] + red_t
        sg_acc[c] = sg_acc[c] + sg_t

    @pl.when(t == tiles - 1)
    def _():
        red[...] = red_acc[c]
        sg[...] = sg_acc[c]


def back_kernel(shards, meta, live, middle, sg, cotc, g2, perm, pick, pick_t, qkv, probs, mixed, first, *rest):
    n = shards
    w_out = rest[:n]
    mg, dqkv, vec = rest[n : n + 3]
    dwo = rest[n + 3 : 2 * n + 3]
    dwa = rest[2 * n + 3 : 3 * n + 3]
    dba = rest[3 * n + 3 : 4 * n + 3]
    drel = rest[4 * n + 3 : 5 * n + 3]
    ag, dmix, dperm, table = rest[5 * n + 3 :]
    rows = middle.shape[0]
    blocks = rows // BLK
    chunk = pl.program_id(0)
    per = dwa[0].shape[1] // GW
    wide = per * BLK
    n0 = meta[1]

    @pl.when(chunk == 0)
    def _():
        vec[...] = jnp.zeros_like(vec)
        table[...] = jnp.zeros_like(table)

    def head(b, carry):
        at = pl.ds(pl.multiple_of(b * BLK, BLK), BLK)
        nrm, scale = norm_stats(middle[at, :])
        g = sg[at, :]
        m = cotc[at, :].astype(F32) + norm_back(g, nrm, scale, g2[...])
        mg[at, :] = m
        kept = m * live[at, :]
        ag[at, :] = kept.astype(BF)
        vec[0:1, :] = vec[0:1, :] + jnp.sum(g * nrm, axis=0, keepdims=True)
        vec[1:2, :] = vec[1:2, :] + jnp.sum(g, axis=0, keepdims=True)
        vec[2:3, :] = vec[2:3, :] + jnp.sum(kept, axis=0, keepdims=True)
        return carry

    lax.fori_loop(0, blocks, head, 0)

    def put(ref, value):
        @pl.when(chunk == 0)
        def _():
            ref[...] = value.astype(ref.dtype)

        @pl.when(chunk > 0)
        def _():
            ref[...] = (ref[...].astype(F32) + value).astype(ref.dtype)

    for s in range(n):
        dmix[:, s * wide : (s + 1) * wide] = dot_nt(ag[...], w_out[s][...]).astype(BF)
        put(dwo[s], dot_tn(mixed[:, s * wide : (s + 1) * wide], ag[...]))

    for g in range(per * n):
        def one(b, carry):
            at = pl.ds(pl.multiple_of(b * BLK, BLK), BLK)
            kind = jnp.where(chunk * blocks + b < n0, 0, 1)
            base = g * GW
            q = qkv[at, base : base + BLK]
            k = qkv[at, base + BLK : base + 2 * BLK]
            v = qkv[at, base + 2 * BLK : base + 3 * BLK]
            do = dmix[at, g * BLK : (g + 1) * BLK]
            p = probs[b, g]
            dp = dot_nt(spread_rows(v), do).reshape(GROUP, BLK, BLK)
            pf = p.astype(F32).reshape(GROUP, BLK, BLK)
            x = pf * dp
            ds = x - pf * jnp.sum(x, axis=1, keepdims=True)
            ds = ds.astype(BF).reshape(GROUP * BLK, BLK)
            table[kind, g] = table[kind, g] + ds.astype(F32)
            dv = fold_rows(dot(p, do))
            dk = fold_rows(dot(ds, q))
            kt = k.astype(F32).T.astype(BF)
            dq = (dot(spread_cols(kt), ds) * HEAD_DIM**-0.5).T
            dperm[at, 0:BLK] = dq.astype(BF)
            dperm[at, BLK : 2 * BLK] = dk.astype(BF)
            dperm[at, 2 * BLK : 3 * BLK] = dv.astype(BF)
            return carry

        lax.fori_loop(0, blocks, one, 0)
        dqkv[:, g * GW : (g + 1) * GW] = dot_nt(dperm[...], perm[...]).astype(BF)

    for s in range(n):
        for g in range(per):
            c = slice(g * GW, (g + 1) * GW)
            at = s * per + g
            d = dqkv[:, at * GW : (at + 1) * GW]
            put(dwa[s].at[:, c], dot_tn(first[...], d))
            put(dba[s].at[:, c], jnp.sum(d.astype(F32), axis=0, keepdims=True))

    @pl.when(chunk == meta[2] - 1)
    def _():
        for s in range(n):
            for h in range(per * GROUP):
                total = jnp.zeros((64, 64), F32)
                for kind in range(2):
                    a = table[kind, s * per + h // GROUP, (h % GROUP) * BLK : (h % GROUP + 1) * BLK, :]
                    a = dot(a.astype(BF), pick[kind]).astype(BF)
                    total = total + dot(pick_t[kind], a)
                drel[s][h * 64 : (h + 1) * 64, :] = total


def row_tiles(rows, size=384):
    return [(a, min(size, rows - a)) for a in range(0, rows, size)]


def finish_kernel(shards, meta, idx, live, xc, cotc, middle, red, mg, dqkv, g1, rb, patches, cot, *rest):
    n = shards
    w = rest[:n]
    result, input_grad, vec = rest[n : n + 3]
    fg, res, hi, lo = rest[n + 3 :]
    rows = xc.shape[0]
    blocks = rows // BLK
    chunk = pl.program_id(0)
    width = w[0].shape[1]

    @pl.when(chunk == 0)
    def _():
        vec[...] = jnp.zeros_like(vec)

    total = dot_nt(dqkv[:, 0:width], w[0][...])
    for s in range(1, n):
        total = total + dot_nt(dqkv[:, s * width : (s + 1) * width], w[s][...])
    fg[...] = total

    def one(b, carry):
        at = pl.ds(pl.multiple_of(b * BLK, BLK), BLK)
        keep = live[at, :]
        nrm, scale = norm_stats(xc[at, :].astype(F32))
        g = fg[at, :]
        up = cotc[at, :].astype(F32)
        delta = mg[at, :] - up + norm_back(g, nrm, scale, g1[...])
        top = delta.astype(BF)
        hi[at, :] = top
        lo[at, :] = (delta - top.astype(F32)).astype(BF)
        res[at, :] = (middle[at, :] + keep * (red[at, :] + rb[...])).astype(BF)
        vec[0:1, :] = vec[0:1, :] + jnp.sum(g * nrm, axis=0, keepdims=True)
        vec[1:2, :] = vec[1:2, :] + jnp.sum(g, axis=0, keepdims=True)
        vec[2:3, :] = vec[2:3, :] + jnp.sum(up * keep, axis=0, keepdims=True)
        return carry

    lax.fori_loop(0, blocks, one, 0)

    for start, size in row_tiles(patches.shape[0]):
        at = slice(start, start + size)
        spots = start + lax.broadcasted_iota(jnp.int32, (size, rows), 0)
        hit = (spots == idx[...].reshape(1, rows)).astype(F32)
        here = jnp.sum(hit, axis=1, keepdims=True) > 0.0
        put = hit.astype(BF)
        new = dot(put, res[...]).astype(BF)
        grad = dot(put, hi[...]) + dot(put, lo[...])

        @pl.when(chunk == 0)
        def _():
            result[at, :] = jnp.where(here, new.astype(F32), patches[at, :].astype(F32)).astype(BF)
            input_grad[at, :] = cot[at, :].astype(F32) + grad

        @pl.when(chunk > 0)
        def _():
            result[at, :] = jnp.where(here, new.astype(F32), result[at, :].astype(F32)).astype(BF)
            input_grad[at, :] = input_grad[at, :] + grad


def guarded(body, axis):
    def run(meta, *refs):
        @pl.when(pl.program_id(axis) < meta[2])
        def _():
            body(meta, *refs)

    return run


def clamp(i, meta):
    return jnp.minimum(i, meta[2] - 1)


def whole_spec(shape):
    zeros = (0,) * len(shape)
    return pl.BlockSpec(shape, lambda *_: zeros, pipeline_mode=pl.Buffered(1))


def chunk_spec(shape):
    zeros = (0,) * (len(shape) - 1)
    return pl.BlockSpec(shape, lambda i, meta: (clamp(i, meta),) + zeros)


def sds(shape, dtype):
    return jax.ShapeDtypeStruct(shape, dtype)


def params(**kw):
    return pltpu.CompilerParams(vmem_limit_bytes=VMEM_LIMIT, **kw)


class Local:
    def __init__(self, rows, shards, width, hidden):
        self.rows = rows
        self.windows = rows // SLOTS
        worst = (self.windows + 1) // 2
        self.per_chunk = min(5, max(worst, 1))
        self.chunks = -(-worst // self.per_chunk)
        self.ch = self.per_chunk * BLK
        self.all = self.ch * self.chunks
        self.shards = shards
        self.per = width // GW
        self.hidden = hidden
        pick, mask = kind_tables()
        self.pick = jnp.asarray(pick, BF)
        self.pick_t = jnp.asarray(pick.transpose(0, 2, 1), BF)
        self.mask = jnp.asarray(mask, BF)
        self.perm = jnp.asarray(group_perm(), BF)

    def layout(self, counts, first_window, bad):
        index, live, nb, n0 = row_map(counts, self.windows, first_window, bad, self.per_chunk * self.chunks)
        nch = jnp.maximum((nb + self.per_chunk - 1) // self.per_chunk, 1)
        self.nch = nch.astype(jnp.int32)
        zero = jnp.zeros((), jnp.int32)
        meta = jnp.stack([nb, n0, nch, bad.astype(jnp.int32), zero, zero, zero, zero]).astype(jnp.int32)
        self.meta = meta
        self.idx_col = index.reshape(-1, 1)
        self.idx_row = index.reshape(self.chunks, 1, self.ch)
        self.live = live.astype(F32).reshape(-1, 1)

    def call(self, body, ins, outs, scratch=(), grid=None, **kw):
        grid = (self.chunks,) if grid is None else grid
        f = pl.pallas_call(
            guarded(body, len(grid) - 1),
            out_shape=[o for o, _ in outs],
            grid_spec=pltpu.PrefetchScalarGridSpec(
                num_scalar_prefetch=1,
                grid=grid,
                in_specs=[s for _, s in ins],
                out_specs=[s for _, s in outs],
                scratch_shapes=list(scratch),
            ),
            compiler_params=params(),
            **kw,
        )
        return f(self.meta, *[a for a, _ in ins])

    def cost(self, flops, read):
        return pl.CostEstimate(flops=int(flops), bytes_accessed=int(read), transcendentals=0)

    def gather(self, patches, cot, g1, b1):
        ch, d = self.ch, patches.shape[1]
        w = lambda a: (a, whole_spec(a.shape))
        row = lambda dt: (sds((self.all, d), dt), chunk_spec((ch, d)))
        col = lambda a: (a, chunk_spec((ch, 1)))
        return self.call(
            gather_kernel,
            [col(self.idx_col), col(self.live), w(patches), w(cot), w(g1), w(b1)],
            [row(BF), row(BF), row(BF), row(BF)],
            name="gather_rows",
            cost_estimate=self.cost(4 * ch * self.rows * d, 8 * self.rows * d),
        )

    def attend(self, xc, first, g2, b2, ob, ws, biases, rels, wos):
        ch, d = self.ch, xc.shape[1]
        w = lambda a: (a, whole_spec(a.shape))
        c = lambda a: (a, chunk_spec((ch,) + a.shape[1:]))
        row = lambda k, dt: (sds((self.all, k), dt), chunk_spec((ch, k)))
        groups = self.per * self.shards
        probs = (
            sds((self.per_chunk * self.chunks, groups, GROUP * BLK, BLK), BF),
            chunk_spec((self.per_chunk, groups, GROUP * BLK, BLK)),
        )
        return self.call(
            partial(attend_kernel, self.shards),
            [c(self.live), c(xc), c(first), w(self.perm), w(self.pick), w(self.mask), w(g2), w(b2), w(ob)]
            + [w(a) for a in (*ws, *biases, *rels, *wos)],
            [row(groups * GW, BF), probs, row(d, BF), row(d, F32), row(d, BF)],
            [pltpu.VMEM((2, groups, GROUP * BLK, BLK), BF), pltpu.VMEM((ch, d), F32)],
            name="attend",
            cost_estimate=self.cost(10 * ch * d * d, 20 * ch * d),
        )

    def feed(self, second, branch, we, wr, be, carry=None, tile=256):
        ch, d = self.ch, second.shape[1]
        hidden = we.shape[1]
        if hidden % tile:
            tile = 128
        tiles = hidden // tile
        c = lambda a: (a, pl.BlockSpec((ch, a.shape[1]), lambda t, i, meta: (clamp(i, meta), 0)))
        last = tiles - 1
        acc = (sds((self.all, d), F32), pl.BlockSpec((ch, d), lambda t, i, meta: (jnp.where(t == last, clamp(i, meta), 0), 0)))
        cols = lambda a: pl.BlockSpec((a, tile), lambda t, i, *_: (0, t))
        rws = pl.BlockSpec((tile, d), lambda t, i, *_: (t, 0))
        ins = [c(second), c(branch), (we, cols(d)), (wr, rws), (be, cols(1))]
        if carry is not None:
            ins += [c(a) for a in carry]
        return self.call(
            partial(feed_kernel, tiles, carry is not None),
            ins,
            [(sds((d, hidden), BF), cols(d)), (sds((hidden, d), BF), rws), (sds((1, hidden), F32), cols(1)), acc, acc],
            [pltpu.VMEM((self.chunks, ch, d), F32), pltpu.VMEM((self.chunks, ch, d), F32)],
            grid=(tiles, self.chunks),
            name="feed",
            cost_estimate=self.cost(12 * ch * d * hidden, 8 * d * hidden),
        )

    def back(self, middle, sg, cotc, g2, qkv, probs, mixed, first, wos):
        ch, d, n = self.ch, middle.shape[1], self.shards
        w = lambda a: (a, whole_spec(a.shape))
        c = lambda a: (a, chunk_spec((ch,) + a.shape[1:]))
        row = lambda k, dt: (sds((self.all, k), dt), chunk_spec((ch, k)))
        o = lambda shape, dt: (sds(shape, dt), whole_spec(shape))
        groups = self.per * n
        pspec = (probs, chunk_spec((self.per_chunk,) + probs.shape[1:]))
        width, wide = self.per * GW, self.per * BLK
        return self.call(
            partial(back_kernel, n),
            [c(self.live), c(middle), c(sg), c(cotc), w(g2), w(self.perm), w(self.pick), w(self.pick_t)]
            + [c(qkv), pspec, c(mixed), c(first)]
            + [w(a) for a in wos],
            [row(d, F32), row(groups * GW, BF), o((8, d), F32)]
            + [o((wide, d), BF)] * n
            + [o((d, width), BF)] * n
            + [o((1, width), F32)] * n
            + [o((self.per * GROUP * 64, 64), F32)] * n,
            [
                pltpu.VMEM((ch, d), BF),
                pltpu.VMEM((ch, groups * BLK), BF),
                pltpu.VMEM((ch, GW), BF),
                pltpu.VMEM((2, groups, GROUP * BLK, BLK), F32),
            ],
            name="back",
            cost_estimate=self.cost(14 * ch * d * d, 30 * ch * d),
        )

    def finish(self, xc, cotc, middle, red, mg, dqkv, g1, rb, patches, cot, ws):
        ch, d = self.ch, xc.shape[1]
        w = lambda a: (a, whole_spec(a.shape))
        c = lambda a: (a, chunk_spec((ch,) + a.shape[1:]))
        o = lambda shape, dt: (sds(shape, dt), whole_spec(shape))
        rspec = (self.idx_row, pl.BlockSpec((1, 1, ch), lambda i, meta: (clamp(i, meta), 0, 0)))
        return self.call(
            partial(finish_kernel, self.shards),
            [rspec, c(self.live), c(xc), c(cotc), c(middle), c(red), c(mg), c(dqkv), w(g1), w(rb), w(patches), w(cot)]
            + [w(a) for a in ws],
            [o(patches.shape, BF), o(patches.shape, F32), o((8, d), F32)],
            [pltpu.VMEM((ch, d), F32), pltpu.VMEM((ch, d), BF), pltpu.VMEM((ch, d), BF), pltpu.VMEM((ch, d), BF)],
            name="finish",
            cost_estimate=self.cost(10 * ch * d * d, 30 * ch * d),
        )


def relative_rows(table):
    codes = np.full((64, 64), -1)
    codes[:SLOTS, :SLOTS] = offset_codes()
    select = jnp.asarray((codes.reshape(1, -1) == np.arange(169)[:, None]).astype(np.float32), BF)
    out = jnp.dot(table, select, preferred_element_type=F32).astype(BF)
    return out.reshape(-1, 64)


def relative_back(grad):
    codes = np.full((64, 64), -1)
    codes[:SLOTS, :SLOTS] = offset_codes()
    select = jnp.asarray((codes.reshape(-1, 1) == np.arange(169)[None]).astype(np.float32), BF)
    return jnp.dot(grad.reshape(-1, 64 * 64).astype(BF), select, preferred_element_type=F32)


def bias_row(bias):
    b = bias.astype(F32)
    return jnp.stack([b[:, 0], jnp.zeros_like(b[:, 0]), b[:, 1]], axis=1).reshape(1, -1)


def score_bound(w, bias):
    gram = lax.dot_general(w, w, (((0,), (0,)), ((), ())), preferred_element_type=F32)
    blk = np.arange(w.shape[1]) // HEAD_DIM
    same = jnp.asarray(blk)[:, None] == jnp.asarray(blk)[None, :]
    sums = jnp.sum(jnp.where(same, gram * gram, 0.0), axis=0)
    part = jnp.asarray(blk % 3)
    fourth = HEAD_DIM * jnp.stack([jnp.max(jnp.where(part == p, sums, 0.0)) for p in range(2)])
    norm = jnp.sqrt(jnp.sqrt(fourth))
    qb = jnp.sqrt(jnp.max(jnp.sum(bias[:, 0].astype(F32) ** 2, axis=1)))
    return jnp.concatenate([norm, qb[None]]) * 1.01


def dead_matter(bounds, table_max, gain, shift):
    d = gain.shape[0]
    reach = 1.01 * (np.sqrt(d) * jnp.max(jnp.abs(gain)) + jnp.sqrt(jnp.sum(shift * shift)))
    q = (reach * bounds[0] + bounds[2]) * HEAD_DIM**-0.5
    top = q * reach * bounds[1] + table_max
    return ~(2.0 * top < MASKED - 500.0)


def halves(a, bit):
    n = a.shape[0] // 2
    return lax.dynamic_slice_in_dim(a, bit * n, n, 0), lax.dynamic_slice_in_dim(a, (1 - bit) * n, n, 0)


def join(a, r, bit):
    return jnp.where(bit == 0, jnp.concatenate([a, r], 0), jnp.concatenate([r, a], 0))


def swap(a, axis, n, step=1):
    return lax.ppermute(a, axis, [(i, i ^ step) for i in range(n)])


def add_halves(a, bit, axis, n, step=1):
    keep, send = halves(a, bit)
    return (keep.astype(F32) + swap(send, axis, n, step).astype(F32)).astype(BF)


def on_device(
    nz,
    nt,
    patches,
    gain_first,
    shift_first,
    attend_weight,
    attend_bias,
    offset_table,
    output_weight,
    output_bias,
    gain_second,
    shift_second,
    expand_weight,
    expand_bias,
    reduce_weight,
    reduce_bias,
    crop_counts,
    cotangent,
):
    fast = nt == 2 and nz == 4
    t, c, y, z = (lax.axis_index(a) for a in ("tensor", "core", "y", "z"))
    rows, d = patches.shape
    windows = rows // SLOTS
    vec = lambda a: a.astype(F32).reshape(1, -1)
    bound = score_bound(attend_weight, attend_bias)
    own_max = jnp.max(jnp.abs(offset_table.astype(F32)))
    bound = jnp.concatenate([bound, own_max[None]])

    if fast:
        def fetch(a):
            half, _ = halves(a, c)
            got = swap(half, "tensor", nt)
            return [a, join(got, swap(got, "core", 2), c)]

        small = lambda a: [a, swap(a, "tensor", nt)]
        both = lambda a: jnp.maximum(a, swap(a, "tensor", nt))
        w_att = fetch(attend_weight)
        w_out = fetch(output_weight)
        w_exp = fetch(expand_weight)
        w_red = fetch(reduce_weight)
    else:
        fetch1 = lambda a: [lax.all_gather(a, "tensor", axis=1, tiled=True)]
        fetch0 = lambda a: [lax.all_gather(a, "tensor", axis=0, tiled=True)]
        small = fetch0
        both = lambda a: lax.pmax(a, "tensor")
        w_att = fetch1(attend_weight)
        w_out = fetch0(output_weight)
        w_exp = fetch1(expand_weight)
        w_red = fetch0(reduce_weight)
    b_att = small(attend_bias)
    tab = small(offset_table)
    b_exp = small(expand_bias)
    bound = both(bound)
    bad = dead_matter(bound, bound[3], gain_first.astype(F32), shift_first.astype(F32))

    n = len(w_att)
    local = Local(rows, n, w_att[0].shape[1], w_exp[0].shape[1])
    local.layout(crop_counts, t * windows, bad)
    xc, cotc, branch, first = local.gather(patches, cotangent, vec(gain_first), vec(shift_first))
    qkv, probs, mixed, middle, second = local.attend(
        xc,
        first,
        vec(gain_second),
        vec(shift_second),
        vec(output_bias),
        w_att,
        [bias_row(b) for b in b_att],
        [relative_rows(a) for a in tab],
        w_out,
    )
    g_exp, g_red, gb_exp = [None] * n, [None] * n, [None] * n
    carry = None
    for s in reversed(range(n)):
        g_exp[s], g_red[s], gb_exp[s], red, sg = local.feed(second, branch, w_exp[s], w_red[s], vec(b_exp[s]), carry)
        carry = (red, sg)
    mg, dqkv, v2, *rest = local.back(middle, sg, cotc, vec(gain_second), qkv, probs, mixed, first, w_out)
    g_out, g_att, gb_att, g_rel = (rest[i * n : (i + 1) * n] for i in range(4))
    result, input_grad, v1 = local.finish(
        xc, cotc, middle, red, mg, dqkv, vec(gain_first), vec(reduce_bias), patches, cotangent, w_att
    )
    g_rel = [relative_back(a) for a in g_rel]

    def bias_grad(a):
        a = a.reshape(-1, 3, HEAD_DIM)
        return jnp.stack([a[:, 0], a[:, 2]], axis=1)

    gb_att = [bias_grad(a) for a in gb_att]
    gb_exp = [a[0] for a in gb_exp]
    vectors = jnp.stack([v1[0], v1[1], v2[2], v2[0], v2[1], v1[2]])

    if fast:
        def cut(which):
            at = jnp.where(which == 0, t, 1 - t) * (d // 2)
            return lax.dynamic_slice_in_dim(vectors, at, d // 2, 1)

        def pack(s):
            parts = [cut(s), gb_att[s], g_rel[s], gb_exp[s]]
            flat = jnp.concatenate([p.reshape(-1) for p in parts])
            size = -(-flat.shape[0] // 1024) * 1024
            return jnp.pad(flat, (0, size - flat.shape[0])).reshape(-1, 128)

        tiny = (pack(0) + swap(pack(1).astype(BF), "tensor", nt).astype(F32)).astype(BF)
        for axis, size, step in (("core", 2, 1), ("y", 2, 1), ("z", nz, 1), ("z", nz, 2)):
            tiny = (tiny.astype(F32) + swap(tiny, axis, size, step).astype(F32)).astype(BF)
        flat = tiny.astype(F32).reshape(-1)
        sizes = [(6, d // 2), gb_att[0].shape, g_rel[0].shape, gb_exp[0].shape]
        smalls, at = [], 0
        for shape in sizes:
            k = int(np.prod(shape))
            smalls.append(flat[at : at + k].reshape(shape))
            at += k
        vectors, gb_att, g_rel, gb_exp = smalls

        def total(own, peer):
            own, peer = (add_halves(a, c, "core", 2) for a in (own, peer))
            a = (own.astype(F32) + swap(peer, "tensor", nt).astype(F32)).astype(BF)
            a = add_halves(a, y, "y", 2)
            a = add_halves(a, z % 2, "z", nz, 1)
            a = add_halves(a, z // 2, "z", nz, 2)
            a = join(a, swap(a, "z", nz, 2), z // 2)
            a = join(a, swap(a, "z", nz, 1), z % 2)
            a = join(a, swap(a, "y", 2), y)
            return join(a, swap(a, "core", 2), c).astype(F32)

        g_exp, g_red, g_out, g_att = (total(*a) for a in (g_exp, g_red, g_out, g_att))
    else:
        dp = ("z", "y", "core")

        def total(a, axis):
            a = lax.psum_scatter(a.astype(BF), "tensor", scatter_dimension=axis, tiled=True)
            return lax.psum(a, dp).astype(F32)

        vectors = total(vectors, 1)
        gb_att, g_rel, gb_exp, g_out, g_red = (total(a[0], 0) for a in (gb_att, g_rel, gb_exp, g_out, g_red))
        g_exp, g_att = (total(a[0], 1) for a in (g_exp, g_att))

    return (
        result,
        input_grad,
        vectors[0],
        vectors[1],
        g_att,
        gb_att,
        g_rel,
        g_out,
        vectors[2],
        vectors[3],
        vectors[4],
        g_exp,
        gb_exp,
        g_red,
        vectors[5],
    )


def solution(mesh):
    nt = mesh.shape["tensor"]
    nz = mesh.shape["dp"] // 4
    grid = Mesh(mesh.devices.reshape(nz, 2, 2, nt), ("z", "y", "core", "tensor"))
    dp = ("z", "y", "core")
    rows = P(dp + ("tensor",), None)
    in_specs = (
        rows,
        P(),
        P(),
        P(None, "tensor"),
        P("tensor", None, None),
        P("tensor", None),
        P("tensor", None),
        P(),
        P(),
        P(),
        P(None, "tensor"),
        P("tensor"),
        P("tensor", None),
        P(),
        P(dp),
        rows,
    )
    out_specs = (
        rows,
        rows,
        P("tensor"),
        P("tensor"),
        P(None, "tensor"),
        P("tensor", None, None),
        P("tensor", None),
        P("tensor", None),
        P("tensor"),
        P("tensor"),
        P("tensor"),
        P(None, "tensor"),
        P("tensor"),
        P("tensor", None),
        P("tensor"),
    )
    return jax.shard_map(partial(on_device, nz, nt), mesh=grid, in_specs=in_specs, out_specs=out_specs, check_vma=False)
```

```python
from functools import partial

import jax
import jax.numpy as jnp
import numpy as np
from jax import lax
from jax.experimental import pallas as pl
from jax.experimental.pallas import tpu as pltpu
from jax.sharding import Mesh
from jax.sharding import PartitionSpec as P

HEAD_DIM = 32
EPSILON = 1e-05
MASKED = 30000.0
SIDE = 7
SLOTS = SIDE * SIDE
BLK = 128
GROUP = 4
GW = 3 * GROUP * HEAD_DIM
BF = jnp.bfloat16
F32 = jnp.float32
VMEM_LIMIT = 60 * 1024 * 1024


def dot(a, b):
    return jnp.dot(a, b, preferred_element_type=F32)


def dot_nt(a, b):
    return lax.dot_general(a, b, (((1,), (1,)), ((), ())), preferred_element_type=F32)


def dot_tn(a, b):
    return lax.dot_general(a, b, (((0,), (0,)), ((), ())), preferred_element_type=F32)


def kind_tables():
    slot = -np.ones((2, BLK), np.int64)
    owner = 100 + np.arange(BLK)[None].repeat(2, 0)
    nine = np.arange(9)
    nine = (nine // 3) * SIDE + nine % 3
    for w in range(2):
        slot[0, w * SLOTS : (w + 1) * SLOTS] = np.arange(SLOTS)
        owner[0, w * SLOTS : (w + 1) * SLOTS] = w
    for w in range(3):
        at = 2 * SLOTS + 9 * w
        slot[0, at : at + 9] = nine
        owner[0, at : at + 9] = 2 + w
    for w in range(14):
        slot[1, 9 * w : 9 * w + 9] = nine
        owner[1, 9 * w : 9 * w + 9] = w
    pick = (slot[:, :, None] == np.arange(64)[None, None, :]).astype(np.float32)
    same = owner[:, :, None] == owner[:, None, :]
    mask = np.where(same, 0.0, -1e30).astype(np.float32)
    return pick, mask


def stride_tables():
    slot, _ = kind_tables()
    s = np.where(slot.sum(2) > 0, slot.argmax(2), -1)
    place = np.where(s >= 0, 13 * (s // SIDE) + s % SIDE, -1)
    up = (place[:, :, None] == np.arange(BLK)).astype(np.float32)
    down = ((84 - place)[:, :, None] == np.arange(BLK)) & (place >= 0)[:, :, None]
    return up, down.astype(np.float32).transpose(0, 2, 1)


def group_perm():
    perm = np.zeros((GW, GW), np.float32)
    for h in range(GROUP):
        for p in range(3):
            for e in range(HEAD_DIM):
                perm[(h * 3 + p) * HEAD_DIM + e, (p * GROUP + h) * HEAD_DIM + e] = 1.0
    return perm


PLAN_HEAD = 8
G1, B1, G2, B2, OB, RB = (slice(i, i + 1) for i in range(6))
AT_C, AT_ME = 6, 7


def bound_kernel(w, bias, table, out):
    width = w.shape[1]
    q = jnp.zeros((1, BLK), F32)
    k = jnp.zeros((1, BLK), F32)
    for start in range(0, width, BLK):
        size = min(BLK, width - start)
        x = w[:, start : start + size]
        gram = dot_tn(x, x)
        a = lax.broadcasted_iota(jnp.int32, (size, size), 0) >> 5
        b = lax.broadcasted_iota(jnp.int32, (size, size), 1) >> 5
        sums = jnp.sum(jnp.where(a == b, gram * gram, 0.0), axis=0, keepdims=True)
        lane = lax.broadcasted_iota(jnp.int32, (1, size), 1) >> 5
        for i in range(size // HEAD_DIM):
            part = (start // HEAD_DIM + i) % 3
            top = jnp.max(jnp.where(lane == i, sums, 0.0), axis=1, keepdims=True)
            if part == 0:
                q = jnp.maximum(q, top)
            if part == 1:
                k = jnp.maximum(k, top)
    qb = bias[...].astype(F32)
    col = lax.broadcasted_iota(jnp.int32, qb.shape, 1)
    qb = jnp.sum(jnp.where(col < HEAD_DIM, qb * qb, 0.0), axis=1, keepdims=True)
    qb = jnp.max(qb, axis=0, keepdims=True)
    top = jnp.max(jnp.max(jnp.abs(table[...].astype(F32)), axis=1, keepdims=True), axis=0, keepdims=True)
    out[...] = jnp.zeros_like(out)
    for i, v in enumerate((q, k, qb, top)):
        out[i : i + 1, :] = jnp.broadcast_to(v, (1, BLK))


def plan_kernel(windows, images, per_chunk, where, counts, bounds, vecs, out):
    d = vecs.shape[1]
    g1, b1 = vecs.at[G1], vecs.at[B1]
    big = bounds[...]

    def root4(v):
        return jnp.sqrt(jnp.sqrt(HEAD_DIM * v))

    reach = jnp.sqrt(float(d)) * jnp.max(jnp.abs(g1[...]), axis=1, keepdims=True)
    reach = 1.02 * (reach + jnp.sqrt(jnp.sum(b1[...] * b1[...], axis=1, keepdims=True)))
    q = 1.01 * (reach * root4(big[0:1, :]) + jnp.sqrt(big[2:3, :])) * HEAD_DIM**-0.5
    top = 1.01 * q * (reach * root4(big[1:2, :])) + big[3:4, :]
    safe = jnp.where(2.0 * top < MASKED - 500.0, 1, 0)
    bad = 1 - jnp.min(safe)
    first = where[0]
    nf = jnp.int32(0)
    nq = jnp.int32(0)
    for i in range(2 * windows + PLAN_HEAD, out.shape[0]):
        out[i] = 0
    for w in range(windows):
        place = first + w
        start = jnp.int32(0)
        offset = jnp.int32(-1)
        for i in range(images):
            total = counts[i] + 2
            inside = (place >= start) & (place < start + total)
            offset = jnp.where(inside, place - start, offset)
            start = start + total
        present = offset >= 0
        whole = present & (offset < 2)
        full = present & (whole | (bad > 0))
        part = present & (~whole) & (bad == 0)
        out[PLAN_HEAD + 2 * windows + w] = whole.astype(jnp.int32)

        @pl.when(full)
        def _():
            out[PLAN_HEAD + nf] = w

        @pl.when(part)
        def _():
            out[PLAN_HEAD + windows + nq] = w

        nf = nf + full.astype(jnp.int32)
        nq = nq + part.astype(jnp.int32)
    n0 = (nf + 1) >> 1
    left = jnp.maximum(nq - 3 * n0, 0)
    n1 = jnp.int32(0)
    for i in range(-(-windows // 14)):
        n1 = n1 + (left > 14 * i).astype(jnp.int32)
    nb = n0 + n1
    chunks = jnp.int32(1)
    for i in range(1, windows):
        chunks = chunks + (nb > per_chunk * i).astype(jnp.int32)
    for i, v in enumerate((nb, n0, chunks, bad, nf, nq, where[1], where[2])):
        out[i] = v


def norm_stats(x):
    mean = jnp.mean(x, axis=1, keepdims=True)
    c = x - mean
    scale = lax.rsqrt(jnp.mean(c * c, axis=1, keepdims=True) + EPSILON)
    return c * scale, scale


def norm_back(grad, normal, scale, gain):
    inner = grad * gain
    mean = jnp.mean(inner, axis=1, keepdims=True)
    proj = jnp.mean(inner * normal, axis=1, keepdims=True)
    return scale * (inner - mean - normal * proj)


def gather_kernel(windows, meta, slots, patches, cot, vecs, xc, cotc, branch, first, live, idx_row, idx, pick):
    rows = xc.shape[0]
    total = patches.shape[0]
    blocks = rows // BLK
    spots = lax.broadcasted_iota(jnp.int32, (BLK, total), 1)
    chunk = pl.program_id(0)
    n0 = meta[1]
    r = lax.broadcasted_iota(jnp.int32, (BLK, 1), 0)

    def listed(first_at, count, i):
        ok = (i >= 0) & (i < count)
        w = meta[first_at + jnp.where(ok, i, 0)]
        return jnp.where(ok, w, -1)

    def spread(ends, wins):
        base = jnp.full((BLK, 1), -1, jnp.int32)
        for end, w in reversed(list(zip(ends, wins))):
            base = jnp.where(r < end, w, base)
        return base

    def one(b, carry):
        at = pl.ds(pl.multiple_of(b * BLK, BLK), BLK)
        block = chunk * blocks + b
        kind0 = block < n0

        @pl.when(kind0)
        def _():
            wins = [listed(PLAN_HEAD, meta[4], 2 * block + i) for i in range(2)]
            wins += [listed(PLAN_HEAD + windows, meta[5], 3 * block + i) for i in range(3)]
            ends = [SLOTS, 2 * SLOTS] + [2 * SLOTS + 9 * (i + 1) for i in range(3)]
            base = spread(ends, wins)
            slot = slots[0]
            where_whole = [
                jnp.where(w >= 0, meta[PLAN_HEAD + 2 * windows + jnp.maximum(w, 0)], 0) for w in wins[:2]
            ] + [jnp.int32(1)] * 3
            sure = spread(ends, where_whole) > 0
            ok = base >= 0
            idx[...] = jnp.where(ok, base * SLOTS + slot, -1)
            live[at, :] = jnp.where(ok & (sure | (slots[2] > 0)), 1.0, 0.0)

        @pl.when(jnp.logical_not(kind0))
        def _():
            start = 3 * n0 + 14 * (block - n0)
            wins = [listed(PLAN_HEAD + windows, meta[5], start + i) for i in range(14)]
            base = spread([9 * (i + 1) for i in range(14)], wins)
            ok = base >= 0
            idx[...] = jnp.where(ok, base * SLOTS + slots[1], -1)
            live[at, :] = jnp.where(ok, 1.0, 0.0)

        here = idx[...]
        wide = jnp.broadcast_to(here.astype(F32), (BLK, BLK))
        idx_row[0, :, at] = wide.T[0:1, :].astype(jnp.int32)
        pick[at, :] = (spots == here).astype(F32).astype(BF)
        return carry

    lax.fori_loop(0, blocks, one, 0)
    x = dot(pick[...], patches[...])
    xc[...] = x.astype(BF)
    up = dot(pick[...], cot[...])
    cotc[...] = up.astype(BF)
    branch[...] = (up * live[...]).astype(BF)
    for b in range(blocks):
        at = slice(b * BLK, (b + 1) * BLK)
        n, _ = norm_stats(xc[at, :].astype(F32))
        first[at, :] = (n * vecs[G1] + vecs[B1]).astype(BF)


def lane_head(shape, axis):
    return lax.broadcasted_iota(jnp.int32, shape, axis) >> 5


def spread_rows(x):
    h = lane_head(x.shape, 1)
    zero = jnp.zeros_like(x)
    return jnp.concatenate([jnp.where(h == i, x, zero) for i in range(GROUP)], axis=0)


def spread_cols(xt):
    h = lane_head(xt.shape, 0)
    zero = jnp.zeros_like(xt)
    return jnp.concatenate([jnp.where(h == i, xt, zero) for i in range(GROUP)], axis=1)


def fold_rows(x):
    h = lane_head((BLK, BLK), 1)
    out = x[0:BLK]
    for i in range(1, GROUP):
        out = jnp.where(h == i, x[i * BLK : (i + 1) * BLK], out)
    return out


def attend_kernel(pieces, groups, tail, prior, meta, live, first, perm, pick, mask, bias, rel, *rest):
    w, rest = rest[:pieces], rest[pieces:]
    if tail:
        (xc, vecs), rest = rest[:2], rest[2:]
        before, rest = rest[:prior], rest[prior:]
        w_before, rest = rest[:prior], rest[prior:]
        w_out, rest = rest[:pieces], rest[pieces:]
        qkv, probs, mixed_out, middle, second, table, mixed, att = rest
    else:
        qkv, probs, mixed_out, table = rest
    rows, d = first.shape
    blocks = rows // BLK
    chunk, step = pl.program_id(0), pl.program_id(1)
    c = meta[AT_C]
    n0 = meta[1]
    near = pl.ds(pl.multiple_of(c * (d // 2), BLK), d // 2)
    far = pl.ds(pl.multiple_of((1 - c) * (d // 2), BLK), d // 2)

    @pl.when(step < groups)
    def _():
        if pieces == 1:
            v = dot(first[...], w[0][...])
        else:
            v = dot(first[:, near], w[0][...]) + dot(first[:, far], w[1][...])
        v = v + bias[...]
        block = lax.broadcasted_iota(jnp.int32, (1, GW), 1) >> 5
        is_q = block == 0
        for i in range(3, 3 * GROUP, 3):
            is_q = is_q | (block == i)
        v = (v * jnp.where(is_q, HEAD_DIM**-0.5, 1.0)).astype(BF)
        qkv[...] = dot(v, perm[...]).astype(BF)
        places = []
        for h in range(GROUP):
            row = rel[pl.ds(step * GROUP + h, 1), :]
            row = pltpu.roll(jnp.broadcast_to(row, (BLK, 2 * BLK)), 2 * BLK - 88, 1, stride=1, stride_axis=0)
            places.append(row[:, 0:BLK].astype(BF))
        for kind in range(2):
            e = pick[kind]
            for h in range(GROUP):
                half = dot(e, places[h]).astype(BF)
                t = dot_nt(half, e) + mask[kind].astype(F32)
                table[kind, h * BLK : (h + 1) * BLK, :] = t.astype(BF)
        for b in range(blocks):
            at = slice(b * BLK, (b + 1) * BLK)
            kind = jnp.where(chunk * blocks + b < n0, 0, 1)
            q = qkv[at, 0:BLK]
            k = qkv[at, BLK : 2 * BLK]
            v = qkv[at, 2 * BLK : 3 * BLK]
            st = dot_nt(spread_rows(k), q) + table[kind].astype(F32)
            dead = (live[at, :] - 1.0) * MASKED
            st = st.reshape(GROUP, BLK, BLK) + jnp.where(meta[3] > 0, dead, 0.0)[None]
            peak = jnp.max(st, axis=1, keepdims=True)
            e = jnp.exp(st - peak)
            p = (e * (1.0 / jnp.sum(e, axis=1, keepdims=True))).astype(BF)
            p = p.reshape(GROUP * BLK, BLK)
            probs[b, 0] = p
            vt = v.astype(F32).T.astype(BF)
            m = dot(spread_cols(vt), p).T.astype(BF)
            mixed_out[at, :] = m
            if tail:
                mixed[at, pl.ds(pl.multiple_of(step * BLK, BLK), BLK)] = m

    if not tail:
        return

    @pl.when(step == groups)
    def _():
        if pieces == 1:
            att[...] = dot(mixed[...], w_out[0][...])
        else:
            att[:, near] = dot(mixed[...], w_out[0][...])
            att[:, far] = dot(mixed[...], w_out[1][...])
        for m, v in zip(before, w_before):
            att[...] = att[...] + dot(m[...], v[...])
        for b in range(blocks):
            at = slice(b * BLK, (b + 1) * BLK)
            m = xc[at, :].astype(F32) + live[at, :] * (att[at, :] + vecs[OB])
            middle[at, :] = m
            nrm, _ = norm_stats(m)
            second[at, :] = (nrm * vecs[G2] + vecs[B2]).astype(BF)


def feed_kernel(tiles, pieces, last, prior, meta, second, branch, *rest):
    we, wr, rest = rest[:pieces], rest[pieces : 2 * pieces], rest[2 * pieces :]
    be, rest = rest[0], rest[1:]
    if last:
        (live, middle, cotc, vecs), rest = rest[:4], rest[4:]
        sg_in, rest = rest[:prior], rest[prior:]
    grads, rest = rest[:tiles], rest[tiles:]
    dbe, red = rest[:2]
    if last:
        (mg, ag, vec), rest = rest[2:5], rest[5:]
    else:
        (sg,), rest = rest[2:3], rest[3:]
    sec, br, e_buf, r_buf, gbuf, ra, sa, half, sem, w_sem, g_sem = rest[:11]
    if last:
        mid_buf, cot_buf, live_buf, sg_buf = rest[11:]
    ch, d = sec.shape
    wide = e_buf.shape[2]
    c0, me = meta[AT_C], meta[AT_ME]
    y = me & 1
    chunks = meta[2]

    def move(a, b, i):
        return pltpu.make_async_copy(a, b, sem.at[i])

    def loads(c):
        rows = pl.ds(pl.multiple_of(c * ch, ch), ch)
        return [move(second.at[rows, :], sec, 0), move(branch.at[rows, :], br, 1)]

    def weights(i):
        if pieces == 1:
            at = pl.ds(pl.multiple_of((i ^ c0) * wide, BLK), wide)
            a, b = we[0].at[:, at], wr[0].at[at, :]
        else:
            a, b = we[i], wr[i]
        return [
            pltpu.make_async_copy(a, e_buf.at[i], w_sem.at[2 * i]),
            pltpu.make_async_copy(b, r_buf.at[i], w_sem.at[2 * i + 1]),
        ]

    def extras(c):
        rows = pl.ds(pl.multiple_of(c * ch, ch), ch)
        out = [
            move(middle.at[rows, :], mid_buf, 2),
            move(cotc.at[rows, :], cot_buf, 3),
            move(live.at[rows, :], live_buf, 4),
        ]
        return out + [move(x.at[rows, :], sg_buf, 5) for x in sg_in]

    def store(i):
        return pltpu.make_async_copy(gbuf.at[i], grads[i], g_sem.at[i])

    if last:
        vec[...] = jnp.zeros_like(vec)

    def chunk(c, carry):
        rows = pl.ds(pl.multiple_of(c * ch, ch), ch)
        for x in loads(c):
            x.start()

        @pl.when(c == 0)
        def _():
            for i in range(tiles):
                for x in weights(i):
                    x.start()

        if last:
            for x in extras(c):
                x.start()
        for x in loads(c):
            x.wait()

        def tile(t, carry):
            for i in range(tiles):

                @pl.when((t == i) & (c == 0))
                def _():
                    for x in weights(i):
                        x.wait()

            at = pl.ds(pl.multiple_of((t ^ c0) * wide, BLK), wide)
            e, r = e_buf[t], r_buf[t]
            u = dot(sec[...], e) + be[:, at]
            cdf = 0.5 * (1.0 + lax.erf(u * 0.7071067811865476))
            h = (u * cdf).astype(BF)
            slope = cdf + u * (jnp.exp(-0.5 * u * u) * 0.3989422804014327)
            pg = (dot_nt(br[...], r) * slope).astype(BF)
            grad_b = jnp.sum(pg.astype(F32), axis=0, keepdims=True)

            def put(low, g):
                n = wide // 2
                for i in range(2):
                    ref = gbuf.at[t, i ^ y, low : low + d, :]
                    part = g[:, i * n : (i + 1) * n]

                    @pl.when(c == 0)
                    def _():
                        ref[...] = part.astype(BF)

                    @pl.when(c > 0)
                    def _():
                        ref[...] = (ref[...].astype(F32) + part).astype(BF)

            put(0, dot_tn(sec[...], pg))
            put(d, dot_tn(br[...], h))

            @pl.when(c == 0)
            def _():
                dbe[:, at] = grad_b

            @pl.when(c > 0)
            def _():
                dbe[:, at] = dbe[:, at] + grad_b

            red_t = dot(h, r)
            sg_t = dot_nt(pg, e)

            @pl.when(t == 0)
            def _():
                ra[...] = red_t
                sa[...] = sg_t

            @pl.when(t > 0)
            def _():
                ra[...] = ra[...] + red_t
                sa[...] = sa[...] + sg_t

            for i in range(tiles):

                @pl.when((t == i) & (c == chunks - 1))
                def _():
                    store(i).start()

            return carry

        lax.fori_loop(0, tiles, tile, 0)
        half[0] = ra[...].astype(BF)
        outs = [move(half.at[0], red.at[rows, :], 0)]
        outs[0].start()
        if not last:
            half[1] = sa[...].astype(BF)
            outs.append(move(half.at[1], sg.at[rows, :], 1))
            outs[1].start()
        else:
            for x in extras(c):
                x.wait()
            for b in range(ch // BLK):
                at = slice(b * BLK, (b + 1) * BLK)
                nrm, scale = norm_stats(mid_buf[at, :])
                g = sa[at, :]
                if prior:
                    g = g + sg_buf[at, :].astype(F32)
                m = cot_buf[at, :].astype(F32) + norm_back(g, nrm, scale, vecs[G2])
                ra[at, :] = m
                kept = m * live_buf[at, :]
                half[1, at, :] = kept.astype(BF)
                vec[0:1, :] = vec[0:1, :] + jnp.sum(g * nrm, axis=0, keepdims=True)
                vec[1:2, :] = vec[1:2, :] + jnp.sum(g, axis=0, keepdims=True)
                vec[2:3, :] = vec[2:3, :] + jnp.sum(kept, axis=0, keepdims=True)
            outs += [move(half.at[1], ag.at[rows, :], 1), move(ra, mg.at[rows, :], 2)]
            for x in outs[1:]:
                x.start()
        for x in outs:
            x.wait()
        return carry

    lax.fori_loop(0, chunks, chunk, 0)
    for i in range(tiles):
        store(i).wait()


def back_kernel(pieces, groups, split, meta, ag, perm, pick, pick_t, qkv, probs, mixed, first, *rest):
    w_out, rest = rest[:pieces], rest[pieces:]
    dqkv, rest = rest[0], rest[1:]
    grads, rest = rest[: 2 if split else 1], rest[2 if split else 1 :]
    dba, drel, dperm, dmix, table = rest
    rows, d = ag.shape
    blocks = rows // BLK
    step, chunk = pl.program_id(0), pl.program_id(1)
    n0 = meta[1]
    c, me = meta[AT_C], meta[AT_ME]
    half = d // 2
    stays = (step >> 1) == (me >> 1)

    def put(ref, value):
        @pl.when(chunk == 0)
        def _():
            ref[...] = value.astype(ref.dtype)

        @pl.when(chunk > 0)
        def _():
            ref[...] = (ref[...].astype(F32) + value).astype(ref.dtype)

    def put_grad(low, high, value):
        if not split:
            put(grads[0].at[0, low:high, :], value)
            return

        @pl.when(stays)
        def _():
            put(grads[0].at[0, low:high, :], value)

        @pl.when(jnp.logical_not(stays))
        def _():
            put(grads[1].at[0, low:high, :], value)

    @pl.when(step == groups)
    def _():
        wide = groups * BLK
        for i in range(2):
            put_grad(i * wide, (i + 1) * wide, dot_tn(mixed[...], ag[:, i * half : (i + 1) * half]))

    @pl.when(step < groups)
    def _():
        @pl.when(chunk == 0)
        def _():
            table[...] = jnp.zeros_like(table)

        if pieces == 1:
            dmix[...] = dot_nt(ag[...], w_out[0][...]).astype(BF)
        else:
            near = pl.ds(pl.multiple_of(c * half, BLK), half)
            far = pl.ds(pl.multiple_of((1 - c) * half, BLK), half)
            dmix[...] = (dot_nt(ag[:, near], w_out[0][...]) + dot_nt(ag[:, far], w_out[1][...])).astype(BF)
        for b in range(blocks):
            at = slice(b * BLK, (b + 1) * BLK)
            kind = jnp.where(chunk * blocks + b < n0, 0, 1)
            q = qkv[at, 0:BLK]
            k = qkv[at, BLK : 2 * BLK]
            v = qkv[at, 2 * BLK : 3 * BLK]
            do = dmix[at, :]
            p = probs[b, 0]
            dp = dot_nt(spread_rows(v), do).reshape(GROUP, BLK, BLK)
            pf = p.astype(F32).reshape(GROUP, BLK, BLK)
            x = pf * dp
            ds = x - pf * jnp.sum(x, axis=1, keepdims=True)
            ds = ds.astype(BF).reshape(GROUP * BLK, BLK)
            table[kind] = table[kind] + ds.astype(F32)
            dv = fold_rows(dot(p, do))
            dk = fold_rows(dot(ds, q))
            kt = k.astype(F32).T.astype(BF)
            dq = (dot(spread_cols(kt), ds) * HEAD_DIM**-0.5).T
            dperm[at, 0:BLK] = dq.astype(BF)
            dperm[at, BLK : 2 * BLK] = dk.astype(BF)
            dperm[at, 2 * BLK : 3 * BLK] = dv.astype(BF)
        x = dot_nt(dperm[...], perm[...]).astype(BF)
        dqkv[...] = x
        put_grad(0, d, dot_tn(first[...], x))
        put(dba, jnp.sum(x.astype(F32), axis=0, keepdims=True))

        @pl.when(chunk == meta[2] - 1)
        def _():
            for h in range(GROUP):
                total = jnp.zeros((BLK, BLK), F32)
                for kind in range(2):
                    a = table[kind, h * BLK : (h + 1) * BLK, :]
                    a = dot(a.astype(BF), pick[kind]).astype(BF)
                    total = total + dot(pick_t[kind], a)
                wide = jnp.concatenate([total, jnp.zeros_like(total)], axis=1)
                wide = pltpu.roll(wide, 0, 1, stride=1, stride_axis=0)
                drel[pl.ds(step * GROUP + h, 1), :] = jnp.sum(wide, axis=0, keepdims=True)


def row_tiles(rows, size=384):
    return [(a, min(size, rows - a)) for a in range(0, rows, size)]


def ends_kernel(pieces, meta, live, xc, cotc, middle, mg, vecs, *rest):
    n = len(pieces)
    red, rest = rest[:n], rest[n:]
    dqkv, rest = rest[:n], rest[n:]
    w = []
    for k in pieces:
        w.append(rest[:k])
        rest = rest[k:]
    res, hi, lo, vec, fg = rest
    rows, d = xc.shape
    blocks = rows // BLK
    chunk = pl.program_id(0)
    c = meta[AT_C]
    half = d // 2

    @pl.when(chunk == 0)
    def _():
        vec[...] = jnp.zeros_like(vec)

    for s in range(n):
        if len(w[s]) == 1:
            v = dot_nt(dqkv[s][...], w[s][0][...])
            fg[...] = v if s == 0 else fg[...] + v
        else:
            for i in range(2):
                cols = pl.ds(pl.multiple_of((c if i == 0 else 1 - c) * half, BLK), half)
                fg[:, cols] = fg[:, cols] + dot_nt(dqkv[s][...], w[s][i][...])

    for b in range(blocks):
        at = slice(b * BLK, (b + 1) * BLK)
        keep = live[at, :]
        nrm, scale = norm_stats(xc[at, :].astype(F32))
        g = fg[at, :]
        up = cotc[at, :].astype(F32)
        delta = mg[at, :] - up + norm_back(g, nrm, scale, vecs[G1])
        top = delta.astype(BF)
        hi[at, :] = top
        lo[at, :] = (delta - top.astype(F32)).astype(BF)
        reduced = vecs[RB]
        for x in red:
            reduced = reduced + x[at, :].astype(F32)
        res[at, :] = (middle[at, :] + keep * reduced).astype(BF)
        vec[0:1, :] = vec[0:1, :] + jnp.sum(g * nrm, axis=0, keepdims=True)
        vec[1:2, :] = vec[1:2, :] + jnp.sum(g, axis=0, keepdims=True)
        vec[2:3, :] = vec[2:3, :] + jnp.sum(up * keep, axis=0, keepdims=True)


def scatter_kernel(meta, idx, res, hi, lo, patches, cot, result, input_grad):
    rows = res.shape[0]
    chunk = pl.program_id(0)
    for start, size in row_tiles(patches.shape[0]):
        at = slice(start, start + size)
        spots = start + lax.broadcasted_iota(jnp.int32, (size, rows), 0)
        hit = (spots == idx[0]).astype(F32)
        here = jnp.sum(hit, axis=1, keepdims=True) > 0.0
        put = hit.astype(BF)
        new = dot(put, res[...])
        grad = dot(put, hi[...]) + dot(put, lo[...])

        @pl.when(chunk == 0)
        def _():
            result[at, :] = jnp.where(here, new, patches[at, :].astype(F32)).astype(BF)
            input_grad[at, :] = cot[at, :].astype(F32) + grad

        @pl.when(chunk > 0)
        def _():
            result[at, :] = jnp.where(here, new, result[at, :].astype(F32)).astype(BF)
            input_grad[at, :] = input_grad[at, :] + grad


SMEM = pl.BlockSpec(memory_space=pltpu.SMEM)
ANY = pl.BlockSpec(memory_space=pl.ANY)
PACK = 24


def pack_kernel(where, v1, v2, *refs):
    n = 2
    db, dba, drel = (refs[i * n : (i + 1) * n] for i in range(3))
    outs = refs[3 * n :]
    d = v1.shape[1]
    half = d // 2
    for s in range(n):
        t = where[0] if s == 0 else 1 - where[0]
        cols = pl.ds(pl.multiple_of(t * half, BLK), half)
        out = outs[s]
        out[...] = jnp.zeros_like(out)
        out[0:1, :] = db[s][...].astype(BF).astype(F32)
        out[1:2, 0 : dba[s].shape[1]] = dba[s][...]
        for i, (v, r) in enumerate(((v1, 0), (v1, 1), (v2, 2), (v2, 0), (v2, 1), (v1, 2))):
            out[2 + i : 3 + i, 0:half] = v[r : r + 1, cols]
        k = drel[s].shape[0]
        out[8 : 8 + k, 0 : drel[s].shape[1]] = drel[s][...]


def pack(t, v1, v2, db, dba, drel):
    v = pl.BlockSpec(memory_space=pltpu.VMEM)
    shape = sds((PACK, db[0].shape[1]), F32)
    return pl.pallas_call(
        pack_kernel,
        in_specs=[SMEM] + [v] * 8,
        out_specs=[v, v],
        out_shape=[shape, shape],
        name="pack",
    )(t, v1, v2, *db, *dba, *drel)


def relative_z(z, ids):
    r = z ^ ids[2]
    return 2 * (r & 1) + (r >> 1)


def place_feed_kernel(ids, a, b, c, e, exp, red):
    @pl.when(pl.program_id(0) < 4)
    def _():
        exp[...] = a[0, 0].astype(F32)
        red[...] = b[0, 0].astype(F32).T

    @pl.when(pl.program_id(0) >= 4)
    def _():
        exp[...] = c[0, 0].astype(F32)
        red[...] = e[0, 0].astype(F32).T


def place_feed(ids, near, far, d, hidden):
    def spec(which, odd):
        def at(j, ids):
            j = jnp.minimum(j, 3) if which == 0 else jnp.maximum(j, 4)
            return ((j >> 1) & 1) ^ ids[1], relative_z(2 * (j & 1) + odd, ids), 0, 0

        return pl.BlockSpec((1, 1, GW, GW), at)

    tile = lambda j, ids: ((j >> 2) ^ ids[0]) * 2 + ((j >> 1) & 1)
    return pl.pallas_call(
        place_feed_kernel,
        grid_spec=pltpu.PrefetchScalarGridSpec(
            num_scalar_prefetch=1,
            grid=(8,),
            in_specs=[spec(0, 0), spec(0, 1), spec(1, 0), spec(1, 1)],
            out_specs=[
                pl.BlockSpec((GW, GW), lambda j, ids: (j & 1, tile(j, ids))),
                pl.BlockSpec((GW, GW), lambda j, ids: (tile(j, ids), j & 1)),
            ],
        ),
        out_shape=[sds((d, hidden), F32), sds((hidden, d), F32)],
        name="place_feed",
    )(ids, near, near, far, far)


def place_attend_kernel(ids, *refs):
    att, out = refs[8:]
    for i in range(4):
        near, far = refs[i], refs[4 + i]
        x = jnp.where((i >> 1) == ids[0], near[0, 0], far[0, 0]).astype(F32)
        if i < 3:
            att[:, i * GW : (i + 1) * GW] = x
        else:
            out[...] = x


def place_attend(ids, near, far, d):
    r = near.shape[2]
    ins = [
        pl.BlockSpec(
            (1, 1, r, GW),
            lambda q, ids, i=i: (relative_z((q & 1) * 2 + (q >> 1), ids), (i & 1) ^ ids[1], 0, 0),
        )
        for i in range(4)
    ]
    return pl.pallas_call(
        place_attend_kernel,
        grid_spec=pltpu.PrefetchScalarGridSpec(
            num_scalar_prefetch=1,
            grid=(4,),
            in_specs=ins + ins,
            out_specs=[
                pl.BlockSpec((r, 3 * GW), lambda q, ids: (q, 0)),
                pl.BlockSpec((r, GW), lambda q, ids: (q & 1, q >> 1)),
            ],
        ),
        out_shape=[sds((d, 3 * GW), F32), sds((GW, d), F32)],
        name="place_attend",
    )(ids, near, near, near, near, far, far, far, far)


def guarded(body, axis):
    def run(meta, *refs):
        @pl.when(pl.program_id(axis) < meta[2])
        def _():
            body(meta, *refs)

    return run


def clamp(i, meta):
    return jnp.minimum(i, meta[2] - 1)


def whole_spec(shape):
    zeros = (0,) * len(shape)
    return pl.BlockSpec(shape, lambda *_: zeros, pipeline_mode=pl.Buffered(1))


def chunk_spec(shape):
    zeros = (0,) * (len(shape) - 1)
    return pl.BlockSpec(shape, lambda i, meta: (clamp(i, meta),) + zeros)


def sds(shape, dtype):
    return jax.ShapeDtypeStruct(shape, dtype)


def w_(a):
    return (a, whole_spec(a.shape))


def o_(shape, dtype):
    return (sds(shape, dtype), whole_spec(shape))


class Local:
    def __init__(self, rows):
        self.rows = rows
        self.windows = rows // SLOTS
        worst = (self.windows + 1) // 2
        self.per_chunk = min(5, max(worst, 1))
        self.chunks = -(-worst // self.per_chunk)
        self.ch = self.per_chunk * BLK
        self.all = self.ch * self.chunks
        pick, mask = kind_tables()
        self.mask = jnp.asarray(mask, BF)
        self.perm = jnp.asarray(group_perm(), BF)
        up, down_t = stride_tables()
        self.up, self.down_t = jnp.asarray(up, BF), jnp.asarray(down_t, BF)
        slot = np.where(pick.sum(2) > 0, pick.argmax(2), 0)
        corner = (slot[0] // SIDE < 3) & (slot[0] % SIDE < 3)
        self.slots = jnp.asarray(np.stack([slot[0], slot[1], corner])[:, :, None], jnp.int32)

    def row(self, k, dt):
        return (sds((self.all, k), dt), chunk_spec((self.ch, k)))

    def c(self, a):
        return (a, chunk_spec((self.ch,) + a.shape[1:]))

    def call(self, body, name, ins, outs, scratch=(), grid=None, axis=0, flops=0, size=0, limit=VMEM_LIMIT):
        f = pl.pallas_call(
            body if axis is None else guarded(body, axis),
            out_shape=[o for o, _ in outs],
            grid_spec=pltpu.PrefetchScalarGridSpec(
                num_scalar_prefetch=1,
                grid=(self.chunks,) if grid is None else grid,
                in_specs=[s for _, s in ins],
                out_specs=[s for _, s in outs],
                scratch_shapes=list(scratch),
            ),
            compiler_params=pltpu.CompilerParams(vmem_limit_bytes=limit),
            cost_estimate=pl.CostEstimate(flops=int(flops), bytes_accessed=int(size), transcendentals=0),
            name=name,
        )
        return f(self.meta, *[a for a, _ in ins])

    def bound(self, w, bias, table):
        ins = [w, bias.reshape(bias.shape[0], -1), table]
        return pl.pallas_call(
            bound_kernel,
            out_shape=sds((8, BLK), F32),
            compiler_params=pltpu.CompilerParams(vmem_limit_bytes=VMEM_LIMIT),
            name="bound",
        )(*ins)

    def plan(self, place, counts, bounds, vecs):
        v = pl.BlockSpec(memory_space=pltpu.VMEM)
        self.meta = pl.pallas_call(
            partial(plan_kernel, self.windows, counts.shape[0], self.per_chunk),
            out_shape=sds((PLAN_HEAD + 3 * self.windows,), jnp.int32),
            in_specs=[SMEM, SMEM, v, v],
            out_specs=SMEM,
            name="plan",
        )(place, counts, bounds, vecs)

    def gather(self, patches, cot, vecs):
        ch, d = self.ch, patches.shape[1]
        idx = (sds((self.chunks, 1, ch), jnp.int32), pl.BlockSpec((1, 1, ch), lambda i, meta: (clamp(i, meta), 0, 0)))
        return self.call(
            partial(gather_kernel, self.windows),
            "gather_rows",
            [w_(self.slots), w_(patches), w_(cot), w_(vecs)],
            [self.row(d, BF)] * 4 + [self.row(1, F32), idx],
            [pltpu.VMEM((BLK, 1), jnp.int32), pltpu.VMEM((ch, self.rows), BF)],
            flops=4 * ch * self.rows * d,
            size=8 * self.rows * d,
        )

    def attend(self, live, first, bias, rel, w, tail=None, before=()):
        ch, d = self.ch, first.shape[1]
        width = w[0].shape[1]
        groups = width // GW
        clip = lambda i, g, meta: jnp.where(i < meta[2], jnp.minimum(g, groups - 1), groups - 1)
        by_chunk = lambda a: (a, pl.BlockSpec((ch,) + a.shape[1:], lambda i, g, meta: (clamp(i, meta), 0)))
        cols = lambda a, k: (a, pl.BlockSpec((a.shape[0], k), lambda i, g, meta: (0, clip(i, g, meta))))
        out = lambda total, k, dt: (
            sds((self.all, total), dt),
            pl.BlockSpec((ch, k), lambda i, g, meta: (clamp(i, meta), clip(i, g, meta))),
        )
        pshape = (self.per_chunk * self.chunks, groups, GROUP * BLK, BLK)
        pspec = pl.BlockSpec((self.per_chunk, 1) + pshape[2:], lambda i, g, meta: (clamp(i, meta), clip(i, g, meta), 0, 0))
        ins = [by_chunk(live), by_chunk(first), w_(self.perm), w_(self.up), w_(self.mask), cols(bias, GW), w_(rel)]
        ins += [cols(a, GW) for a in w]
        outs = [out(width, GW, BF), (sds(pshape, BF), pspec), out(groups * BLK, BLK, BF)]
        scratch = [pltpu.VMEM((2, GROUP * BLK, BLK), BF)]
        steps = groups
        if tail is not None:
            steps += 1
            xc, vecs, wo = tail
            ins += [by_chunk(xc), w_(vecs)]
            ins += [by_chunk(m) for m, _ in before] + [w_(a) for _, a in before] + [w_(a) for a in wo]
            outs += [
                (sds((self.all, d), dt), pl.BlockSpec((ch, d), lambda i, g, meta: (clamp(i, meta), 0)))
                for dt in (F32, BF)
            ]
            scratch += [pltpu.VMEM((ch, groups * BLK), BF), pltpu.VMEM((ch, d), F32)]
        return self.call(
            partial(attend_kernel, len(w), groups, tail is not None, len(before)),
            "attend",
            ins,
            outs,
            scratch,
            grid=(self.chunks, steps),
            flops=0.16 * ch * d * width,
            size=0.4 * ch * d,
        )

    def feed(self, second, branch, we, wr, be, last=None):
        ch, d = self.ch, second.shape[1]
        hidden = be.shape[1]
        pieces = len(we)
        wide = 2 * GW
        tiles = hidden // wide
        any_ = lambda a: (a, ANY)
        full = lambda dt: (sds((self.all, d), dt), ANY)
        ins = [any_(a) for a in (second, branch, *we, *wr)] + [w_(be)]
        outs = [(sds((2, 2 * d, GW), BF), ANY)] * tiles + [o_((1, hidden), F32), full(BF)]
        v = pltpu.VMEM
        scratch = [v((ch, d), BF)] * 2 + [v((tiles, d, wide), BF), v((tiles, wide, d), BF)]
        scratch += [v((tiles, 2, 2 * d, GW), BF), v((ch, d), F32), v((ch, d), F32), v((2, ch, d), BF)]
        dma = pltpu.SemaphoreType.DMA
        scratch += [dma((6,)), dma((2 * tiles,)), dma((tiles,))]
        prior = 0
        if last is None:
            outs += [full(BF)]
        else:
            live, middle, cotc, vecs, sums = last
            prior = len(sums)
            ins += [any_(live), any_(middle), any_(cotc), w_(vecs)] + [any_(a) for a in sums]
            outs += [full(F32), full(BF), o_((8, d), F32)]
            scratch += [v((ch, d), F32), v((ch, d), BF), v((ch, 1), F32), v((ch, d), BF)]
        return self.call(
            partial(feed_kernel, tiles, pieces, last is not None, prior),
            "feed",
            ins,
            outs,
            scratch,
            grid=(1,),
            axis=None,
            flops=12 * ch * d * hidden,
            size=8 * d * hidden,
        )

    def back(self, ag, qkv, probs, mixed, first, wo):
        ch, d = self.ch, first.shape[1]
        width = qkv.shape[1]
        groups = width // GW
        split = groups == 3
        clip = lambda g: jnp.minimum(g, groups - 1)
        by_chunk = lambda a: (a, pl.BlockSpec((ch,) + a.shape[1:], lambda g, i, meta: (clamp(i, meta), 0)))
        cols = pl.BlockSpec((ch, GW), lambda g, i, meta: (clamp(i, meta), clip(g)))
        pspec = pl.BlockSpec((self.per_chunk, 1) + probs.shape[2:], lambda g, i, meta: (clamp(i, meta), clip(g), 0, 0))
        one = (1, 2 * groups * BLK, GW)
        if split:

            def tile(start):
                return lambda g, i, meta: (
                    (jnp.clip(g - start(meta[AT_ME] >> 1), 0, 1) ^ meta[AT_ME]) & 1,
                    0,
                    0,
                )

            shape = sds((2,) + one[1:], BF)
            grads = [(shape, pl.BlockSpec(one, tile(lambda h: 2 * h))), (shape, pl.BlockSpec(one, tile(lambda h: 2 - 2 * h)))]
        else:
            grads = [(sds((groups + 1,) + one[1:], BF), pl.BlockSpec(one, lambda g, i, meta: (g, 0, 0)))]
        rows = lambda a, k: pl.BlockSpec((k, a), lambda g, i, meta: (clip(g), 0))
        return self.call(
            partial(back_kernel, len(wo), groups, split),
            "back",
            [by_chunk(ag), w_(self.perm), w_(self.up), w_(self.down_t), (qkv, cols), (probs, pspec)]
            + [by_chunk(mixed), by_chunk(first)]
            + [(a, rows(a.shape[1], BLK)) for a in wo],
            [(sds((self.all, width), BF), cols), *grads]
            + [(sds((1, width), F32), pl.BlockSpec((1, GW), lambda g, i, meta: (0, clip(g))))]
            + [o_((groups * GROUP, 2 * BLK), F32)],
            [pltpu.VMEM((ch, GW), BF), pltpu.VMEM((ch, BLK), BF), pltpu.VMEM((2, GROUP * BLK, BLK), F32)],
            grid=(groups + 1, self.chunks),
            axis=1,
            flops=14 * ch * d * width,
            size=30 * ch * d,
        )

    def ends(self, live, xc, cotc, middle, mg, vecs, red, dqkv, ws):
        ch, d = self.ch, xc.shape[1]
        c = self.c
        return self.call(
            partial(ends_kernel, [len(a) for a in ws]),
            "ends",
            [c(live), c(xc), c(cotc), c(middle), c(mg), w_(vecs)]
            + [c(a) for a in (*red, *dqkv)]
            + [w_(a) for s in ws for a in s],
            [self.row(d, BF)] * 3 + [o_((8, d), F32)],
            [pltpu.VMEM((ch, d), F32)],
            flops=6 * ch * d * d,
            size=30 * ch * d,
        )

    def scatter(self, idx, res, hi, lo, patches, cot):
        ch, d = self.ch, patches.shape[1]
        rspec = (idx, pl.BlockSpec((1, 1, ch), lambda i, meta: (clamp(i, meta), 0, 0)))
        return self.call(
            scatter_kernel,
            "scatter",
            [rspec, self.c(res), self.c(hi), self.c(lo), w_(patches), w_(cot)],
            [o_(patches.shape, BF), o_(patches.shape, F32)],
            flops=6 * ch * self.rows * d,
            size=12 * self.rows * d,
        )


CODES = 169


def pad_table(table):
    return jnp.pad(table.astype(F32), ((0, 0), (4, 2 * BLK - CODES - 4)))


def bias_row(bias):
    b = bias.astype(F32)
    return jnp.stack([b[:, 0], jnp.zeros_like(b[:, 0]), b[:, 1]], axis=1).reshape(1, -1)


def pick_half(a, bit, axis=0):
    n = a.shape[axis] // 2
    return lax.dynamic_slice_in_dim(a, bit * n, n, axis)


def swap(a, axis, n, step=1):
    return lax.ppermute(a, axis, [(i, i ^ step) for i in range(n)])


def plus(*xs):
    total = xs[0].astype(F32)
    for x in xs[1:]:
        total = total + x.astype(F32)
    return total.astype(BF)


def after(x, *deps):
    return lax.optimization_barrier((x, *deps))[0]


def on_device(
    nz,
    nt,
    patches,
    gain_first,
    shift_first,
    attend_weight,
    attend_bias,
    offset_table,
    output_weight,
    output_bias,
    gain_second,
    shift_second,
    expand_weight,
    expand_bias,
    reduce_weight,
    reduce_bias,
    crop_counts,
    cotangent,
):
    fast = nt == 2 and nz == 4
    t, c, y, z = (lax.axis_index(a) for a in ("tensor", "core", "y", "z"))
    rows, d = patches.shape
    local = Local(rows)
    vec = lambda a: a.astype(F32).reshape(1, -1)
    vecs = jnp.stack([gain_first, shift_first, gain_second, shift_second, output_bias, reduce_bias]).astype(F32)
    bound = local.bound(attend_weight, attend_bias, offset_table)
    if fast:
        got, w_att_in, w_out_in = lax.optimization_barrier(
            (swap(bound, "tensor", nt), attend_weight, output_weight)
        )
        bound = jnp.maximum(bound, got)
        x_att = swap(pick_half(pick_half(w_att_in, c), y), "tensor", nt)
        x_out = swap(pick_half(w_out_in, c, 1), "tensor", nt)
        small = lambda a: [a, swap(a, "tensor", nt)]
        me = c * 2 + y
    else:
        w_att = [[lax.all_gather(attend_weight, "tensor", axis=1, tiled=True)]]
        w_out = [[lax.all_gather(output_weight, "tensor", axis=0, tiled=True)]]
        w_exp = [[lax.all_gather(expand_weight, "tensor", axis=1, tiled=True)]]
        w_red = [[lax.all_gather(reduce_weight, "tensor", axis=0, tiled=True)]]
        bound = lax.pmax(bound, "tensor")
        small = lambda a: [lax.all_gather(a, "tensor", axis=0, tiled=True)]
        me = c = 0 * c
    place = jnp.stack([t * local.windows, c, me]).astype(jnp.int32)
    local.plan(place, crop_counts, bound, vecs)
    bias, rel, b_exp = small(attend_bias), small(pad_table(offset_table)), small(expand_bias)
    xc, cotc, branch, first, live, idx = local.gather(patches, cotangent, vecs)

    if fast:
        xc, first, x_att, x_out, bias, rel, b_exp = lax.optimization_barrier(
            (xc, first, x_att, x_out, bias, rel, b_exp)
        )
    bias, b_exp = [bias_row(b) for b in bias], [vec(a) for a in b_exp]
    if fast:
        s_exp = after(pick_half(pick_half(expand_weight, c, 1), y, 1), x_att)
        first, s_exp = lax.optimization_barrier((first, s_exp))
        x_exp = swap(s_exp, "tensor", nt)
        y_att = swap(x_att, "y", 2)
        w_out = [[output_weight], [x_out, swap(x_out, "core", 2)]]
        qkv0, probs0, mixed0 = local.attend(live, first, bias[0], rel[0], [attend_weight])
        y_att, x_exp, mixed0 = lax.optimization_barrier((y_att, x_exp, mixed0))
        x_att = jnp.where(y == 0, jnp.concatenate([x_att, y_att], 0), jnp.concatenate([y_att, x_att], 0))
        w_att = [[attend_weight], [x_att, swap(x_att, "core", 2)]]
        y_exp = swap(x_exp, "y", 2)
        first, s_red = lax.optimization_barrier((first, after(pick_half(reduce_weight, c, 0), w_att[1][0])))
        x_red = swap(s_red, "tensor", nt)
        held = [(qkv0, probs0, mixed0)]
        before = [(mixed0, output_weight)]
    else:
        held, before = [], []
    qkv1, probs1, mixed1, middle, second = local.attend(
        live, first, bias[-1], rel[-1], w_att[-1], (xc, vecs, w_out[-1]), before
    )
    held.append((qkv1, probs1, mixed1))
    n = len(w_att)

    def bias_grad(a):
        a = a.reshape(-1, 3, HEAD_DIM)
        return jnp.stack([a[:, 0], a[:, 2]], axis=1)

    if fast:
        y_exp, x_red, second = lax.optimization_barrier((y_exp, x_red, second))
        x_exp = jnp.where(y == 0, jnp.concatenate([x_exp, y_exp], 1), jnp.concatenate([y_exp, x_exp], 1))
        second, x_exp = lax.optimization_barrier((second, x_exp))
        k0, s0, db0, red0, sg0 = local.feed(second, branch, [expand_weight], [reduce_weight], b_exp[0])
        e1 = [x_exp, swap(x_exp, "core", 2)]
        r1 = [x_red, swap(x_red, "core", 2)]
        k1, s1, db1, red1, mg, ag, v2 = local.feed(second, branch, e1, r1, b_exp[1], (live, middle, cotc, vecs, [sg0]))
        def split(keep, got):
            h = keep.shape[1] // 2
            return [plus(keep[:, i * h : (i + 1) * h], got[:, i * h : (i + 1) * h]) for i in range(2)]

        def first_leg(own, peer):
            return swap(peer[0], "tensor", nt), swap(jnp.stack([own[1][1], peer[1][1]]), "y", 2)

        def second_leg(own, peer, gx, gy):
            low = plus(own[0][1], gx[1])
            up = plus(own[0][0], gx[0])
            peer_b = plus(peer[1][0], gy[1])
            own_b = plus(own[1][0], gy[0])
            return up, swap(low, "y", 2), own_b, swap(peer_b, "tensor", nt)

        def z_first(up, gy, own_b, gx):
            a, b = plus(up, gy), plus(own_b, gx)
            return jnp.where(z % 2 == 0, a, b), jnp.where(z % 2 == 0, b, a)

        def z_second(keep, got):
            hi = z // 2
            total = lambda i: plus(pick_half(keep, i), pick_half(got, i))
            return total(hi), total(1 - hi)

        ff_peer = split(k1, swap(s1, "core", 2))
        ff_own = split(k0, swap(s0, "core", 2))
        ag, *ff = lax.optimization_barrier((ag, *ff_own, *ff_peer))
        ff_own, ff_peer = ff[:2], ff[2:]
        fx, fy = first_leg(ff_own, ff_peer)
        dq1, gk1, gs1, dba1, drel1 = local.back(ag, *held[1], first, w_out[1])
        fx, fy, dq1, gs1, ag = lax.optimization_barrier((fx, fy, dq1, gs1, ag))
        ff_up, fy, ff_b, fx = second_leg(ff_own, ff_peer, fx, fy)
        got1 = swap(gs1, "core", 2)
        dq0, gk0, gs0, dba0, drel0 = local.back(ag, *held[0], first, w_out[0])
        got1, fx, fy, dq0, gs0 = lax.optimization_barrier((got1, fx, fy, dq0, gs0))
        at_peer = split(gk1, got1)
        at_own = split(gk0, swap(gs0, "core", 2))
        ax, ay = first_leg(at_own, at_peer)
        ff_keep, ff_send = z_first(ff_up, fy, ff_b, fx)
        ff_got = swap(ff_send, "z", nz, 1)
        mg, *at4, ff_keep, ff_send = lax.optimization_barrier((mg, *at_own, *at_peer, ff_keep, ff_send))
        res, hi, lo, v1 = local.ends(live, xc, cotc, middle, mg, vecs, [red0, red1], [dq0, dq1], w_att)
        ax, ay, ff_got, res = lax.optimization_barrier((ax, ay, ff_got, res))
        up, ay, own_b, ax = second_leg(at_own, at_peer, ax, ay)
        ff_keep, ff_send = z_second(ff_keep, ff_got)
        ff_got = swap(ff_send, "z", nz, 2)
        v1, up, own_b, ff_keep, ff_send = lax.optimization_barrier((v1, up, own_b, ff_keep, ff_send))
        mine, other = pack(t.reshape(1).astype(jnp.int32), v1, v2, (db0, db1), (dba0, dba1), (drel0, drel1))
        ff_got, ax, ay, mine, other = lax.optimization_barrier((ff_got, ax, ay, mine, other))
        ids = jnp.stack([c, y, z]).astype(jnp.int32)
        keep, send = z_first(up, ay, own_b, ax)
        got = swap(send, "z", nz, 1)
        ff = plus(ff_keep, ff_got)
        ff2 = swap(ff, "z", nz, 2)
        tiny = plus(mine, swap(other.astype(BF), "tensor", nt))
        keep, ff, got, tiny = lax.optimization_barrier((keep, ff, got, tiny))
        keep, send = z_second(keep, got)
        got = swap(send, "z", nz, 2)
        tiny = plus(tiny, swap(tiny, "core", 2))
        keep, send, ff2, got, tiny = lax.optimization_barrier((keep, send, ff2, got, tiny))
        ff = jnp.stack([ff, ff2])
        att = plus(keep, got)
        ff1 = swap(ff, "z", nz, 1)
        att_y = swap(att, "y", 2)
        tiny = plus(tiny, swap(tiny, "y", 2))
        ff, att, att_y, tiny = lax.optimization_barrier((ff, att, att_y, tiny))
        att = jnp.stack([att, att_y])
        att2 = swap(att, "z", nz, 2)
        tiny = plus(tiny, swap(tiny, "z", nz, 1))
        att, ff1, tiny = lax.optimization_barrier((att, ff1, tiny))
        ff = jnp.concatenate([ff, ff1], 0)
        ffy = swap(ff, "y", 2)
        tiny = plus(tiny, swap(tiny, "z", nz, 2))
        ff, att2, tiny, res = lax.optimization_barrier((ff, att2, tiny, res))
        att = jnp.stack([att, att2])
        att1 = swap(att, "z", nz, 1)
        att, res = lax.optimization_barrier((att, res))
        result, input_grad = local.scatter(idx, res, hi, lo, patches, cotangent)
        att1, ffy, result = lax.optimization_barrier((att1, ffy, result))
        att = jnp.concatenate([att, att1], 0)
        att_far = swap(att, "core", 2)
        ff, ffy, att_far = lax.optimization_barrier((ff, ffy, att_far))
        ff = jnp.stack([ff, ffy])
        far = swap(ff, "core", 2)
        g_att, g_out = place_attend(ids, att, att_far, d)
        g_exp, g_red = place_feed(ids, ff, far, d, 4 * GW)
        tiny = tiny.astype(F32)
        gb_exp, gb_att = tiny[0], bias_grad(tiny[1, : 3 * GW])
        vectors, g_rel = tiny[2:8, : d // 2], tiny[8 : 8 + drel0.shape[0], :CODES]
    else:
        *tiles, gb_exp, red, mg, ag, v2 = local.feed(second, branch, w_exp[0], w_red[0], b_exp[0], (live, middle, cotc, vecs, []))
        dq, ga, dba, drel = local.back(ag, *held[0], first, w_out[0])
        res, hi, lo, v1 = local.ends(live, xc, cotc, middle, mg, vecs, [red], [dq], w_att)
        result, input_grad = local.scatter(idx, res, hi, lo, patches, cotangent)
        ff = jnp.concatenate(tiles, 0)
        g_exp = ff[:, 0:d].transpose(1, 0, 2).reshape(d, -1)
        g_red = ff[:, d:].transpose(0, 2, 1).reshape(-1, d)
        g_att = ga[0 : dq.shape[1] // GW, 0:d].transpose(1, 0, 2).reshape(d, -1)
        g_out = ga[dq.shape[1] // GW].reshape(2, d, d // 2).transpose(1, 0, 2).reshape(d, d)
        dp = ("z", "y", "core")

        def total(a, axis):
            a = lax.psum_scatter(a.astype(BF), "tensor", scatter_dimension=axis, tiled=True)
            return lax.psum(a, dp).astype(F32)

        vectors = total(jnp.stack([v1[0], v1[1], v2[2], v2[0], v2[1], v1[2]]), 1)
        gb_att, g_rel, gb_exp = total(bias_grad(dba), 0), total(drel[:, :CODES], 0), total(gb_exp[0], 0)
        g_exp, g_att, g_out, g_red = total(g_exp, 1), total(g_att, 1), total(g_out, 0), total(g_red, 0)

    return (
        result,
        input_grad,
        vectors[0],
        vectors[1],
        g_att,
        gb_att,
        g_rel,
        g_out,
        vectors[2],
        vectors[3],
        vectors[4],
        g_exp,
        gb_exp,
        g_red,
        vectors[5],
    )


def solution(mesh):
    nt = mesh.shape["tensor"]
    nz = mesh.shape["dp"] // 4
    grid = Mesh(mesh.devices.reshape(nz, 2, 2, nt), ("z", "y", "core", "tensor"))
    dp = ("z", "y", "core")
    rows = P(dp + ("tensor",), None)
    in_specs = (
        rows,
        P(),
        P(),
        P(None, "tensor"),
        P("tensor", None, None),
        P("tensor", None),
        P("tensor", None),
        P(),
        P(),
        P(),
        P(None, "tensor"),
        P("tensor"),
        P("tensor", None),
        P(),
        P(dp),
        rows,
    )
    out_specs = (
        rows,
        rows,
        P("tensor"),
        P("tensor"),
        P(None, "tensor"),
        P("tensor", None, None),
        P("tensor", None),
        P("tensor", None),
        P("tensor"),
        P("tensor"),
        P("tensor"),
        P(None, "tensor"),
        P("tensor"),
        P("tensor", None),
        P("tensor"),
    )
    return jax.shard_map(partial(on_device, nz, nt), mesh=grid, in_specs=in_specs, out_specs=out_specs, check_vma=False)
```

```python
from functools import partial

import jax
import jax.numpy as jnp
import numpy as np
from jax import lax
from jax.experimental import pallas as pl
from jax.experimental.pallas import tpu as pltpu
from jax.sharding import Mesh
from jax.sharding import PartitionSpec as P

HEAD_DIM = 32
EPSILON = 1e-05
MASKED = 30000.0
SIDE = 7
SLOTS = SIDE * SIDE
BLK = 128
GROUP = 4
GW = 3 * GROUP * HEAD_DIM
BF = jnp.bfloat16
F32 = jnp.float32
VMEM_LIMIT = 60 * 1024 * 1024


def dot(a, b):
    return jnp.dot(a, b, preferred_element_type=F32)


def dot_nt(a, b):
    return lax.dot_general(a, b, (((1,), (1,)), ((), ())), preferred_element_type=F32)


def dot_tn(a, b):
    return lax.dot_general(a, b, (((0,), (0,)), ((), ())), preferred_element_type=F32)


def kind_tables():
    slot = -np.ones((2, BLK), np.int64)
    owner = 100 + np.arange(BLK)[None].repeat(2, 0)
    nine = np.arange(9)
    nine = (nine // 3) * SIDE + nine % 3
    for w in range(2):
        slot[0, w * SLOTS : (w + 1) * SLOTS] = np.arange(SLOTS)
        owner[0, w * SLOTS : (w + 1) * SLOTS] = w
    for w in range(3):
        at = 2 * SLOTS + 9 * w
        slot[0, at : at + 9] = nine
        owner[0, at : at + 9] = 2 + w
    for w in range(14):
        slot[1, 9 * w : 9 * w + 9] = nine
        owner[1, 9 * w : 9 * w + 9] = w
    pick = (slot[:, :, None] == np.arange(64)[None, None, :]).astype(np.float32)
    same = owner[:, :, None] == owner[:, None, :]
    mask = np.where(same, 0.0, -1e30).astype(np.float32)
    return pick, mask


def stride_tables():
    slot, _ = kind_tables()
    s = np.where(slot.sum(2) > 0, slot.argmax(2), -1)
    place = np.where(s >= 0, 13 * (s // SIDE) + s % SIDE, -1)
    up = (place[:, :, None] == np.arange(BLK)).astype(np.float32)
    down = ((84 - place)[:, :, None] == np.arange(BLK)) & (place >= 0)[:, :, None]
    return up, down.astype(np.float32).transpose(0, 2, 1)


def group_perm():
    perm = np.zeros((GW, GW), np.float32)
    for h in range(GROUP):
        for p in range(3):
            for e in range(HEAD_DIM):
                perm[(h * 3 + p) * HEAD_DIM + e, (p * GROUP + h) * HEAD_DIM + e] = 1.0
    return perm


PLAN_HEAD = 8
G1, B1, G2, B2, OB, RB = (slice(i, i + 1) for i in range(6))
AT_C, AT_ME = 6, 7


def bound_kernel(w, bias, table, out):
    width = w.shape[1]
    q = jnp.zeros((1, BLK), F32)
    k = jnp.zeros((1, BLK), F32)
    for start in range(0, width, BLK):
        size = min(BLK, width - start)
        x = w[:, start : start + size]
        gram = dot_tn(x, x)
        a = lax.broadcasted_iota(jnp.int32, (size, size), 0) >> 5
        b = lax.broadcasted_iota(jnp.int32, (size, size), 1) >> 5
        sums = jnp.sum(jnp.where(a == b, gram * gram, 0.0), axis=0, keepdims=True)
        lane = lax.broadcasted_iota(jnp.int32, (1, size), 1) >> 5
        for i in range(size // HEAD_DIM):
            part = (start // HEAD_DIM + i) % 3
            top = jnp.max(jnp.where(lane == i, sums, 0.0), axis=1, keepdims=True)
            if part == 0:
                q = jnp.maximum(q, top)
            if part == 1:
                k = jnp.maximum(k, top)
    qb = bias[...].astype(F32)
    col = lax.broadcasted_iota(jnp.int32, qb.shape, 1)
    qb = jnp.sum(jnp.where(col < HEAD_DIM, qb * qb, 0.0), axis=1, keepdims=True)
    qb = jnp.max(qb, axis=0, keepdims=True)
    top = jnp.max(jnp.max(jnp.abs(table[...].astype(F32)), axis=1, keepdims=True), axis=0, keepdims=True)
    out[...] = jnp.zeros_like(out)
    for i, v in enumerate((q, k, qb, top)):
        out[i : i + 1, :] = jnp.broadcast_to(v, (1, BLK))


def plan_kernel(windows, images, per_chunk, where, counts, bounds, vecs, out):
    d = vecs.shape[1]
    g1, b1 = vecs.at[G1], vecs.at[B1]
    big = bounds[...]

    def root4(v):
        return jnp.sqrt(jnp.sqrt(HEAD_DIM * v))

    reach = jnp.sqrt(float(d)) * jnp.max(jnp.abs(g1[...]), axis=1, keepdims=True)
    reach = 1.02 * (reach + jnp.sqrt(jnp.sum(b1[...] * b1[...], axis=1, keepdims=True)))
    q = 1.01 * (reach * root4(big[0:1, :]) + jnp.sqrt(big[2:3, :])) * HEAD_DIM**-0.5
    top = 1.01 * q * (reach * root4(big[1:2, :])) + big[3:4, :]
    safe = jnp.where(2.0 * top < MASKED - 500.0, 1, 0)
    bad = 1 - jnp.min(safe)
    first = where[0]
    nf = jnp.int32(0)
    nq = jnp.int32(0)
    for i in range(2 * windows + PLAN_HEAD, out.shape[0]):
        out[i] = 0
    for w in range(windows):
        place = first + w
        start = jnp.int32(0)
        offset = jnp.int32(-1)
        for i in range(images):
            total = counts[i] + 2
            inside = (place >= start) & (place < start + total)
            offset = jnp.where(inside, place - start, offset)
            start = start + total
        present = offset >= 0
        whole = present & (offset < 2)
        full = present & (whole | (bad > 0))
        part = present & (~whole) & (bad == 0)
        out[PLAN_HEAD + 2 * windows + w] = whole.astype(jnp.int32)

        @pl.when(full)
        def _():
            out[PLAN_HEAD + nf] = w

        @pl.when(part)
        def _():
            out[PLAN_HEAD + windows + nq] = w

        nf = nf + full.astype(jnp.int32)
        nq = nq + part.astype(jnp.int32)
    n0 = (nf + 1) >> 1
    left = jnp.maximum(nq - 3 * n0, 0)
    n1 = jnp.int32(0)
    for i in range(-(-windows // 14)):
        n1 = n1 + (left > 14 * i).astype(jnp.int32)
    nb = n0 + n1
    chunks = jnp.int32(1)
    for i in range(1, windows):
        chunks = chunks + (nb > per_chunk * i).astype(jnp.int32)
    for i, v in enumerate((nb, n0, chunks, bad, nf, nq, where[1], where[2])):
        out[i] = v


def norm_stats(x):
    mean = jnp.mean(x, axis=1, keepdims=True)
    c = x - mean
    scale = lax.rsqrt(jnp.mean(c * c, axis=1, keepdims=True) + EPSILON)
    return c * scale, scale


def norm_back(grad, normal, scale, gain):
    inner = grad * gain
    mean = jnp.mean(inner, axis=1, keepdims=True)
    proj = jnp.mean(inner * normal, axis=1, keepdims=True)
    return scale * (inner - mean - normal * proj)


def gather_kernel(windows, meta, slots, patches, cot, vecs, xc, cotc, branch, first, live, idx_row, idx, pick):
    rows = xc.shape[0]
    total = patches.shape[0]
    blocks = rows // BLK
    spots = lax.broadcasted_iota(jnp.int32, (BLK, total), 1)
    chunk = pl.program_id(0)
    n0 = meta[1]
    r = lax.broadcasted_iota(jnp.int32, (BLK, 1), 0)

    def listed(first_at, count, i):
        ok = (i >= 0) & (i < count)
        w = meta[first_at + jnp.where(ok, i, 0)]
        return jnp.where(ok, w, -1)

    def spread(ends, wins):
        base = jnp.full((BLK, 1), -1, jnp.int32)
        for end, w in reversed(list(zip(ends, wins))):
            base = jnp.where(r < end, w, base)
        return base

    def one(b, carry):
        at = pl.ds(pl.multiple_of(b * BLK, BLK), BLK)
        block = chunk * blocks + b
        kind0 = block < n0

        @pl.when(kind0)
        def _():
            wins = [listed(PLAN_HEAD, meta[4], 2 * block + i) for i in range(2)]
            wins += [listed(PLAN_HEAD + windows, meta[5], 3 * block + i) for i in range(3)]
            ends = [SLOTS, 2 * SLOTS] + [2 * SLOTS + 9 * (i + 1) for i in range(3)]
            base = spread(ends, wins)
            slot = slots[0]
            where_whole = [
                jnp.where(w >= 0, meta[PLAN_HEAD + 2 * windows + jnp.maximum(w, 0)], 0) for w in wins[:2]
            ] + [jnp.int32(1)] * 3
            sure = spread(ends, where_whole) > 0
            ok = base >= 0
            idx[...] = jnp.where(ok, base * SLOTS + slot, -1)
            live[at, :] = jnp.where(ok & (sure | (slots[2] > 0)), 1.0, 0.0)

        @pl.when(jnp.logical_not(kind0))
        def _():
            start = 3 * n0 + 14 * (block - n0)
            wins = [listed(PLAN_HEAD + windows, meta[5], start + i) for i in range(14)]
            base = spread([9 * (i + 1) for i in range(14)], wins)
            ok = base >= 0
            idx[...] = jnp.where(ok, base * SLOTS + slots[1], -1)
            live[at, :] = jnp.where(ok, 1.0, 0.0)

        here = idx[...]
        wide = jnp.broadcast_to(here.astype(F32), (BLK, BLK))
        idx_row[0, :, at] = wide.T[0:1, :].astype(jnp.int32)
        pick[at, :] = (spots == here).astype(F32).astype(BF)
        return carry

    lax.fori_loop(0, blocks, one, 0)
    x = dot(pick[...], patches[...])
    xc[...] = x.astype(BF)
    up = dot(pick[...], cot[...])
    cotc[...] = up.astype(BF)
    branch[...] = (up * live[...]).astype(BF)
    for b in range(blocks):
        at = slice(b * BLK, (b + 1) * BLK)
        n, _ = norm_stats(xc[at, :].astype(F32))
        first[at, :] = (n * vecs[G1] + vecs[B1]).astype(BF)


def lane_head(shape, axis):
    return lax.broadcasted_iota(jnp.int32, shape, axis) >> 5


def spread_rows(x):
    h = lane_head(x.shape, 1)
    zero = jnp.zeros_like(x)
    return jnp.concatenate([jnp.where(h == i, x, zero) for i in range(GROUP)], axis=0)


def spread_cols(xt):
    h = lane_head(xt.shape, 0)
    zero = jnp.zeros_like(xt)
    return jnp.concatenate([jnp.where(h == i, xt, zero) for i in range(GROUP)], axis=1)


def fold_rows(x):
    h = lane_head((BLK, BLK), 1)
    out = x[0:BLK]
    for i in range(1, GROUP):
        out = jnp.where(h == i, x[i * BLK : (i + 1) * BLK], out)
    return out


def run_copies(pairs, sem):
    copies = [pltpu.make_async_copy(x, y, sem.at[i]) for i, (x, y) in enumerate(pairs)]
    for x in copies:
        x.start()
    for x in copies:
        x.wait()


def attend_kernel(pieces, groups, tail, prior, meta, live, first, perm, pick, mask, bias, rel, *rest):
    w, rest = rest[:pieces], rest[pieces:]
    if tail:
        (xc, vecs), rest = rest[:2], rest[2:]
        before, rest = rest[:prior], rest[prior:]
        w_before, rest = rest[:prior], rest[prior:]
        w_out, rest = rest[:pieces], rest[pieces:]
    k = 3 + prior if tail else 2
    sources, rest = rest[:k], rest[k:]
    loaded = (live, first) + ((xc, *before) if tail else ())
    if tail:
        qkv_out, probs_out, mixed_out, middle_out, second_out, table, qkv, probs, mixed, in_sem, sem = rest[:11]
        middle, second, att = rest[11:]
    else:
        qkv_out, probs_out, mixed_out, table, qkv, probs, mixed, in_sem, sem = rest
    rows, d = first.shape
    blocks = rows // BLK
    step = pl.program_id(0)
    chunks = meta[2]
    c = meta[AT_C]
    n0 = meta[1]
    near = pl.ds(pl.multiple_of(c * (d // 2), BLK), d // 2)
    far = pl.ds(pl.multiple_of((1 - c) * (d // 2), BLK), d // 2)
    last = groups if tail else groups - 1

    def reload(chunk):
        @pl.when(chunks > 1)
        def _():
            at = pl.ds(pl.multiple_of(chunk * rows, rows), rows)
            run_copies([(x.at[at, :], y) for x, y in zip(sources, loaded)], in_sem)

    def stores(chunk, g):
        at = pl.ds(pl.multiple_of(chunk * rows, rows), rows)
        cols = pl.ds(pl.multiple_of(g * GW, BLK), GW)
        return (
            pltpu.make_async_copy(qkv, qkv_out.at[at, cols], sem.at[0]),
            pltpu.make_async_copy(probs, probs_out.at[pl.ds(chunk * blocks, blocks), g], sem.at[1]),
        )

    def group(i, carry):
        chunk = chunks - 1 - i
        reload(chunk)
        if pieces == 1:
            v = dot(first[...], w[0][...])
        else:
            v = dot(first[:, near], w[0][...]) + dot(first[:, far], w[1][...])
        v = v + bias[...]
        block = lax.broadcasted_iota(jnp.int32, (1, GW), 1) >> 5
        is_q = block == 0
        for j in range(3, 3 * GROUP, 3):
            is_q = is_q | (block == j)
        v = (v * jnp.where(is_q, HEAD_DIM**-0.5, 1.0)).astype(BF)

        @pl.when((step > 0) | (i > 0))
        def _():
            for x in stores(0, 0):
                x.wait()

        qkv[...] = dot(v, perm[...]).astype(BF)
        stores(chunk, step)[0].start()
        for b in range(blocks):
            at = slice(b * BLK, (b + 1) * BLK)
            kind = jnp.where(chunk * blocks + b < n0, 0, 1)
            q = qkv[at, 0:BLK]
            k = qkv[at, BLK : 2 * BLK]
            v = qkv[at, 2 * BLK : 3 * BLK]
            st = dot_nt(spread_rows(k), q) + table[kind].astype(F32)
            dead = (live[at, :] - 1.0) * MASKED
            st = st.reshape(GROUP, BLK, BLK) + jnp.where(meta[3] > 0, dead, 0.0)[None]
            peak = jnp.max(st, axis=1, keepdims=True)
            e = jnp.exp(st - peak)
            p = (e * (1.0 / jnp.sum(e, axis=1, keepdims=True))).astype(BF)
            p = p.reshape(GROUP * BLK, BLK)
            probs[b] = p
            vt = v.astype(F32).T.astype(BF)
            m = dot(spread_cols(vt), p).T.astype(BF)
            mixed[chunk, at, pl.ds(pl.multiple_of(step * BLK, BLK), BLK)] = m
        stores(chunk, step)[1].start()
        return carry

    @pl.when(step < groups)
    def _():
        places = []
        for h in range(GROUP):
            row = rel[pl.ds(step * GROUP + h, 1), :]
            row = pltpu.roll(jnp.broadcast_to(row, (BLK, 2 * BLK)), 2 * BLK - 88, 1, stride=1, stride_axis=0)
            places.append(row[:, 0:BLK].astype(BF))
        for kind in range(2):
            e = pick[kind]
            for h in range(GROUP):
                half = dot(e, places[h]).astype(BF)
                t = dot_nt(half, e) + mask[kind].astype(F32)
                table[kind, h * BLK : (h + 1) * BLK, :] = t.astype(BF)
        lax.fori_loop(0, chunks, group, 0)

    def project(i, carry):
        chunk = chunks - 1 - i
        reload(chunk)
        if pieces == 1:
            att[...] = dot(mixed[chunk], w_out[0][...])
        else:
            att[:, near] = dot(mixed[chunk], w_out[0][...])
            att[:, far] = dot(mixed[chunk], w_out[1][...])
        for m, v in zip(before, w_before):
            att[...] = att[...] + dot(m[...], v[...])
        for b in range(blocks):
            at = slice(b * BLK, (b + 1) * BLK)
            m = xc[at, :].astype(F32) + live[at, :] * (att[at, :] + vecs[OB])
            middle[at, :] = m
            nrm, _ = norm_stats(m)
            second[at, :] = (nrm * vecs[G2] + vecs[B2]).astype(BF)
        at = pl.ds(pl.multiple_of(chunk * rows, rows), rows)
        run_copies([(middle, middle_out.at[at, :]), (second, second_out.at[at, :])], in_sem)
        return carry

    def give(chunk):
        at = pl.ds(pl.multiple_of(chunk * rows, rows), rows)
        return pltpu.make_async_copy(mixed.at[chunk], mixed_out.at[at, :], sem.at[2])

    if tail:

        @pl.when(step == groups)
        def _():
            lax.fori_loop(0, chunks, project, 0)

    @pl.when(step == last)
    def _():
        for x in stores(0, 0):
            x.wait()

        def out(i, carry):
            give(i).start()
            give(i).wait()
            return carry

        lax.fori_loop(0, chunks, out, 0)


def feed_kernel(tiles, pieces, last, prior, meta, second, branch, *rest):
    we, wr, rest = rest[:pieces], rest[pieces : 2 * pieces], rest[2 * pieces :]
    be, rest = rest[0], rest[1:]
    if last:
        (live, middle, cotc, vecs), rest = rest[:4], rest[4:]
        sg_in, rest = rest[:prior], rest[prior:]
    grads, rest = rest[:tiles], rest[tiles:]
    dbe, red = rest[:2]
    if last:
        (mg, ag, vec), rest = rest[2:5], rest[5:]
    else:
        (sg,), rest = rest[2:3], rest[3:]
    sec, br, e_buf, r_buf, gbuf, ra, sa, half, sem, w_sem, g_sem = rest[:11]
    if last:
        mid_buf, cot_buf, live_buf, sg_buf = rest[11:]
    ch, d = sec.shape
    wide = e_buf.shape[2]
    c0, me = meta[AT_C], meta[AT_ME]
    y = me & 1
    chunks = meta[2]

    def move(a, b, i):
        return pltpu.make_async_copy(a, b, sem.at[i])

    def loads(c):
        rows = pl.ds(pl.multiple_of(c * ch, ch), ch)
        return [move(second.at[rows, :], sec, 0), move(branch.at[rows, :], br, 1)]

    def weights(i):
        if pieces == 1:
            at = pl.ds(pl.multiple_of((i ^ c0) * wide, BLK), wide)
            a, b = we[0].at[:, at], wr[0].at[at, :]
        else:
            a, b = we[i], wr[i]
        return [
            pltpu.make_async_copy(a, e_buf.at[i], w_sem.at[2 * i]),
            pltpu.make_async_copy(b, r_buf.at[i], w_sem.at[2 * i + 1]),
        ]

    def extras(c):
        rows = pl.ds(pl.multiple_of(c * ch, ch), ch)
        out = [
            move(middle.at[rows, :], mid_buf, 2),
            move(cotc.at[rows, :], cot_buf, 3),
            move(live.at[rows, :], live_buf, 4),
        ]
        return out + [move(x.at[rows, :], sg_buf, 5) for x in sg_in]

    def store(i):
        return pltpu.make_async_copy(gbuf.at[i], grads[i], g_sem.at[i])

    if last:
        vec[...] = jnp.zeros_like(vec)

    def chunk(c, carry):
        rows = pl.ds(pl.multiple_of(c * ch, ch), ch)
        for x in loads(c):
            x.start()

        @pl.when(c == 0)
        def _():
            for i in range(tiles):
                for x in weights(i):
                    x.start()

        if last:
            for x in extras(c):
                x.start()
        for x in loads(c):
            x.wait()

        def tile(t, carry):
            for i in range(tiles):

                @pl.when((t == i) & (c == 0))
                def _():
                    for x in weights(i):
                        x.wait()

            at = pl.ds(pl.multiple_of((t ^ c0) * wide, BLK), wide)
            e, r = e_buf[t], r_buf[t]
            u = dot(sec[...], e) + be[:, at]
            cdf = 0.5 * (1.0 + lax.erf(u * 0.7071067811865476))
            h = (u * cdf).astype(BF)
            slope = cdf + u * (jnp.exp(-0.5 * u * u) * 0.3989422804014327)
            pg = (dot_nt(br[...], r) * slope).astype(BF)
            grad_b = jnp.sum(pg.astype(F32), axis=0, keepdims=True)

            def put(low, g):
                n = wide // 2
                for i in range(2):
                    ref = gbuf.at[t, i ^ y, low : low + d, :]
                    part = g[:, i * n : (i + 1) * n]

                    @pl.when(c == 0)
                    def _():
                        ref[...] = part.astype(BF)

                    @pl.when(c > 0)
                    def _():
                        ref[...] = (ref[...].astype(F32) + part).astype(BF)

            put(0, dot_tn(sec[...], pg))
            put(d, dot_tn(br[...], h))

            @pl.when(c == 0)
            def _():
                dbe[:, at] = grad_b

            @pl.when(c > 0)
            def _():
                dbe[:, at] = dbe[:, at] + grad_b

            red_t = dot(h, r)
            sg_t = dot_nt(pg, e)

            @pl.when(t == 0)
            def _():
                ra[...] = red_t
                sa[...] = sg_t

            @pl.when(t > 0)
            def _():
                ra[...] = ra[...] + red_t
                sa[...] = sa[...] + sg_t

            for i in range(tiles):

                @pl.when((t == i) & (c == chunks - 1))
                def _():
                    store(i).start()

            return carry

        lax.fori_loop(0, tiles, tile, 0)
        half[0] = ra[...].astype(BF)
        outs = [move(half.at[0], red.at[rows, :], 0)]
        outs[0].start()
        if not last:
            half[1] = sa[...].astype(BF)
            outs.append(move(half.at[1], sg.at[rows, :], 1))
            outs[1].start()
        else:
            for x in extras(c):
                x.wait()
            for b in range(ch // BLK):
                at = slice(b * BLK, (b + 1) * BLK)
                nrm, scale = norm_stats(mid_buf[at, :])
                g = sa[at, :]
                if prior:
                    g = g + sg_buf[at, :].astype(F32)
                m = cot_buf[at, :].astype(F32) + norm_back(g, nrm, scale, vecs[G2])
                ra[at, :] = m
                kept = m * live_buf[at, :]
                half[1, at, :] = kept.astype(BF)
                vec[0:1, :] = vec[0:1, :] + jnp.sum(g * nrm, axis=0, keepdims=True)
                vec[1:2, :] = vec[1:2, :] + jnp.sum(g, axis=0, keepdims=True)
                vec[2:3, :] = vec[2:3, :] + jnp.sum(kept, axis=0, keepdims=True)
            outs += [move(half.at[1], ag.at[rows, :], 1), move(ra, mg.at[rows, :], 2)]
            for x in outs[1:]:
                x.start()
        for x in outs:
            x.wait()
        return carry

    lax.fori_loop(0, chunks, chunk, 0)
    for i in range(tiles):
        store(i).wait()


def back_kernel(pieces, groups, split, meta, ag, perm, pick, pick_t, qkv, probs, mixed, first, *rest):
    w_out, rest = rest[:pieces], rest[pieces:]
    sources, rest = rest[:5], rest[5:]
    dqkv, rest = rest[0], rest[1:]
    grads, rest = rest[: 2 if split else 1], rest[2 if split else 1 :]
    dba, drel, dperm, dmix, table, out, in_sem, sem = rest
    rows, d = ag.shape
    blocks = rows // BLK
    step = pl.program_id(0)
    chunks = meta[2]
    n0 = meta[1]
    c, me = meta[AT_C], meta[AT_ME]
    half = d // 2
    stays = (step >> 1) == (me >> 1)

    def reload(chunk):
        @pl.when(chunks > 1)
        def _():
            at = pl.ds(pl.multiple_of(chunk * rows, rows), rows)
            g = jnp.minimum(step, groups - 1)
            cols = pl.ds(pl.multiple_of(g * GW, BLK), GW)
            ag_h, qkv_h, probs_h, mixed_h, first_h = sources
            pairs = [(ag_h.at[at, :], ag), (qkv_h.at[at, cols], qkv), (mixed_h.at[at, :], mixed), (first_h.at[at, :], first)]
            pairs += [(probs_h.at[pl.ds(chunk * blocks, blocks), g], probs.at[:, 0])]
            run_copies(pairs, in_sem)

    def store(chunk, g):
        at = pl.ds(pl.multiple_of(chunk * rows, rows), rows)
        cols = pl.ds(pl.multiple_of(g * GW, BLK), GW)
        return pltpu.make_async_copy(out, dqkv.at[at, cols], sem.at[0])

    def put(i, ref, value):
        @pl.when(i == 0)
        def _():
            ref[...] = value.astype(ref.dtype)

        @pl.when(i > 0)
        def _():
            ref[...] = (ref[...].astype(F32) + value).astype(ref.dtype)

    def put_grad(i, low, high, value):
        if not split:
            put(i, grads[0].at[0, low:high, :], value)
            return

        @pl.when(stays)
        def _():
            put(i, grads[0].at[0, low:high, :], value)

        @pl.when(jnp.logical_not(stays))
        def _():
            put(i, grads[1].at[0, low:high, :], value)

    def weights(i, carry):
        reload(chunks - 1 - i)
        wide = groups * BLK
        for j in range(2):
            put_grad(i, j * wide, (j + 1) * wide, dot_tn(mixed[...], ag[:, j * half : (j + 1) * half]))
        return carry

    def heads(i, carry):
        chunk = chunks - 1 - i
        reload(chunk)
        if pieces == 1:
            dmix[...] = dot_nt(ag[...], w_out[0][...]).astype(BF)
        else:
            near = pl.ds(pl.multiple_of(c * half, BLK), half)
            far = pl.ds(pl.multiple_of((1 - c) * half, BLK), half)
            dmix[...] = (dot_nt(ag[:, near], w_out[0][...]) + dot_nt(ag[:, far], w_out[1][...])).astype(BF)
        for b in range(blocks):
            at = slice(b * BLK, (b + 1) * BLK)
            kind = jnp.where(chunk * blocks + b < n0, 0, 1)
            q = qkv[at, 0:BLK]
            k = qkv[at, BLK : 2 * BLK]
            v = qkv[at, 2 * BLK : 3 * BLK]
            do = dmix[at, :]
            p = probs[b, 0]
            dp = dot_nt(spread_rows(v), do).reshape(GROUP, BLK, BLK)
            pf = p.astype(F32).reshape(GROUP, BLK, BLK)
            x = pf * dp
            ds = x - pf * jnp.sum(x, axis=1, keepdims=True)
            ds = ds.astype(BF).reshape(GROUP * BLK, BLK)
            table[kind] = table[kind] + ds.astype(F32)
            dv = fold_rows(dot(p, do))
            dk = fold_rows(dot(ds, q))
            kt = k.astype(F32).T.astype(BF)
            dq = (dot(spread_cols(kt), ds) * HEAD_DIM**-0.5).T
            dperm[at, 0:BLK] = dq.astype(BF)
            dperm[at, BLK : 2 * BLK] = dk.astype(BF)
            dperm[at, 2 * BLK : 3 * BLK] = dv.astype(BF)
        x = dot_nt(dperm[...], perm[...]).astype(BF)

        @pl.when((step > 0) | (i > 0))
        def _():
            store(0, 0).wait()

        out[...] = x
        store(chunk, step).start()
        put_grad(i, 0, d, dot_tn(first[...], x))
        put(i, dba, jnp.sum(x.astype(F32), axis=0, keepdims=True))
        return carry

    @pl.when(step == groups)
    def _():
        lax.fori_loop(0, chunks, weights, 0)
        store(0, 0).wait()

    @pl.when(step < groups)
    def _():
        table[...] = jnp.zeros_like(table)
        lax.fori_loop(0, chunks, heads, 0)
        for h in range(GROUP):
            total = jnp.zeros((BLK, BLK), F32)
            for kind in range(2):
                a = table[kind, h * BLK : (h + 1) * BLK, :]
                a = dot(a.astype(BF), pick[kind]).astype(BF)
                total = total + dot(pick_t[kind], a)
            wide = jnp.concatenate([total, jnp.zeros_like(total)], axis=1)
            wide = pltpu.roll(wide, 0, 1, stride=1, stride_axis=0)
            drel[pl.ds(step * GROUP + h, 1), :] = jnp.sum(wide, axis=0, keepdims=True)


def row_tiles(rows, size=384):
    return [(a, min(size, rows - a)) for a in range(0, rows, size)]


def ends_kernel(pieces, meta, live, xc, cotc, mg, vecs, *rest):
    n = len(pieces)
    dqkv, rest = rest[:n], rest[n:]
    w = []
    for k in pieces:
        w.append(rest[:k])
        rest = rest[k:]
    hi, lo, vec, fg = rest
    rows, d = xc.shape
    blocks = rows // BLK
    chunk = pl.program_id(0)
    c = meta[AT_C]
    half = d // 2

    @pl.when(chunk == 0)
    def _():
        vec[...] = jnp.zeros_like(vec)

    for s in range(n):
        if len(w[s]) == 1:
            v = dot_nt(dqkv[s][...], w[s][0][...])
            fg[...] = v if s == 0 else fg[...] + v
        else:
            for i in range(2):
                cols = pl.ds(pl.multiple_of((c if i == 0 else 1 - c) * half, BLK), half)
                fg[:, cols] = fg[:, cols] + dot_nt(dqkv[s][...], w[s][i][...])

    for b in range(blocks):
        at = slice(b * BLK, (b + 1) * BLK)
        keep = live[at, :]
        nrm, scale = norm_stats(xc[at, :].astype(F32))
        g = fg[at, :]
        up = cotc[at, :].astype(F32)
        delta = mg[at, :] - up + norm_back(g, nrm, scale, vecs[G1])
        top = delta.astype(BF)
        hi[at, :] = top
        lo[at, :] = (delta - top.astype(F32)).astype(BF)
        vec[0:1, :] = vec[0:1, :] + jnp.sum(g * nrm, axis=0, keepdims=True)
        vec[1:2, :] = vec[1:2, :] + jnp.sum(g, axis=0, keepdims=True)
        vec[2:3, :] = vec[2:3, :] + jnp.sum(up * keep, axis=0, keepdims=True)


def result_kernel(prior, meta, idx, live, middle, vecs, patches, *rest):
    red, (result, res) = rest[:prior], rest[prior:]
    rows = middle.shape[0]
    chunk = pl.program_id(0)
    for b in range(rows // BLK):
        at = slice(b * BLK, (b + 1) * BLK)
        reduced = vecs[RB]
        for x in red:
            reduced = reduced + x[at, :].astype(F32)
        res[at, :] = (middle[at, :] + live[at, :] * reduced).astype(BF)
    for start, size in row_tiles(patches.shape[0]):
        at = slice(start, start + size)
        spots = start + lax.broadcasted_iota(jnp.int32, (size, rows), 0)
        hit = (spots == idx[0]).astype(F32)
        here = jnp.sum(hit, axis=1, keepdims=True) > 0.0
        new = dot(hit.astype(BF), res[...])

        @pl.when(chunk == 0)
        def _():
            result[at, :] = jnp.where(here, new, patches[at, :].astype(F32)).astype(BF)

        @pl.when(chunk > 0)
        def _():
            result[at, :] = jnp.where(here, new, result[at, :].astype(F32)).astype(BF)


def scatter_kernel(meta, idx, hi, lo, cot, input_grad):
    rows = hi.shape[0]
    chunk = pl.program_id(0)
    for start, size in row_tiles(cot.shape[0]):
        at = slice(start, start + size)
        spots = start + lax.broadcasted_iota(jnp.int32, (size, rows), 0)
        put = (spots == idx[0]).astype(F32).astype(BF)
        grad = dot(put, hi[...]) + dot(put, lo[...])

        @pl.when(chunk == 0)
        def _():
            input_grad[at, :] = cot[at, :].astype(F32) + grad

        @pl.when(chunk > 0)
        def _():
            input_grad[at, :] = input_grad[at, :] + grad


SMEM = pl.BlockSpec(memory_space=pltpu.SMEM)
ANY = pl.BlockSpec(memory_space=pl.ANY)
PACK = 24


def pack_kernel(where, v1, v2, *refs):
    n = 2
    db, dba, drel = (refs[i * n : (i + 1) * n] for i in range(3))
    outs = refs[3 * n :]
    d = v1.shape[1]
    half = d // 2
    for s in range(n):
        t = where[0] if s == 0 else 1 - where[0]
        cols = pl.ds(pl.multiple_of(t * half, BLK), half)
        out = outs[s]
        out[...] = jnp.zeros_like(out)
        out[0:1, :] = db[s][...].astype(BF).astype(F32)
        out[1:2, 0 : dba[s].shape[1]] = dba[s][...]
        for i, (v, r) in enumerate(((v1, 0), (v1, 1), (v2, 2), (v2, 0), (v2, 1), (v1, 2))):
            out[2 + i : 3 + i, 0:half] = v[r : r + 1, cols]
        k = drel[s].shape[0]
        out[8 : 8 + k, 0 : drel[s].shape[1]] = drel[s][...]


def pack(t, v1, v2, db, dba, drel):
    v = pl.BlockSpec(memory_space=pltpu.VMEM)
    shape = sds((PACK, db[0].shape[1]), F32)
    return pl.pallas_call(
        pack_kernel,
        in_specs=[SMEM] + [v] * 8,
        out_specs=[v, v],
        out_shape=[shape, shape],
        name="pack",
    )(t, v1, v2, *db, *dba, *drel)


def relative_z(z, ids):
    r = z ^ ids[2]
    return 2 * (r & 1) + (r >> 1)


def place_feed_kernel(ids, a, b, *rest):
    exp, red = rest[-2:]
    exp[...] = a[0, 0].astype(F32)
    red[...] = b[0, 0].astype(F32).T


def place_feed(ids, x, d, hidden, onto=()):
    other = 1 if onto else 0

    def spec(odd):
        return pl.BlockSpec(
            (1, 1, GW, GW), lambda j, ids: ((j >> 1) ^ ids[1], relative_z(2 * (j & 1) + odd, ids), 0, 0)
        )

    tile = lambda j, ids: (other ^ ids[0]) * 2 + (j >> 1)
    return pl.pallas_call(
        place_feed_kernel,
        grid_spec=pltpu.PrefetchScalarGridSpec(
            num_scalar_prefetch=1,
            grid=(4,),
            in_specs=[spec(0), spec(1)] + [ANY] * len(onto),
            out_specs=[
                pl.BlockSpec((GW, GW), lambda j, ids: (j & 1, tile(j, ids))),
                pl.BlockSpec((GW, GW), lambda j, ids: (tile(j, ids), j & 1)),
            ],
        ),
        out_shape=[sds((d, hidden), F32), sds((hidden, d), F32)],
        input_output_aliases={3: 0, 4: 1} if onto else {},
        name="place_feed",
    )(ids, x, x, *onto)


def place_attend_kernel(ids, *refs):
    att, out = refs[8:]
    for i in range(4):
        near, far = refs[i], refs[4 + i]
        x = jnp.where((i >> 1) == ids[0], near[0, 0], far[0, 0]).astype(F32)
        if i < 3:
            att[:, i * GW : (i + 1) * GW] = x
        else:
            out[...] = x


def place_attend(ids, near, far, d):
    r = near.shape[2]
    ins = [
        pl.BlockSpec(
            (1, 1, r, GW),
            lambda q, ids, i=i: (relative_z((q & 1) * 2 + (q >> 1), ids), (i & 1) ^ ids[1], 0, 0),
        )
        for i in range(4)
    ]
    return pl.pallas_call(
        place_attend_kernel,
        grid_spec=pltpu.PrefetchScalarGridSpec(
            num_scalar_prefetch=1,
            grid=(4,),
            in_specs=ins + ins,
            out_specs=[
                pl.BlockSpec((r, 3 * GW), lambda q, ids: (q, 0)),
                pl.BlockSpec((r, GW), lambda q, ids: (q & 1, q >> 1)),
            ],
        ),
        out_shape=[sds((d, 3 * GW), F32), sds((GW, d), F32)],
        name="place_attend",
    )(ids, near, near, near, near, far, far, far, far)


def guarded(body, axis):
    def run(meta, *refs):
        @pl.when(pl.program_id(axis) < meta[2])
        def _():
            body(meta, *refs)

    return run


def clamp(i, meta):
    return jnp.minimum(i, meta[2] - 1)


def whole_spec(shape):
    zeros = (0,) * len(shape)
    return pl.BlockSpec(shape, lambda *_: zeros, pipeline_mode=pl.Buffered(1))


def chunk_spec(shape):
    zeros = (0,) * (len(shape) - 1)
    return pl.BlockSpec(shape, lambda i, meta: (clamp(i, meta),) + zeros)


def sds(shape, dtype):
    return jax.ShapeDtypeStruct(shape, dtype)


def w_(a):
    return (a, whole_spec(a.shape))


def o_(shape, dtype):
    return (sds(shape, dtype), whole_spec(shape))


class Local:
    def __init__(self, rows):
        self.rows = rows
        self.windows = rows // SLOTS
        worst = (self.windows + 1) // 2
        self.per_chunk = min(5, max(worst, 1))
        self.chunks = -(-worst // self.per_chunk)
        self.ch = self.per_chunk * BLK
        self.all = self.ch * self.chunks
        pick, mask = kind_tables()
        self.mask = jnp.asarray(mask, BF)
        self.perm = jnp.asarray(group_perm(), BF)
        up, down_t = stride_tables()
        self.up, self.down_t = jnp.asarray(up, BF), jnp.asarray(down_t, BF)
        slot = np.where(pick.sum(2) > 0, pick.argmax(2), 0)
        corner = (slot[0] // SIDE < 3) & (slot[0] % SIDE < 3)
        self.slots = jnp.asarray(np.stack([slot[0], slot[1], corner])[:, :, None], jnp.int32)

    def row(self, k, dt):
        return (sds((self.all, k), dt), chunk_spec((self.ch, k)))

    def c(self, a):
        return (a, chunk_spec((self.ch,) + a.shape[1:]))

    def call(self, body, name, ins, outs, scratch=(), grid=None, axis=0, flops=0, size=0, limit=VMEM_LIMIT):
        f = pl.pallas_call(
            body if axis is None else guarded(body, axis),
            out_shape=[o for o, _ in outs],
            grid_spec=pltpu.PrefetchScalarGridSpec(
                num_scalar_prefetch=1,
                grid=(self.chunks,) if grid is None else grid,
                in_specs=[s for _, s in ins],
                out_specs=[s for _, s in outs],
                scratch_shapes=list(scratch),
            ),
            compiler_params=pltpu.CompilerParams(vmem_limit_bytes=limit),
            cost_estimate=pl.CostEstimate(flops=int(flops), bytes_accessed=int(size), transcendentals=0),
            name=name,
        )
        return f(self.meta, *[a for a, _ in ins])

    def bound(self, w, bias, table):
        ins = [w, bias.reshape(bias.shape[0], -1), table]
        return pl.pallas_call(
            bound_kernel,
            out_shape=sds((8, BLK), F32),
            compiler_params=pltpu.CompilerParams(vmem_limit_bytes=VMEM_LIMIT),
            name="bound",
        )(*ins)

    def plan(self, place, counts, bounds, vecs):
        v = pl.BlockSpec(memory_space=pltpu.VMEM)
        self.meta = pl.pallas_call(
            partial(plan_kernel, self.windows, counts.shape[0], self.per_chunk),
            out_shape=sds((PLAN_HEAD + 3 * self.windows,), jnp.int32),
            in_specs=[SMEM, SMEM, v, v],
            out_specs=SMEM,
            name="plan",
        )(place, counts, bounds, vecs)

    def gather(self, patches, cot, vecs):
        ch, d = self.ch, patches.shape[1]
        idx = (sds((self.chunks, 1, ch), jnp.int32), pl.BlockSpec((1, 1, ch), lambda i, meta: (clamp(i, meta), 0, 0)))
        return self.call(
            partial(gather_kernel, self.windows),
            "gather_rows",
            [w_(self.slots), w_(patches), w_(cot), w_(vecs)],
            [self.row(d, BF)] * 4 + [self.row(1, F32), idx],
            [pltpu.VMEM((BLK, 1), jnp.int32), pltpu.VMEM((ch, self.rows), BF)],
            flops=4 * ch * self.rows * d,
            size=8 * self.rows * d,
        )

    def attend(self, live, first, bias, rel, w, tail=None, before=()):
        ch, d = self.ch, first.shape[1]
        width = w[0].shape[1]
        groups = width // GW
        clip = lambda g: jnp.minimum(g, groups - 1)
        block = lambda a: (a, pl.BlockSpec((ch,) + a.shape[1:], lambda g, meta: (0, 0), pipeline_mode=pl.Buffered(1)))
        cols = lambda a, k: (a, pl.BlockSpec((a.shape[0], k), lambda g, meta: (0, clip(g))))
        full = lambda k, dt: (sds((self.all, k), dt), ANY)
        pshape = (self.per_chunk * self.chunks, groups, GROUP * BLK, BLK)
        ins = [block(live), block(first), w_(self.perm), w_(self.up), w_(self.mask), cols(bias, GW), w_(rel)]
        ins += [cols(a, GW) for a in w]
        outs = [full(width, BF), (sds(pshape, BF), ANY), full(groups * BLK, BF)]
        v, dma = pltpu.VMEM, pltpu.SemaphoreType.DMA
        scratch = [v((2, GROUP * BLK, BLK), BF), v((ch, GW), BF), v((self.per_chunk, GROUP * BLK, BLK), BF)]
        scratch += [v((self.chunks, ch, groups * BLK), BF), dma((4,)), dma((3,))]
        steps = groups
        again = [live, first]
        if tail is not None:
            steps += 1
            xc, vecs, wo = tail
            ins += [block(xc), w_(vecs)]
            ins += [block(m) for m, _ in before] + [w_(a) for _, a in before] + [w_(a) for a in wo]
            again += [xc] + [m for m, _ in before]
            outs += [full(d, F32), full(d, BF)]
            scratch += [v((ch, d), F32), v((ch, d), BF), v((ch, d), F32)]
        ins += [(a, ANY) for a in again]
        return self.call(
            partial(attend_kernel, len(w), groups, tail is not None, len(before)),
            "attend",
            ins,
            outs,
            scratch,
            grid=(steps,),
            axis=None,
            flops=0.16 * ch * d * width,
            size=0.4 * ch * d,
        )

    def feed(self, second, branch, we, wr, be, last=None):
        ch, d = self.ch, second.shape[1]
        hidden = be.shape[1]
        pieces = len(we)
        wide = 2 * GW
        tiles = hidden // wide
        any_ = lambda a: (a, ANY)
        full = lambda dt: (sds((self.all, d), dt), ANY)
        ins = [any_(a) for a in (second, branch, *we, *wr)] + [w_(be)]
        outs = [(sds((2, 2 * d, GW), BF), ANY)] * tiles + [o_((1, hidden), F32), full(BF)]
        v = pltpu.VMEM
        scratch = [v((ch, d), BF)] * 2 + [v((tiles, d, wide), BF), v((tiles, wide, d), BF)]
        scratch += [v((tiles, 2, 2 * d, GW), BF), v((ch, d), F32), v((ch, d), F32), v((2, ch, d), BF)]
        dma = pltpu.SemaphoreType.DMA
        scratch += [dma((6,)), dma((2 * tiles,)), dma((tiles,))]
        prior = 0
        if last is None:
            outs += [full(BF)]
        else:
            live, middle, cotc, vecs, sums = last
            prior = len(sums)
            ins += [any_(live), any_(middle), any_(cotc), w_(vecs)] + [any_(a) for a in sums]
            outs += [full(F32), full(BF), o_((8, d), F32)]
            scratch += [v((ch, d), F32), v((ch, d), BF), v((ch, 1), F32), v((ch, d), BF)]
        return self.call(
            partial(feed_kernel, tiles, pieces, last is not None, prior),
            "feed",
            ins,
            outs,
            scratch,
            grid=(1,),
            axis=None,
            flops=12 * ch * d * hidden,
            size=8 * d * hidden,
        )

    def back(self, ag, qkv, probs, mixed, first, wo):
        ch, d = self.ch, first.shape[1]
        width = qkv.shape[1]
        groups = width // GW
        split = groups == 3
        clip = lambda g: jnp.minimum(g, groups - 1)
        block = lambda a: (a, pl.BlockSpec((ch,) + a.shape[1:], lambda g, meta: (0, 0), pipeline_mode=pl.Buffered(1)))
        cols = pl.BlockSpec((ch, GW), lambda g, meta: (0, clip(g)))
        pspec = pl.BlockSpec((self.per_chunk, 1) + probs.shape[2:], lambda g, meta: (0, clip(g), 0, 0))
        one = (1, 2 * groups * BLK, GW)
        if split:

            def tile(start):
                return lambda g, meta: (
                    (jnp.clip(g - start(meta[AT_ME] >> 1), 0, 1) ^ meta[AT_ME]) & 1,
                    0,
                    0,
                )

            shape = sds((2,) + one[1:], BF)
            grads = [(shape, pl.BlockSpec(one, tile(lambda h: 2 * h))), (shape, pl.BlockSpec(one, tile(lambda h: 2 - 2 * h)))]
        else:
            grads = [(sds((groups + 1,) + one[1:], BF), pl.BlockSpec(one, lambda g, meta: (g, 0, 0)))]
        v, dma = pltpu.VMEM, pltpu.SemaphoreType.DMA
        return self.call(
            partial(back_kernel, len(wo), groups, split),
            "back",
            [block(ag), w_(self.perm), w_(self.up), w_(self.down_t), (qkv, cols), (probs, pspec)]
            + [block(mixed), block(first)]
            + [(a, pl.BlockSpec((BLK, a.shape[1]), lambda g, meta: (clip(g), 0))) for a in wo]
            + [(a, ANY) for a in (ag, qkv, probs, mixed, first)],
            [(sds((self.all, width), BF), ANY), *grads]
            + [(sds((1, width), F32), pl.BlockSpec((1, GW), lambda g, meta: (0, clip(g))))]
            + [o_((groups * GROUP, 2 * BLK), F32)],
            [v((ch, GW), BF), v((ch, BLK), BF), v((2, GROUP * BLK, BLK), F32), v((ch, GW), BF), dma((5,)), dma((1,))],
            grid=(groups + 1,),
            axis=None,
            flops=14 * ch * d * width,
            size=30 * ch * d,
        )

    def ends(self, live, xc, cotc, mg, vecs, dqkv, ws):
        ch, d = self.ch, xc.shape[1]
        c = self.c
        return self.call(
            partial(ends_kernel, [len(a) for a in ws]),
            "ends",
            [c(live), c(xc), c(cotc), c(mg), w_(vecs)] + [c(a) for a in dqkv] + [w_(a) for s in ws for a in s],
            [self.row(d, BF)] * 2 + [o_((8, d), F32)],
            [pltpu.VMEM((ch, d), F32)],
            flops=6 * ch * d * d,
            size=30 * ch * d,
        )

    def by_row(self, idx):
        return (idx, pl.BlockSpec((1, 1, self.ch), lambda i, meta: (clamp(i, meta), 0, 0)))

    def result(self, idx, live, middle, vecs, patches, red):
        ch, d = self.ch, patches.shape[1]
        c = self.c
        (out,) = self.call(
            partial(result_kernel, len(red)),
            "result",
            [self.by_row(idx), c(live), c(middle), w_(vecs), w_(patches)] + [c(a) for a in red],
            [o_(patches.shape, BF)],
            [pltpu.VMEM((ch, d), BF)],
            flops=2 * ch * self.rows * d,
            size=12 * self.rows * d,
        )
        return out

    def scatter(self, idx, hi, lo, cot):
        ch, d = self.ch, cot.shape[1]
        (out,) = self.call(
            scatter_kernel,
            "scatter",
            [self.by_row(idx), self.c(hi), self.c(lo), w_(cot)],
            [o_(cot.shape, F32)],
            flops=4 * ch * self.rows * d,
            size=12 * self.rows * d,
        )
        return out


CODES = 169


def pad_table(table):
    return jnp.pad(table.astype(F32), ((0, 0), (4, 2 * BLK - CODES - 4)))


def bias_row(bias):
    b = bias.astype(F32)
    return jnp.stack([b[:, 0], jnp.zeros_like(b[:, 0]), b[:, 1]], axis=1).reshape(1, -1)


def pick_half(a, bit, axis=0):
    n = a.shape[axis] // 2
    return lax.dynamic_slice_in_dim(a, bit * n, n, axis)


def swap(a, axis, n, step=1):
    return lax.ppermute(a, axis, [(i, i ^ step) for i in range(n)])


def plus(*xs):
    total = xs[0].astype(F32)
    for x in xs[1:]:
        total = total + x.astype(F32)
    return total.astype(BF)


def after(x, *deps):
    return lax.optimization_barrier((x, *deps))[0]


def on_device(
    nz,
    nt,
    patches,
    gain_first,
    shift_first,
    attend_weight,
    attend_bias,
    offset_table,
    output_weight,
    output_bias,
    gain_second,
    shift_second,
    expand_weight,
    expand_bias,
    reduce_weight,
    reduce_bias,
    crop_counts,
    cotangent,
):
    fast = nt == 2 and nz == 4
    t, c, y, z = (lax.axis_index(a) for a in ("tensor", "core", "y", "z"))
    rows, d = patches.shape
    local = Local(rows)
    vec = lambda a: a.astype(F32).reshape(1, -1)
    vecs = jnp.stack([gain_first, shift_first, gain_second, shift_second, output_bias, reduce_bias]).astype(F32)
    bound = local.bound(attend_weight, attend_bias, offset_table)
    if fast:
        got, w_att_in, w_out_in = lax.optimization_barrier(
            (swap(bound, "tensor", nt), attend_weight, output_weight)
        )
        bound = jnp.maximum(bound, got)
        x_att = swap(pick_half(pick_half(w_att_in, c), y), "tensor", nt)
        x_out = swap(pick_half(w_out_in, c, 1), "tensor", nt)
        small = lambda a: [a, swap(a, "tensor", nt)]
        me = c * 2 + y
    else:
        w_att = [[lax.all_gather(attend_weight, "tensor", axis=1, tiled=True)]]
        w_out = [[lax.all_gather(output_weight, "tensor", axis=0, tiled=True)]]
        w_exp = [[lax.all_gather(expand_weight, "tensor", axis=1, tiled=True)]]
        w_red = [[lax.all_gather(reduce_weight, "tensor", axis=0, tiled=True)]]
        bound = lax.pmax(bound, "tensor")
        small = lambda a: [lax.all_gather(a, "tensor", axis=0, tiled=True)]
        me = c = 0 * c
    place = jnp.stack([t * local.windows, c, me]).astype(jnp.int32)
    local.plan(place, crop_counts, bound, vecs)
    bias, rel, b_exp = small(attend_bias), small(pad_table(offset_table)), small(expand_bias)
    xc, cotc, branch, first, live, idx = local.gather(patches, cotangent, vecs)

    if fast:
        xc, first, x_att, x_out, bias, rel, b_exp = lax.optimization_barrier(
            (xc, first, x_att, x_out, bias, rel, b_exp)
        )
    bias, b_exp = [bias_row(b) for b in bias], [vec(a) for a in b_exp]
    if fast:
        s_exp = after(pick_half(pick_half(expand_weight, c, 1), y, 1), x_att)
        first, s_exp = lax.optimization_barrier((first, s_exp))
        x_exp = swap(s_exp, "tensor", nt)
        y_att = swap(x_att, "y", 2)
        w_out = [[output_weight], [x_out, swap(x_out, "core", 2)]]
        qkv0, probs0, mixed0 = local.attend(live, first, bias[0], rel[0], [attend_weight])
        y_att, x_exp, mixed0 = lax.optimization_barrier((y_att, x_exp, mixed0))
        x_att = jnp.where(y == 0, jnp.concatenate([x_att, y_att], 0), jnp.concatenate([y_att, x_att], 0))
        w_att = [[attend_weight], [x_att, swap(x_att, "core", 2)]]
        y_exp = swap(x_exp, "y", 2)
        first, s_red = lax.optimization_barrier((first, after(pick_half(reduce_weight, c, 0), w_att[1][0])))
        x_red = swap(s_red, "tensor", nt)
        held = [(qkv0, probs0, mixed0)]
        before = [(mixed0, output_weight)]
    else:
        held, before = [], []
    qkv1, probs1, mixed1, middle, second = local.attend(
        live, first, bias[-1], rel[-1], w_att[-1], (xc, vecs, w_out[-1]), before
    )
    held.append((qkv1, probs1, mixed1))
    n = len(w_att)

    def bias_grad(a):
        a = a.reshape(-1, 3, HEAD_DIM)
        return jnp.stack([a[:, 0], a[:, 2]], axis=1)

    if fast:
        y_exp, x_red, second = lax.optimization_barrier((y_exp, x_red, second))
        x_exp = jnp.where(y == 0, jnp.concatenate([x_exp, y_exp], 1), jnp.concatenate([y_exp, x_exp], 1))
        second, x_exp = lax.optimization_barrier((second, x_exp))
        k0, s0, db0, red0, sg0 = local.feed(second, branch, [expand_weight], [reduce_weight], b_exp[0])
        e1 = [x_exp, swap(x_exp, "core", 2)]
        r1 = [x_red, swap(x_red, "core", 2)]
        k1, s1, db1, red1, mg, ag, v2 = local.feed(second, branch, e1, r1, b_exp[1], (live, middle, cotc, vecs, [sg0]))
        def split(keep, got):
            h = keep.shape[1] // 2
            return [plus(keep[:, i * h : (i + 1) * h], got[:, i * h : (i + 1) * h]) for i in range(2)]

        def first_leg(own, peer):
            return swap(peer[0], "tensor", nt), swap(jnp.stack([own[1][1], peer[1][1]]), "y", 2)

        def second_leg(own, peer, gx, gy):
            low = plus(own[0][1], gx[1])
            up = plus(own[0][0], gx[0])
            peer_b = plus(peer[1][0], gy[1])
            own_b = plus(own[1][0], gy[0])
            return up, swap(low, "y", 2), own_b, swap(peer_b, "tensor", nt)

        def z_first(up, gy, own_b, gx):
            a, b = plus(up, gy), plus(own_b, gx)
            return jnp.where(z % 2 == 0, a, b), jnp.where(z % 2 == 0, b, a)

        def z_second(keep, got):
            hi = z // 2
            total = lambda i: plus(pick_half(keep, i), pick_half(got, i))
            return total(hi), total(1 - hi)

        ff_peer = split(k1, swap(s1, "core", 2))
        ff_own = split(k0, swap(s0, "core", 2))
        ag, *ff = lax.optimization_barrier((ag, *ff_own, *ff_peer))
        ff_own, ff_peer = ff[:2], ff[2:]
        fx, fy = first_leg(ff_own, ff_peer)
        dq1, gk1, gs1, dba1, drel1 = local.back(ag, *held[1], first, w_out[1])
        dq1, gs1, red0 = lax.optimization_barrier((dq1, gs1, red0))
        got1 = swap(gs1, "core", 2)
        result = local.result(idx, live, middle, vecs, patches, [red0, red1])
        fx, fy, dq1, result, ag = lax.optimization_barrier((fx, fy, dq1, result, ag))
        ff_up, fy, ff_b, fx = second_leg(ff_own, ff_peer, fx, fy)
        dq0, gk0, gs0, dba0, drel0 = local.back(ag, *held[0], first, w_out[0])
        got1, fx, fy, dq0, gs0 = lax.optimization_barrier((got1, fx, fy, dq0, gs0))
        at_peer = split(gk1, got1)
        at_own = split(gk0, swap(gs0, "core", 2))
        ax, ay = first_leg(at_own, at_peer)
        ff_keep, ff_send = z_first(ff_up, fy, ff_b, fx)
        ff_got = swap(ff_send, "z", nz, 1)
        mg, *at4, ff_keep, ff_send = lax.optimization_barrier((mg, *at_own, *at_peer, ff_keep, ff_send))
        hi, lo, v1 = local.ends(live, xc, cotc, mg, vecs, [dq0, dq1], w_att)
        ff_got, hi = lax.optimization_barrier((ff_got, hi))
        ff_keep, ff_send = z_second(ff_keep, ff_got)
        ff_got = swap(ff_send, "z", nz, 2)
        ax, ay, hi, ff_send = lax.optimization_barrier((ax, ay, hi, ff_send))
        up, ay, own_b, ax = second_leg(at_own, at_peer, ax, ay)
        v1, up, own_b, ff_keep, ff_send = lax.optimization_barrier((v1, up, own_b, ff_keep, ff_send))
        mine, other = pack(t.reshape(1).astype(jnp.int32), v1, v2, (db0, db1), (dba0, dba1), (drel0, drel1))
        ids = jnp.stack([c, y, z]).astype(jnp.int32)
        barrier = lambda *xs: lax.optimization_barrier(xs)
        ax, ay, mine, other = barrier(ax, ay, mine, other)
        keep, send = z_first(up, ay, own_b, ax)
        got = swap(send, "z", nz, 1)
        tiny_got = swap(other.astype(BF), "tensor", nt)
        ff_got, keep, send = barrier(ff_got, keep, send)
        ff = plus(ff_keep, ff_got)
        ff2 = swap(ff, "z", nz, 2)
        got, tiny_got, ff = barrier(got, tiny_got, ff)
        keep, send = z_second(keep, got)
        got = swap(send, "z", nz, 2)
        tiny = plus(mine, tiny_got)
        tiny_got = swap(tiny, "core", 2)
        ff2, send, tiny, tiny_got = barrier(ff2, send, tiny, tiny_got)
        ff = jnp.stack([ff, ff2])
        ff1 = swap(ff, "z", nz, 1)
        tiny = plus(tiny, tiny_got)
        tiny_got = swap(tiny, "y", 2)
        got, ff, tiny = barrier(got, ff, tiny)
        att = plus(keep, got)
        att_y = swap(att, "y", 2)
        att, att_y, tiny_got = barrier(att, att_y, tiny_got)
        att = jnp.stack([att, att_y])
        tiny = plus(tiny, tiny_got)
        ff1, att, tiny = barrier(ff1, att, tiny)
        tiny_got = swap(tiny, "z", nz, 1)
        ff = jnp.concatenate([ff, ff1], 0)
        ffy = swap(ff, "y", 2)
        att2 = swap(att, "z", nz, 2)
        ff, att, hi, tiny = barrier(ff, att, hi, tiny)
        input_grad = local.scatter(idx, hi, lo, cotangent)
        tiny_got, input_grad, att = barrier(tiny_got, input_grad, att)
        tiny = plus(tiny, tiny_got)
        tiny_got = swap(tiny, "z", nz, 2)
        att2, att, tiny = barrier(att2, att, tiny)
        att = jnp.stack([att, att2])
        att1 = swap(att, "z", nz, 1)
        tiny = plus(tiny, tiny_got).astype(F32)
        gb_exp, gb_att = tiny[0], bias_grad(tiny[1, : 3 * GW])
        smalls = [tiny[2 + i, : d // 2] for i in range(6)]
        g_rel = tiny[8 : 8 + drel0.shape[0], :CODES]
        att1, ffy, ff, att, gb_exp, gb_att, g_rel, *smalls = barrier(att1, ffy, ff, att, gb_exp, gb_att, g_rel, *smalls)
        ff = jnp.stack([ff, ffy])
        far = swap(ff, "core", 2)
        att = jnp.concatenate([att, att1], 0)
        att_far = swap(att, "core", 2)
        ff, att = barrier(ff, att)
        g_ff = place_feed(ids, ff, d, 4 * GW)
        far, g_ff = barrier(far, g_ff)
        g_exp, g_red = place_feed(ids, far, d, 4 * GW, g_ff)
        g_att, g_out = place_attend(ids, att, att_far, d)
        vectors = smalls
    else:
        *tiles, gb_exp, red, mg, ag, v2 = local.feed(second, branch, w_exp[0], w_red[0], b_exp[0], (live, middle, cotc, vecs, []))
        dq, ga, dba, drel = local.back(ag, *held[0], first, w_out[0])
        hi, lo, v1 = local.ends(live, xc, cotc, mg, vecs, [dq], w_att)
        result = local.result(idx, live, middle, vecs, patches, [red])
        input_grad = local.scatter(idx, hi, lo, cotangent)
        ff = jnp.concatenate(tiles, 0)
        g_exp = ff[:, 0:d].transpose(1, 0, 2).reshape(d, -1)
        g_red = ff[:, d:].transpose(0, 2, 1).reshape(-1, d)
        g_att = ga[0 : dq.shape[1] // GW, 0:d].transpose(1, 0, 2).reshape(d, -1)
        g_out = ga[dq.shape[1] // GW].reshape(2, d, d // 2).transpose(1, 0, 2).reshape(d, d)
        dp = ("z", "y", "core")

        def total(a, axis):
            a = lax.psum_scatter(a.astype(BF), "tensor", scatter_dimension=axis, tiled=True)
            return lax.psum(a, dp).astype(F32)

        vectors = total(jnp.stack([v1[0], v1[1], v2[2], v2[0], v2[1], v1[2]]), 1)
        gb_att, g_rel, gb_exp = total(bias_grad(dba), 0), total(drel[:, :CODES], 0), total(gb_exp[0], 0)
        g_exp, g_att, g_out, g_red = total(g_exp, 1), total(g_att, 1), total(g_out, 0), total(g_red, 0)

    return (
        result,
        input_grad,
        vectors[0],
        vectors[1],
        g_att,
        gb_att,
        g_rel,
        g_out,
        vectors[2],
        vectors[3],
        vectors[4],
        g_exp,
        gb_exp,
        g_red,
        vectors[5],
    )


def solution(mesh):
    nt = mesh.shape["tensor"]
    nz = mesh.shape["dp"] // 4
    grid = Mesh(mesh.devices.reshape(nz, 2, 2, nt), ("z", "y", "core", "tensor"))
    dp = ("z", "y", "core")
    rows = P(dp + ("tensor",), None)
    in_specs = (
        rows,
        P(),
        P(),
        P(None, "tensor"),
        P("tensor", None, None),
        P("tensor", None),
        P("tensor", None),
        P(),
        P(),
        P(),
        P(None, "tensor"),
        P("tensor"),
        P("tensor", None),
        P(),
        P(dp),
        rows,
    )
    out_specs = (
        rows,
        rows,
        P("tensor"),
        P("tensor"),
        P(None, "tensor"),
        P("tensor", None, None),
        P("tensor", None),
        P("tensor", None),
        P("tensor"),
        P("tensor"),
        P("tensor"),
        P(None, "tensor"),
        P("tensor"),
        P("tensor", None),
        P("tensor"),
    )
    return jax.shard_map(partial(on_device, nz, nt), mesh=grid, in_specs=in_specs, out_specs=out_specs, check_vma=False)
```

```python
from functools import partial

import jax
import jax.numpy as jnp
import numpy as np
from jax import lax
from jax.experimental import pallas as pl
from jax.experimental.pallas import tpu as pltpu
from jax.sharding import Mesh
from jax.sharding import PartitionSpec as P

HEAD_DIM = 32
EPSILON = 1e-05
MASKED = 30000.0
SIDE = 7
SLOTS = SIDE * SIDE
BLK = 128
GROUP = 4
GW = 3 * GROUP * HEAD_DIM
BF = jnp.bfloat16
F32 = jnp.float32
VMEM_LIMIT = 60 * 1024 * 1024


def dot(a, b):
    return jnp.dot(a, b, preferred_element_type=F32)


def dot_nt(a, b):
    return lax.dot_general(a, b, (((1,), (1,)), ((), ())), preferred_element_type=F32)


def dot_tn(a, b):
    return lax.dot_general(a, b, (((0,), (0,)), ((), ())), preferred_element_type=F32)


def kind_tables():
    slot = -np.ones((2, BLK), np.int64)
    owner = 100 + np.arange(BLK)[None].repeat(2, 0)
    nine = np.arange(9)
    nine = (nine // 3) * SIDE + nine % 3
    for w in range(2):
        slot[0, w * SLOTS : (w + 1) * SLOTS] = np.arange(SLOTS)
        owner[0, w * SLOTS : (w + 1) * SLOTS] = w
    for w in range(3):
        at = 2 * SLOTS + 9 * w
        slot[0, at : at + 9] = nine
        owner[0, at : at + 9] = 2 + w
    for w in range(14):
        slot[1, 9 * w : 9 * w + 9] = nine
        owner[1, 9 * w : 9 * w + 9] = w
    pick = (slot[:, :, None] == np.arange(64)[None, None, :]).astype(np.float32)
    same = owner[:, :, None] == owner[:, None, :]
    mask = np.where(same, 0.0, -1e30).astype(np.float32)
    return pick, mask


def stride_tables():
    slot, _ = kind_tables()
    s = np.where(slot.sum(2) > 0, slot.argmax(2), -1)
    place = np.where(s >= 0, 13 * (s // SIDE) + s % SIDE, -1)
    up = (place[:, :, None] == np.arange(BLK)).astype(np.float32)
    down = ((84 - place)[:, :, None] == np.arange(BLK)) & (place >= 0)[:, :, None]
    return up, down.astype(np.float32).transpose(0, 2, 1)


def group_perm():
    perm = np.zeros((GW, GW), np.float32)
    for h in range(GROUP):
        for p in range(3):
            for e in range(HEAD_DIM):
                perm[(h * 3 + p) * HEAD_DIM + e, (p * GROUP + h) * HEAD_DIM + e] = 1.0
    return perm


PLAN_HEAD = 8
G1, B1, G2, B2, OB, RB = (slice(i, i + 1) for i in range(6))
AT_C, AT_ME = 6, 7


def bound_kernel(w, bias, table, out):
    width = w.shape[1]
    q = jnp.zeros((1, BLK), F32)
    k = jnp.zeros((1, BLK), F32)
    for start in range(0, width, BLK):
        size = min(BLK, width - start)
        x = w[:, start : start + size]
        gram = dot_tn(x, x)
        a = lax.broadcasted_iota(jnp.int32, (size, size), 0) >> 5
        b = lax.broadcasted_iota(jnp.int32, (size, size), 1) >> 5
        sums = jnp.sum(jnp.where(a == b, gram * gram, 0.0), axis=0, keepdims=True)
        lane = lax.broadcasted_iota(jnp.int32, (1, size), 1) >> 5
        for i in range(size // HEAD_DIM):
            part = (start // HEAD_DIM + i) % 3
            top = jnp.max(jnp.where(lane == i, sums, 0.0), axis=1, keepdims=True)
            if part == 0:
                q = jnp.maximum(q, top)
            if part == 1:
                k = jnp.maximum(k, top)
    qb = bias[...].astype(F32)
    col = lax.broadcasted_iota(jnp.int32, qb.shape, 1)
    qb = jnp.sum(jnp.where(col < HEAD_DIM, qb * qb, 0.0), axis=1, keepdims=True)
    qb = jnp.max(qb, axis=0, keepdims=True)
    top = jnp.max(jnp.max(jnp.abs(table[...].astype(F32)), axis=1, keepdims=True), axis=0, keepdims=True)
    out[...] = jnp.zeros_like(out)
    for i, v in enumerate((q, k, qb, top)):
        out[i : i + 1, :] = jnp.broadcast_to(v, (1, BLK))


def plan_kernel(windows, images, per_chunk, where, counts, bounds, vecs, out):
    d = vecs.shape[1]
    g1, b1 = vecs.at[G1], vecs.at[B1]
    big = bounds[...]

    def root4(v):
        return jnp.sqrt(jnp.sqrt(HEAD_DIM * v))

    reach = jnp.sqrt(float(d)) * jnp.max(jnp.abs(g1[...]), axis=1, keepdims=True)
    reach = 1.02 * (reach + jnp.sqrt(jnp.sum(b1[...] * b1[...], axis=1, keepdims=True)))
    q = 1.01 * (reach * root4(big[0:1, :]) + jnp.sqrt(big[2:3, :])) * HEAD_DIM**-0.5
    top = 1.01 * q * (reach * root4(big[1:2, :])) + big[3:4, :]
    safe = jnp.where(2.0 * top < MASKED - 500.0, 1, 0)
    bad = 1 - jnp.min(safe)
    first = where[0]
    nf = jnp.int32(0)
    nq = jnp.int32(0)
    for i in range(2 * windows + PLAN_HEAD, out.shape[0]):
        out[i] = 0
    for w in range(windows):
        place = first + w
        start = jnp.int32(0)
        offset = jnp.int32(-1)
        for i in range(images):
            total = counts[i] + 2
            inside = (place >= start) & (place < start + total)
            offset = jnp.where(inside, place - start, offset)
            start = start + total
        present = offset >= 0
        whole = present & (offset < 2)
        full = present & (whole | (bad > 0))
        part = present & (~whole) & (bad == 0)
        out[PLAN_HEAD + 2 * windows + w] = whole.astype(jnp.int32)

        @pl.when(full)
        def _():
            out[PLAN_HEAD + nf] = w

        @pl.when(part)
        def _():
            out[PLAN_HEAD + windows + nq] = w

        nf = nf + full.astype(jnp.int32)
        nq = nq + part.astype(jnp.int32)
    n0 = (nf + 1) >> 1
    left = jnp.maximum(nq - 3 * n0, 0)
    n1 = jnp.int32(0)
    for i in range(-(-windows // 14)):
        n1 = n1 + (left > 14 * i).astype(jnp.int32)
    nb = n0 + n1
    chunks = jnp.int32(1)
    for i in range(1, windows):
        chunks = chunks + (nb > per_chunk * i).astype(jnp.int32)
    for i, v in enumerate((nb, n0, chunks, bad, nf, nq, where[1], where[2])):
        out[i] = v


def norm_stats(x):
    mean = jnp.mean(x, axis=1, keepdims=True)
    c = x - mean
    scale = lax.rsqrt(jnp.mean(c * c, axis=1, keepdims=True) + EPSILON)
    return c * scale, scale


def norm_back(grad, normal, scale, gain):
    inner = grad * gain
    mean = jnp.mean(inner, axis=1, keepdims=True)
    proj = jnp.mean(inner * normal, axis=1, keepdims=True)
    return scale * (inner - mean - normal * proj)


def gather_kernel(windows, meta, slots, patches, cot, vecs, xc, cotc, branch, first, live, idx_row, idx, pick):
    rows = xc.shape[0]
    total = patches.shape[0]
    blocks = rows // BLK
    spots = lax.broadcasted_iota(jnp.int32, (BLK, total), 1)
    chunk = pl.program_id(0)
    n0 = meta[1]
    r = lax.broadcasted_iota(jnp.int32, (BLK, 1), 0)

    def listed(first_at, count, i):
        ok = (i >= 0) & (i < count)
        w = meta[first_at + jnp.where(ok, i, 0)]
        return jnp.where(ok, w, -1)

    def spread(ends, wins):
        base = jnp.full((BLK, 1), -1, jnp.int32)
        for end, w in reversed(list(zip(ends, wins))):
            base = jnp.where(r < end, w, base)
        return base

    def one(b, carry):
        at = pl.ds(pl.multiple_of(b * BLK, BLK), BLK)
        block = chunk * blocks + b
        kind0 = block < n0

        @pl.when(kind0)
        def _():
            wins = [listed(PLAN_HEAD, meta[4], 2 * block + i) for i in range(2)]
            wins += [listed(PLAN_HEAD + windows, meta[5], 3 * block + i) for i in range(3)]
            ends = [SLOTS, 2 * SLOTS] + [2 * SLOTS + 9 * (i + 1) for i in range(3)]
            base = spread(ends, wins)
            slot = slots[0]
            where_whole = [
                jnp.where(w >= 0, meta[PLAN_HEAD + 2 * windows + jnp.maximum(w, 0)], 0) for w in wins[:2]
            ] + [jnp.int32(1)] * 3
            sure = spread(ends, where_whole) > 0
            ok = base >= 0
            idx[...] = jnp.where(ok, base * SLOTS + slot, -1)
            live[at, :] = jnp.where(ok & (sure | (slots[2] > 0)), 1.0, 0.0)

        @pl.when(jnp.logical_not(kind0))
        def _():
            start = 3 * n0 + 14 * (block - n0)
            wins = [listed(PLAN_HEAD + windows, meta[5], start + i) for i in range(14)]
            base = spread([9 * (i + 1) for i in range(14)], wins)
            ok = base >= 0
            idx[...] = jnp.where(ok, base * SLOTS + slots[1], -1)
            live[at, :] = jnp.where(ok, 1.0, 0.0)

        here = idx[...]
        wide = jnp.broadcast_to(here.astype(F32), (BLK, BLK))
        idx_row[0, :, at] = wide.T[0:1, :].astype(jnp.int32)
        pick[at, :] = (spots == here).astype(F32).astype(BF)
        return carry

    lax.fori_loop(0, blocks, one, 0)
    x = dot(pick[...], patches[...])
    xc[...] = x.astype(BF)
    up = dot(pick[...], cot[...])
    cotc[...] = up.astype(BF)
    branch[...] = (up * live[...]).astype(BF)
    for b in range(blocks):
        at = slice(b * BLK, (b + 1) * BLK)
        n, _ = norm_stats(xc[at, :].astype(F32))
        first[at, :] = (n * vecs[G1] + vecs[B1]).astype(BF)


def lane_head(shape, axis):
    return lax.broadcasted_iota(jnp.int32, shape, axis) >> 5


def spread_rows(x):
    h = lane_head(x.shape, 1)
    zero = jnp.zeros_like(x)
    return jnp.concatenate([jnp.where(h == i, x, zero) for i in range(GROUP)], axis=0)


def spread_cols(xt):
    h = lane_head(xt.shape, 0)
    zero = jnp.zeros_like(xt)
    return jnp.concatenate([jnp.where(h == i, xt, zero) for i in range(GROUP)], axis=1)


def fold_rows(x):
    h = lane_head((BLK, BLK), 1)
    out = x[0:BLK]
    for i in range(1, GROUP):
        out = jnp.where(h == i, x[i * BLK : (i + 1) * BLK], out)
    return out


def run_copies(pairs, sem):
    copies = [pltpu.make_async_copy(x, y, sem.at[i]) for i, (x, y) in enumerate(pairs)]
    for x in copies:
        x.start()
    for x in copies:
        x.wait()


def attend_kernel(pieces, groups, tail, prior, meta, live, first, perm, pick, mask, bias, rel, *rest):
    w, rest = rest[:pieces], rest[pieces:]
    if tail:
        (xc, vecs), rest = rest[:2], rest[2:]
        before, rest = rest[:prior], rest[prior:]
        w_before, rest = rest[:prior], rest[prior:]
        w_out, rest = rest[:pieces], rest[pieces:]
    k = 3 + prior if tail else 2
    sources, rest = rest[:k], rest[k:]
    loaded = (live, first) + ((xc, *before) if tail else ())
    if tail:
        qkv_out, probs_out, mixed_out, middle_out, second_out, table, qkv, probs, mixed, in_sem, sem = rest[:11]
        middle, second, att = rest[11:]
    else:
        qkv_out, probs_out, mixed_out, table, qkv, probs, mixed, in_sem, sem = rest
    rows, d = first.shape
    blocks = rows // BLK
    step = pl.program_id(0)
    chunks = meta[2]
    c = meta[AT_C]
    n0 = meta[1]
    near = pl.ds(pl.multiple_of(c * (d // 2), BLK), d // 2)
    far = pl.ds(pl.multiple_of((1 - c) * (d // 2), BLK), d // 2)
    last = groups if tail else groups - 1

    def reload(chunk):
        @pl.when(chunks > 1)
        def _():
            at = pl.ds(pl.multiple_of(chunk * rows, rows), rows)
            run_copies([(x.at[at, :], y) for x, y in zip(sources, loaded)], in_sem)

    def stores(chunk, g):
        at = pl.ds(pl.multiple_of(chunk * rows, rows), rows)
        cols = pl.ds(pl.multiple_of(g * GW, BLK), GW)
        return (
            pltpu.make_async_copy(qkv, qkv_out.at[at, cols], sem.at[0]),
            pltpu.make_async_copy(probs, probs_out.at[pl.ds(chunk * blocks, blocks), g], sem.at[1]),
        )

    def group(i, carry):
        chunk = chunks - 1 - i
        reload(chunk)
        if pieces == 1:
            v = dot(first[...], w[0][...])
        else:
            v = dot(first[:, near], w[0][...]) + dot(first[:, far], w[1][...])
        v = v + bias[...]
        block = lax.broadcasted_iota(jnp.int32, (1, GW), 1) >> 5
        is_q = block == 0
        for j in range(3, 3 * GROUP, 3):
            is_q = is_q | (block == j)
        v = (v * jnp.where(is_q, HEAD_DIM**-0.5, 1.0)).astype(BF)

        @pl.when((step > 0) | (i > 0))
        def _():
            for x in stores(0, 0):
                x.wait()

        qkv[...] = dot(v, perm[...]).astype(BF)
        stores(chunk, step)[0].start()
        for b in range(blocks):
            at = slice(b * BLK, (b + 1) * BLK)
            kind = jnp.where(chunk * blocks + b < n0, 0, 1)
            q = qkv[at, 0:BLK]
            k = qkv[at, BLK : 2 * BLK]
            v = qkv[at, 2 * BLK : 3 * BLK]
            st = dot_nt(spread_rows(k), q) + table[kind].astype(F32)
            dead = (live[at, :] - 1.0) * MASKED
            st = st.reshape(GROUP, BLK, BLK) + jnp.where(meta[3] > 0, dead, 0.0)[None]
            peak = jnp.max(st, axis=1, keepdims=True)
            e = jnp.exp(st - peak)
            p = (e * (1.0 / jnp.sum(e, axis=1, keepdims=True))).astype(BF)
            p = p.reshape(GROUP * BLK, BLK)
            probs[b] = p
            vt = v.astype(F32).T.astype(BF)
            m = dot(spread_cols(vt), p).T.astype(BF)
            mixed[chunk, at, pl.ds(pl.multiple_of(step * BLK, BLK), BLK)] = m
        stores(chunk, step)[1].start()
        return carry

    @pl.when(step < groups)
    def _():
        places = []
        for h in range(GROUP):
            row = rel[pl.ds(step * GROUP + h, 1), :]
            row = pltpu.roll(jnp.broadcast_to(row, (BLK, 2 * BLK)), 2 * BLK - 88, 1, stride=1, stride_axis=0)
            places.append(row[:, 0:BLK].astype(BF))
        for kind in range(2):
            e = pick[kind]
            for h in range(GROUP):
                half = dot(e, places[h]).astype(BF)
                t = dot_nt(half, e) + mask[kind].astype(F32)
                table[kind, h * BLK : (h + 1) * BLK, :] = t.astype(BF)
        lax.fori_loop(0, chunks, group, 0)

    def project(i, carry):
        chunk = chunks - 1 - i
        reload(chunk)
        if pieces == 1:
            att[...] = dot(mixed[chunk], w_out[0][...])
        else:
            att[:, near] = dot(mixed[chunk], w_out[0][...])
            att[:, far] = dot(mixed[chunk], w_out[1][...])
        for m, v in zip(before, w_before):
            att[...] = att[...] + dot(m[...], v[...])
        for b in range(blocks):
            at = slice(b * BLK, (b + 1) * BLK)
            m = xc[at, :].astype(F32) + live[at, :] * (att[at, :] + vecs[OB])
            middle[at, :] = m
            nrm, _ = norm_stats(m)
            second[at, :] = (nrm * vecs[G2] + vecs[B2]).astype(BF)
        at = pl.ds(pl.multiple_of(chunk * rows, rows), rows)
        run_copies([(middle, middle_out.at[at, :]), (second, second_out.at[at, :])], in_sem)
        return carry

    def give(chunk):
        at = pl.ds(pl.multiple_of(chunk * rows, rows), rows)
        return pltpu.make_async_copy(mixed.at[chunk], mixed_out.at[at, :], sem.at[2])

    if tail:

        @pl.when(step == groups)
        def _():
            lax.fori_loop(0, chunks, project, 0)

    @pl.when(step == last)
    def _():
        for x in stores(0, 0):
            x.wait()

        def out(i, carry):
            give(i).start()
            give(i).wait()
            return carry

        lax.fori_loop(0, chunks, out, 0)


def feed_kernel(tiles, pieces, last, prior, meta, second, branch, *rest):
    we, wr, rest = rest[:pieces], rest[pieces : 2 * pieces], rest[2 * pieces :]
    be, rest = rest[0], rest[1:]
    if last:
        (live, middle, cotc, vecs), rest = rest[:4], rest[4:]
        sg_in, rest = rest[:prior], rest[prior:]
    grads, rest = rest[:tiles], rest[tiles:]
    dbe, red = rest[:2]
    if last:
        (mg, ag, vec), rest = rest[2:5], rest[5:]
    else:
        (sg,), rest = rest[2:3], rest[3:]
    sec, br, e_buf, r_buf, gbuf, ra, sa, half, sem, w_sem, g_sem = rest[:11]
    if last:
        mid_buf, cot_buf, live_buf, sg_buf = rest[11:]
    ch, d = sec.shape
    wide = e_buf.shape[2]
    c0, me = meta[AT_C], meta[AT_ME]
    y = me & 1
    chunks = meta[2]

    def move(a, b, i):
        return pltpu.make_async_copy(a, b, sem.at[i])

    def loads(c):
        rows = pl.ds(pl.multiple_of(c * ch, ch), ch)
        return [move(second.at[rows, :], sec, 0), move(branch.at[rows, :], br, 1)]

    def weights(i):
        if pieces == 1:
            at = pl.ds(pl.multiple_of((i ^ c0) * wide, BLK), wide)
            a, b = we[0].at[:, at], wr[0].at[at, :]
        else:
            a, b = we[i], wr[i]
        return [
            pltpu.make_async_copy(a, e_buf.at[i], w_sem.at[2 * i]),
            pltpu.make_async_copy(b, r_buf.at[i], w_sem.at[2 * i + 1]),
        ]

    def extras(c):
        rows = pl.ds(pl.multiple_of(c * ch, ch), ch)
        out = [
            move(middle.at[rows, :], mid_buf, 2),
            move(cotc.at[rows, :], cot_buf, 3),
            move(live.at[rows, :], live_buf, 4),
        ]
        return out + [move(x.at[rows, :], sg_buf, 5) for x in sg_in]

    def store(i):
        return pltpu.make_async_copy(gbuf.at[i], grads[i], g_sem.at[i])

    if last:
        vec[...] = jnp.zeros_like(vec)

    def chunk(c, carry):
        rows = pl.ds(pl.multiple_of(c * ch, ch), ch)
        for x in loads(c):
            x.start()

        @pl.when(c == 0)
        def _():
            for i in range(tiles):
                for x in weights(i):
                    x.start()

        if last:
            for x in extras(c):
                x.start()
        for x in loads(c):
            x.wait()

        def tile(t, carry):
            for i in range(tiles):

                @pl.when((t == i) & (c == 0))
                def _():
                    for x in weights(i):
                        x.wait()

            at = pl.ds(pl.multiple_of((t ^ c0) * wide, BLK), wide)
            e, r = e_buf[t], r_buf[t]
            u = dot(sec[...], e) + be[:, at]
            cdf = 0.5 * (1.0 + lax.erf(u * 0.7071067811865476))
            h = (u * cdf).astype(BF)
            slope = cdf + u * (jnp.exp(-0.5 * u * u) * 0.3989422804014327)
            pg = (dot_nt(br[...], r) * slope).astype(BF)
            grad_b = jnp.sum(pg.astype(F32), axis=0, keepdims=True)

            def put(low, g):
                n = wide // 2
                for i in range(2):
                    ref = gbuf.at[t, i ^ y, low : low + d, :]
                    part = g[:, i * n : (i + 1) * n]

                    @pl.when(c == 0)
                    def _():
                        ref[...] = part.astype(BF)

                    @pl.when(c > 0)
                    def _():
                        ref[...] = (ref[...].astype(F32) + part).astype(BF)

            put(0, dot_tn(sec[...], pg))
            put(d, dot_tn(br[...], h))

            @pl.when(c == 0)
            def _():
                dbe[:, at] = grad_b

            @pl.when(c > 0)
            def _():
                dbe[:, at] = dbe[:, at] + grad_b

            red_t = dot(h, r)
            sg_t = dot_nt(pg, e)

            @pl.when(t == 0)
            def _():
                ra[...] = red_t
                sa[...] = sg_t

            @pl.when(t > 0)
            def _():
                ra[...] = ra[...] + red_t
                sa[...] = sa[...] + sg_t

            for i in range(tiles):

                @pl.when((t == i) & (c == chunks - 1))
                def _():
                    store(i).start()

            return carry

        lax.fori_loop(0, tiles, tile, 0)
        half[0] = ra[...].astype(BF)
        outs = [move(half.at[0], red.at[rows, :], 0)]
        outs[0].start()
        if not last:
            half[1] = sa[...].astype(BF)
            outs.append(move(half.at[1], sg.at[rows, :], 1))
            outs[1].start()
        else:
            for x in extras(c):
                x.wait()
            for b in range(ch // BLK):
                at = slice(b * BLK, (b + 1) * BLK)
                nrm, scale = norm_stats(mid_buf[at, :])
                g = sa[at, :]
                if prior:
                    g = g + sg_buf[at, :].astype(F32)
                m = cot_buf[at, :].astype(F32) + norm_back(g, nrm, scale, vecs[G2])
                ra[at, :] = m
                kept = m * live_buf[at, :]
                half[1, at, :] = kept.astype(BF)
                vec[0:1, :] = vec[0:1, :] + jnp.sum(g * nrm, axis=0, keepdims=True)
                vec[1:2, :] = vec[1:2, :] + jnp.sum(g, axis=0, keepdims=True)
                vec[2:3, :] = vec[2:3, :] + jnp.sum(kept, axis=0, keepdims=True)
            outs += [move(half.at[1], ag.at[rows, :], 1), move(ra, mg.at[rows, :], 2)]
            for x in outs[1:]:
                x.start()
        for x in outs:
            x.wait()
        return carry

    lax.fori_loop(0, chunks, chunk, 0)
    for i in range(tiles):
        store(i).wait()


def back_kernel(pieces, groups, split, meta, ag, perm, pick, pick_t, qkv, probs, mixed, first, *rest):
    w_out, rest = rest[:pieces], rest[pieces:]
    sources, rest = rest[:5], rest[5:]
    dqkv, rest = rest[0], rest[1:]
    grads, rest = rest[: 2 if split else 1], rest[2 if split else 1 :]
    dba, drel, dperm, dmix, table, out, in_sem, sem = rest
    rows, d = ag.shape
    blocks = rows // BLK
    step = pl.program_id(0)
    chunks = meta[2]
    n0 = meta[1]
    c, me = meta[AT_C], meta[AT_ME]
    half = d // 2
    stays = (step >> 1) == (me >> 1)

    def reload(chunk):
        @pl.when(chunks > 1)
        def _():
            at = pl.ds(pl.multiple_of(chunk * rows, rows), rows)
            g = jnp.minimum(step, groups - 1)
            cols = pl.ds(pl.multiple_of(g * GW, BLK), GW)
            ag_h, qkv_h, probs_h, mixed_h, first_h = sources
            pairs = [(ag_h.at[at, :], ag), (qkv_h.at[at, cols], qkv), (mixed_h.at[at, :], mixed), (first_h.at[at, :], first)]
            pairs += [(probs_h.at[pl.ds(chunk * blocks, blocks), g], probs.at[:, 0])]
            run_copies(pairs, in_sem)

    def store(chunk, g):
        at = pl.ds(pl.multiple_of(chunk * rows, rows), rows)
        cols = pl.ds(pl.multiple_of(g * GW, BLK), GW)
        return pltpu.make_async_copy(out, dqkv.at[at, cols], sem.at[0])

    def put(i, ref, value):
        @pl.when(i == 0)
        def _():
            ref[...] = value.astype(ref.dtype)

        @pl.when(i > 0)
        def _():
            ref[...] = (ref[...].astype(F32) + value).astype(ref.dtype)

    def put_grad(i, low, high, value):
        if not split:
            put(i, grads[0].at[0, low:high, :], value)
            return

        @pl.when(stays)
        def _():
            put(i, grads[0].at[0, low:high, :], value)

        @pl.when(jnp.logical_not(stays))
        def _():
            put(i, grads[1].at[0, low:high, :], value)

    def weights(i, carry):
        reload(chunks - 1 - i)
        wide = groups * BLK
        for j in range(2):
            put_grad(i, j * wide, (j + 1) * wide, dot_tn(mixed[...], ag[:, j * half : (j + 1) * half]))
        return carry

    def heads(i, carry):
        chunk = chunks - 1 - i
        reload(chunk)
        if pieces == 1:
            dmix[...] = dot_nt(ag[...], w_out[0][...]).astype(BF)
        else:
            near = pl.ds(pl.multiple_of(c * half, BLK), half)
            far = pl.ds(pl.multiple_of((1 - c) * half, BLK), half)
            dmix[...] = (dot_nt(ag[:, near], w_out[0][...]) + dot_nt(ag[:, far], w_out[1][...])).astype(BF)
        for b in range(blocks):
            at = slice(b * BLK, (b + 1) * BLK)
            kind = jnp.where(chunk * blocks + b < n0, 0, 1)
            q = qkv[at, 0:BLK]
            k = qkv[at, BLK : 2 * BLK]
            v = qkv[at, 2 * BLK : 3 * BLK]
            do = dmix[at, :]
            p = probs[b, 0]
            dp = dot_nt(spread_rows(v), do).reshape(GROUP, BLK, BLK)
            pf = p.astype(F32).reshape(GROUP, BLK, BLK)
            x = pf * dp
            ds = x - pf * jnp.sum(x, axis=1, keepdims=True)
            ds = ds.astype(BF).reshape(GROUP * BLK, BLK)
            table[kind] = table[kind] + ds.astype(F32)
            dv = fold_rows(dot(p, do))
            dk = fold_rows(dot(ds, q))
            kt = k.astype(F32).T.astype(BF)
            dq = (dot(spread_cols(kt), ds) * HEAD_DIM**-0.5).T
            dperm[at, 0:BLK] = dq.astype(BF)
            dperm[at, BLK : 2 * BLK] = dk.astype(BF)
            dperm[at, 2 * BLK : 3 * BLK] = dv.astype(BF)
        x = dot_nt(dperm[...], perm[...]).astype(BF)

        @pl.when((step > 0) | (i > 0))
        def _():
            store(0, 0).wait()

        out[...] = x
        store(chunk, step).start()
        put_grad(i, 0, d, dot_tn(first[...], x))
        put(i, dba, jnp.sum(x.astype(F32), axis=0, keepdims=True))
        return carry

    @pl.when(step == groups)
    def _():
        lax.fori_loop(0, chunks, weights, 0)
        store(0, 0).wait()

    @pl.when(step < groups)
    def _():
        table[...] = jnp.zeros_like(table)
        lax.fori_loop(0, chunks, heads, 0)
        for h in range(GROUP):
            total = jnp.zeros((BLK, BLK), F32)
            for kind in range(2):
                a = table[kind, h * BLK : (h + 1) * BLK, :]
                a = dot(a.astype(BF), pick[kind]).astype(BF)
                total = total + dot(pick_t[kind], a)
            wide = jnp.concatenate([total, jnp.zeros_like(total)], axis=1)
            wide = pltpu.roll(wide, 0, 1, stride=1, stride_axis=0)
            drel[pl.ds(step * GROUP + h, 1), :] = jnp.sum(wide, axis=0, keepdims=True)


def row_tiles(rows, size=384):
    return [(a, min(size, rows - a)) for a in range(0, rows, size)]


def ends_kernel(pieces, meta, live, xc, cotc, mg, vecs, *rest):
    n = len(pieces)
    dqkv, rest = rest[:n], rest[n:]
    w = []
    for k in pieces:
        w.append(rest[:k])
        rest = rest[k:]
    hi, lo, vec, fg = rest
    rows, d = xc.shape
    blocks = rows // BLK
    chunk = pl.program_id(0)
    c = meta[AT_C]
    half = d // 2

    @pl.when(chunk == 0)
    def _():
        vec[...] = jnp.zeros_like(vec)

    for s in range(n):
        if len(w[s]) == 1:
            v = dot_nt(dqkv[s][...], w[s][0][...])
            fg[...] = v if s == 0 else fg[...] + v
        else:
            for i in range(2):
                cols = pl.ds(pl.multiple_of((c if i == 0 else 1 - c) * half, BLK), half)
                fg[:, cols] = fg[:, cols] + dot_nt(dqkv[s][...], w[s][i][...])

    for b in range(blocks):
        at = slice(b * BLK, (b + 1) * BLK)
        keep = live[at, :]
        nrm, scale = norm_stats(xc[at, :].astype(F32))
        g = fg[at, :]
        up = cotc[at, :].astype(F32)
        delta = mg[at, :] - up + norm_back(g, nrm, scale, vecs[G1])
        top = delta.astype(BF)
        hi[at, :] = top
        lo[at, :] = (delta - top.astype(F32)).astype(BF)
        vec[0:1, :] = vec[0:1, :] + jnp.sum(g * nrm, axis=0, keepdims=True)
        vec[1:2, :] = vec[1:2, :] + jnp.sum(g, axis=0, keepdims=True)
        vec[2:3, :] = vec[2:3, :] + jnp.sum(up * keep, axis=0, keepdims=True)


def result_kernel(prior, meta, idx, live, middle, vecs, patches, *rest):
    red, (result, res) = rest[:prior], rest[prior:]
    rows = middle.shape[0]
    chunk = pl.program_id(0)
    for b in range(rows // BLK):
        at = slice(b * BLK, (b + 1) * BLK)
        reduced = vecs[RB]
        for x in red:
            reduced = reduced + x[at, :].astype(F32)
        res[at, :] = (middle[at, :] + live[at, :] * reduced).astype(BF)
    for start, size in row_tiles(patches.shape[0]):
        at = slice(start, start + size)
        spots = start + lax.broadcasted_iota(jnp.int32, (size, rows), 0)
        hit = (spots == idx[0]).astype(F32)
        here = jnp.sum(hit, axis=1, keepdims=True) > 0.0
        new = dot(hit.astype(BF), res[...])

        @pl.when(chunk == 0)
        def _():
            result[at, :] = jnp.where(here, new, patches[at, :].astype(F32)).astype(BF)

        @pl.when(chunk > 0)
        def _():
            result[at, :] = jnp.where(here, new, result[at, :].astype(F32)).astype(BF)


def scatter_kernel(meta, idx, hi, lo, cot, input_grad):
    rows = hi.shape[0]
    chunk = pl.program_id(0)
    for start, size in row_tiles(cot.shape[0]):
        at = slice(start, start + size)
        spots = start + lax.broadcasted_iota(jnp.int32, (size, rows), 0)
        put = (spots == idx[0]).astype(F32).astype(BF)
        grad = dot(put, hi[...]) + dot(put, lo[...])

        @pl.when(chunk == 0)
        def _():
            input_grad[at, :] = cot[at, :].astype(F32) + grad

        @pl.when(chunk > 0)
        def _():
            input_grad[at, :] = input_grad[at, :] + grad


SMEM = pl.BlockSpec(memory_space=pltpu.SMEM)
ANY = pl.BlockSpec(memory_space=pl.ANY)
SHORT = pl.CostEstimate(flops=1000, bytes_accessed=1000, transcendentals=0)
PACK = 24


def pack_kernel(where, v1, v2, *refs):
    n = 2
    db, dba, drel = (refs[i * n : (i + 1) * n] for i in range(3))
    outs = refs[3 * n :]
    d = v1.shape[1]
    half = d // 2
    for s in range(n):
        t = where[0] if s == 0 else 1 - where[0]
        cols = pl.ds(pl.multiple_of(t * half, BLK), half)
        out = outs[s]
        out[...] = jnp.zeros_like(out)
        out[0:1, :] = db[s][...].astype(BF).astype(F32)
        out[1:2, 0 : dba[s].shape[1]] = dba[s][...]
        for i, (v, r) in enumerate(((v1, 0), (v1, 1), (v2, 2), (v2, 0), (v2, 1), (v1, 2))):
            out[2 + i : 3 + i, 0:half] = v[r : r + 1, cols]
        k = drel[s].shape[0]
        out[8 : 8 + k, 0 : drel[s].shape[1]] = drel[s][...]


def pack(t, v1, v2, db, dba, drel):
    v = pl.BlockSpec(memory_space=pltpu.VMEM)
    shape = sds((PACK, db[0].shape[1]), F32)
    return pl.pallas_call(
        pack_kernel,
        in_specs=[SMEM] + [v] * 8,
        out_specs=[v, v],
        out_shape=[shape, shape],
        cost_estimate=SHORT,
        name="pack",
    )(t, v1, v2, *db, *dba, *drel)


def place_feed_kernel(ids, e0, e1, r0, r1, *rest):
    exp, red = rest[-2:]
    low = ids[2] & 1
    exp[...] = jnp.where(low == 0, e0[0], e1[0]).astype(F32)
    red[...] = jnp.where(low == 1, r0[0], r1[0]).astype(F32).T


def place_feed(ids, near, far, d, hidden, other_core, other_y, onto=()):
    spec = pl.BlockSpec((1, GW, GW), lambda j, ids: (j ^ (ids[2] >> 1), 0, 0))
    tile = lambda ids: (ids[0] ^ other_core) * 2 + (ids[1] ^ other_y)
    return pl.pallas_call(
        place_feed_kernel,
        grid_spec=pltpu.PrefetchScalarGridSpec(
            num_scalar_prefetch=1,
            grid=(2,),
            in_specs=[spec] * 4 + [ANY] * len(onto),
            out_specs=[
                pl.BlockSpec((GW, GW), lambda j, ids: (j, tile(ids))),
                pl.BlockSpec((GW, GW), lambda j, ids: (tile(ids), j)),
            ],
        ),
        out_shape=[sds((d, hidden), F32), sds((hidden, d), F32)],
        input_output_aliases={5: 0, 6: 1} if onto else {},
        cost_estimate=SHORT,
        name="place_feed",
    )(ids, near, far, near, far, *onto)


def place_attend_kernel(ids, *refs):
    att, out = refs[-2:]
    for i in range(4):
        near, far = refs[i], refs[4 + i]
        x = jnp.where((i >> 1) == ids[0], near[0, 0], far[0, 0]).astype(F32)
        if i < 3:
            att[:, i * GW : (i + 1) * GW] = x
        else:
            out[...] = x


def place_attend(ids, near, far, d, other, onto=()):
    r = near.shape[2]
    ins = [
        pl.BlockSpec((1, 1, r, GW), lambda j, ids, i=i: (j ^ (ids[2] >> 1), (i & 1) ^ ids[1], 0, 0))
        for i in range(4)
    ]
    half = lambda ids: (ids[2] & 1) ^ other
    return pl.pallas_call(
        place_attend_kernel,
        grid_spec=pltpu.PrefetchScalarGridSpec(
            num_scalar_prefetch=1,
            grid=(2,),
            in_specs=ins + ins + [ANY] * len(onto),
            out_specs=[
                pl.BlockSpec((r, 3 * GW), lambda j, ids: (2 * half(ids) + j, 0)),
                pl.BlockSpec((r, GW), lambda j, ids: (j, half(ids))),
            ],
        ),
        out_shape=[sds((d, 3 * GW), F32), sds((GW, d), F32)],
        input_output_aliases={9: 0, 10: 1} if onto else {},
        cost_estimate=SHORT,
        name="place_attend",
    )(ids, near, near, near, near, far, far, far, far, *onto)


def guarded(body, axis):
    def run(meta, *refs):
        @pl.when(pl.program_id(axis) < meta[2])
        def _():
            body(meta, *refs)

    return run


def clamp(i, meta):
    return jnp.minimum(i, meta[2] - 1)


def whole_spec(shape):
    zeros = (0,) * len(shape)
    return pl.BlockSpec(shape, lambda *_: zeros, pipeline_mode=pl.Buffered(1))


def chunk_spec(shape):
    zeros = (0,) * (len(shape) - 1)
    return pl.BlockSpec(shape, lambda i, meta: (clamp(i, meta),) + zeros)


def sds(shape, dtype):
    return jax.ShapeDtypeStruct(shape, dtype)


def w_(a):
    return (a, whole_spec(a.shape))


def o_(shape, dtype):
    return (sds(shape, dtype), whole_spec(shape))


class Local:
    def __init__(self, rows):
        self.rows = rows
        self.windows = rows // SLOTS
        worst = (self.windows + 1) // 2
        self.per_chunk = min(5, max(worst, 1))
        self.chunks = -(-worst // self.per_chunk)
        self.ch = self.per_chunk * BLK
        self.all = self.ch * self.chunks
        pick, mask = kind_tables()
        self.mask = jnp.asarray(mask, BF)
        self.perm = jnp.asarray(group_perm(), BF)
        up, down_t = stride_tables()
        self.up, self.down_t = jnp.asarray(up, BF), jnp.asarray(down_t, BF)
        slot = np.where(pick.sum(2) > 0, pick.argmax(2), 0)
        corner = (slot[0] // SIDE < 3) & (slot[0] % SIDE < 3)
        self.slots = jnp.asarray(np.stack([slot[0], slot[1], corner])[:, :, None], jnp.int32)

    def row(self, k, dt):
        return (sds((self.all, k), dt), chunk_spec((self.ch, k)))

    def c(self, a):
        return (a, chunk_spec((self.ch,) + a.shape[1:]))

    def call(self, body, name, ins, outs, scratch=(), grid=None, axis=0, flops=0, size=0, limit=VMEM_LIMIT):
        f = pl.pallas_call(
            body if axis is None else guarded(body, axis),
            out_shape=[o for o, _ in outs],
            grid_spec=pltpu.PrefetchScalarGridSpec(
                num_scalar_prefetch=1,
                grid=(self.chunks,) if grid is None else grid,
                in_specs=[s for _, s in ins],
                out_specs=[s for _, s in outs],
                scratch_shapes=list(scratch),
            ),
            compiler_params=pltpu.CompilerParams(vmem_limit_bytes=limit),
            cost_estimate=pl.CostEstimate(flops=int(flops), bytes_accessed=int(size), transcendentals=0),
            name=name,
        )
        return f(self.meta, *[a for a, _ in ins])

    def bound(self, w, bias, table):
        ins = [w, bias.reshape(bias.shape[0], -1), table]
        return pl.pallas_call(
            bound_kernel,
            out_shape=sds((8, BLK), F32),
            compiler_params=pltpu.CompilerParams(vmem_limit_bytes=VMEM_LIMIT),
            name="bound",
        )(*ins)

    def plan(self, place, counts, bounds, vecs):
        v = pl.BlockSpec(memory_space=pltpu.VMEM)
        self.meta = pl.pallas_call(
            partial(plan_kernel, self.windows, counts.shape[0], self.per_chunk),
            out_shape=sds((PLAN_HEAD + 3 * self.windows,), jnp.int32),
            in_specs=[SMEM, SMEM, v, v],
            out_specs=SMEM,
            name="plan",
        )(place, counts, bounds, vecs)

    def gather(self, patches, cot, vecs):
        ch, d = self.ch, patches.shape[1]
        idx = (sds((self.chunks, 1, ch), jnp.int32), pl.BlockSpec((1, 1, ch), lambda i, meta: (clamp(i, meta), 0, 0)))
        return self.call(
            partial(gather_kernel, self.windows),
            "gather_rows",
            [w_(self.slots), w_(patches), w_(cot), w_(vecs)],
            [self.row(d, BF)] * 4 + [self.row(1, F32), idx],
            [pltpu.VMEM((BLK, 1), jnp.int32), pltpu.VMEM((ch, self.rows), BF)],
            flops=4 * ch * self.rows * d,
            size=8 * self.rows * d,
        )

    def attend(self, live, first, bias, rel, w, tail=None, before=()):
        ch, d = self.ch, first.shape[1]
        width = w[0].shape[1]
        groups = width // GW
        clip = lambda g: jnp.minimum(g, groups - 1)
        block = lambda a: (a, pl.BlockSpec((ch,) + a.shape[1:], lambda g, meta: (0, 0), pipeline_mode=pl.Buffered(1)))
        cols = lambda a, k: (a, pl.BlockSpec((a.shape[0], k), lambda g, meta: (0, clip(g))))
        full = lambda k, dt: (sds((self.all, k), dt), ANY)
        pshape = (self.per_chunk * self.chunks, groups, GROUP * BLK, BLK)
        ins = [block(live), block(first), w_(self.perm), w_(self.up), w_(self.mask), cols(bias, GW), w_(rel)]
        ins += [cols(a, GW) for a in w]
        outs = [full(width, BF), (sds(pshape, BF), ANY), full(groups * BLK, BF)]
        v, dma = pltpu.VMEM, pltpu.SemaphoreType.DMA
        scratch = [v((2, GROUP * BLK, BLK), BF), v((ch, GW), BF), v((self.per_chunk, GROUP * BLK, BLK), BF)]
        scratch += [v((self.chunks, ch, groups * BLK), BF), dma((4,)), dma((3,))]
        steps = groups
        again = [live, first]
        if tail is not None:
            steps += 1
            xc, vecs, wo = tail
            ins += [block(xc), w_(vecs)]
            ins += [block(m) for m, _ in before] + [w_(a) for _, a in before] + [w_(a) for a in wo]
            again += [xc] + [m for m, _ in before]
            outs += [full(d, F32), full(d, BF)]
            scratch += [v((ch, d), F32), v((ch, d), BF), v((ch, d), F32)]
        ins += [(a, ANY) for a in again]
        return self.call(
            partial(attend_kernel, len(w), groups, tail is not None, len(before)),
            "attend",
            ins,
            outs,
            scratch,
            grid=(steps,),
            axis=None,
            flops=0.16 * ch * d * width,
            size=0.4 * ch * d,
        )

    def feed(self, second, branch, we, wr, be, last=None):
        ch, d = self.ch, second.shape[1]
        hidden = be.shape[1]
        pieces = len(we)
        wide = 2 * GW
        tiles = hidden // wide
        any_ = lambda a: (a, ANY)
        full = lambda dt: (sds((self.all, d), dt), ANY)
        ins = [any_(a) for a in (second, branch, *we, *wr)] + [w_(be)]
        outs = [(sds((2, 2 * d, GW), BF), ANY)] * tiles + [o_((1, hidden), F32), full(BF)]
        v = pltpu.VMEM
        scratch = [v((ch, d), BF)] * 2 + [v((tiles, d, wide), BF), v((tiles, wide, d), BF)]
        scratch += [v((tiles, 2, 2 * d, GW), BF), v((ch, d), F32), v((ch, d), F32), v((2, ch, d), BF)]
        dma = pltpu.SemaphoreType.DMA
        scratch += [dma((6,)), dma((2 * tiles,)), dma((tiles,))]
        prior = 0
        if last is None:
            outs += [full(BF)]
        else:
            live, middle, cotc, vecs, sums = last
            prior = len(sums)
            ins += [any_(live), any_(middle), any_(cotc), w_(vecs)] + [any_(a) for a in sums]
            outs += [full(F32), full(BF), o_((8, d), F32)]
            scratch += [v((ch, d), F32), v((ch, d), BF), v((ch, 1), F32), v((ch, d), BF)]
        return self.call(
            partial(feed_kernel, tiles, pieces, last is not None, prior),
            "feed",
            ins,
            outs,
            scratch,
            grid=(1,),
            axis=None,
            flops=12 * ch * d * hidden,
            size=8 * d * hidden,
        )

    def back(self, ag, qkv, probs, mixed, first, wo):
        ch, d = self.ch, first.shape[1]
        width = qkv.shape[1]
        groups = width // GW
        split = groups == 3
        clip = lambda g: jnp.minimum(g, groups - 1)
        block = lambda a: (a, pl.BlockSpec((ch,) + a.shape[1:], lambda g, meta: (0, 0), pipeline_mode=pl.Buffered(1)))
        cols = pl.BlockSpec((ch, GW), lambda g, meta: (0, clip(g)))
        pspec = pl.BlockSpec((self.per_chunk, 1) + probs.shape[2:], lambda g, meta: (0, clip(g), 0, 0))
        one = (1, 2 * groups * BLK, GW)
        if split:

            def tile(start):
                return lambda g, meta: (
                    (jnp.clip(g - start(meta[AT_ME] >> 1), 0, 1) ^ meta[AT_ME]) & 1,
                    0,
                    0,
                )

            shape = sds((2,) + one[1:], BF)
            grads = [(shape, pl.BlockSpec(one, tile(lambda h: 2 * h))), (shape, pl.BlockSpec(one, tile(lambda h: 2 - 2 * h)))]
        else:
            grads = [(sds((groups + 1,) + one[1:], BF), pl.BlockSpec(one, lambda g, meta: (g, 0, 0)))]
        v, dma = pltpu.VMEM, pltpu.SemaphoreType.DMA
        return self.call(
            partial(back_kernel, len(wo), groups, split),
            "back",
            [block(ag), w_(self.perm), w_(self.up), w_(self.down_t), (qkv, cols), (probs, pspec)]
            + [block(mixed), block(first)]
            + [(a, pl.BlockSpec((BLK, a.shape[1]), lambda g, meta: (clip(g), 0))) for a in wo]
            + [(a, ANY) for a in (ag, qkv, probs, mixed, first)],
            [(sds((self.all, width), BF), ANY), *grads]
            + [(sds((1, width), F32), pl.BlockSpec((1, GW), lambda g, meta: (0, clip(g))))]
            + [o_((groups * GROUP, 2 * BLK), F32)],
            [v((ch, GW), BF), v((ch, BLK), BF), v((2, GROUP * BLK, BLK), F32), v((ch, GW), BF), dma((5,)), dma((1,))],
            grid=(groups + 1,),
            axis=None,
            flops=14 * ch * d * width,
            size=30 * ch * d,
        )

    def ends(self, live, xc, cotc, mg, vecs, dqkv, ws):
        ch, d = self.ch, xc.shape[1]
        c = self.c
        return self.call(
            partial(ends_kernel, [len(a) for a in ws]),
            "ends",
            [c(live), c(xc), c(cotc), c(mg), w_(vecs)] + [c(a) for a in dqkv] + [w_(a) for s in ws for a in s],
            [self.row(d, BF)] * 2 + [o_((8, d), F32)],
            [pltpu.VMEM((ch, d), F32)],
            flops=6 * ch * d * d,
            size=30 * ch * d,
        )

    def by_row(self, idx):
        return (idx, pl.BlockSpec((1, 1, self.ch), lambda i, meta: (clamp(i, meta), 0, 0)))

    def result(self, idx, live, middle, vecs, patches, red):
        ch, d = self.ch, patches.shape[1]
        c = self.c
        (out,) = self.call(
            partial(result_kernel, len(red)),
            "result",
            [self.by_row(idx), c(live), c(middle), w_(vecs), w_(patches)] + [c(a) for a in red],
            [o_(patches.shape, BF)],
            [pltpu.VMEM((ch, d), BF)],
            flops=2 * ch * self.rows * d,
            size=12 * self.rows * d,
        )
        return out

    def scatter(self, idx, hi, lo, cot):
        ch, d = self.ch, cot.shape[1]
        (out,) = self.call(
            scatter_kernel,
            "scatter",
            [self.by_row(idx), self.c(hi), self.c(lo), w_(cot)],
            [o_(cot.shape, F32)],
            flops=4 * ch * self.rows * d,
            size=12 * self.rows * d,
        )
        return out


CODES = 169


def pad_table(table):
    return jnp.pad(table.astype(F32), ((0, 0), (4, 2 * BLK - CODES - 4)))


def bias_row(bias):
    b = bias.astype(F32)
    return jnp.stack([b[:, 0], jnp.zeros_like(b[:, 0]), b[:, 1]], axis=1).reshape(1, -1)


def pick_half(a, bit, axis=0):
    n = a.shape[axis] // 2
    return lax.dynamic_slice_in_dim(a, bit * n, n, axis)


def swap(a, axis, n, step=1):
    return lax.ppermute(a, axis, [(i, i ^ step) for i in range(n)])


def plus(*xs):
    total = xs[0].astype(F32)
    for x in xs[1:]:
        total = total + x.astype(F32)
    return total.astype(BF)


def after(x, *deps):
    return lax.optimization_barrier((x, *deps))[0]


def on_device(
    nz,
    nt,
    patches,
    gain_first,
    shift_first,
    attend_weight,
    attend_bias,
    offset_table,
    output_weight,
    output_bias,
    gain_second,
    shift_second,
    expand_weight,
    expand_bias,
    reduce_weight,
    reduce_bias,
    crop_counts,
    cotangent,
):
    fast = nt == 2 and nz == 4
    t, c, y, z = (lax.axis_index(a) for a in ("tensor", "core", "y", "z"))
    rows, d = patches.shape
    local = Local(rows)
    vec = lambda a: a.astype(F32).reshape(1, -1)
    vecs = jnp.stack([gain_first, shift_first, gain_second, shift_second, output_bias, reduce_bias]).astype(F32)
    bound = local.bound(attend_weight, attend_bias, offset_table)
    if fast:
        got, w_att_in, w_out_in = lax.optimization_barrier(
            (swap(bound, "tensor", nt), attend_weight, output_weight)
        )
        bound = jnp.maximum(bound, got)
        x_att = swap(pick_half(pick_half(w_att_in, c), y), "tensor", nt)
        x_out = swap(pick_half(w_out_in, c, 1), "tensor", nt)
        small = lambda a: [a, swap(a, "tensor", nt)]
        me = c * 2 + y
    else:
        w_att = [[lax.all_gather(attend_weight, "tensor", axis=1, tiled=True)]]
        w_out = [[lax.all_gather(output_weight, "tensor", axis=0, tiled=True)]]
        w_exp = [[lax.all_gather(expand_weight, "tensor", axis=1, tiled=True)]]
        w_red = [[lax.all_gather(reduce_weight, "tensor", axis=0, tiled=True)]]
        bound = lax.pmax(bound, "tensor")
        small = lambda a: [lax.all_gather(a, "tensor", axis=0, tiled=True)]
        me = c = 0 * c
    place = jnp.stack([t * local.windows, c, me]).astype(jnp.int32)
    local.plan(place, crop_counts, bound, vecs)
    bias, rel, b_exp = small(attend_bias), small(pad_table(offset_table)), small(expand_bias)
    xc, cotc, branch, first, live, idx = local.gather(patches, cotangent, vecs)

    if fast:
        xc, first, x_att, bias, rel, b_exp = lax.optimization_barrier((xc, first, x_att, bias, rel, b_exp))
    bias, b_exp = [bias_row(b) for b in bias], [vec(a) for a in b_exp]
    if fast:
        s_exp = after(pick_half(pick_half(expand_weight, c, 1), y, 1), x_att)
        first, s_exp = lax.optimization_barrier((first, s_exp))
        x_exp = swap(s_exp, "tensor", nt)
        y_att = swap(x_att, "y", 2)
        w_out = [[output_weight], [x_out, swap(x_out, "core", 2)]]
        qkv0, probs0, mixed0 = local.attend(live, first, bias[0], rel[0], [attend_weight])
        y_att, x_exp, x_out, mixed0 = lax.optimization_barrier((y_att, x_exp, x_out, mixed0))
        x_att = jnp.where(y == 0, jnp.concatenate([x_att, y_att], 0), jnp.concatenate([y_att, x_att], 0))
        w_att = [[attend_weight], [x_att, swap(x_att, "core", 2)]]
        y_exp = swap(x_exp, "y", 2)
        first, s_red = lax.optimization_barrier((first, after(pick_half(reduce_weight, c, 0), w_att[1][0])))
        x_red = swap(s_red, "tensor", nt)
        held = [(qkv0, probs0, mixed0)]
        before = [(mixed0, output_weight)]
    else:
        held, before = [], []
    qkv1, probs1, mixed1, middle, second = local.attend(
        live, first, bias[-1], rel[-1], w_att[-1], (xc, vecs, w_out[-1]), before
    )
    held.append((qkv1, probs1, mixed1))
    n = len(w_att)

    def bias_grad(a):
        a = a.reshape(-1, 3, HEAD_DIM)
        return jnp.stack([a[:, 0], a[:, 2]], axis=1)

    if fast:
        y_exp, x_red, second = lax.optimization_barrier((y_exp, x_red, second))
        x_exp = jnp.where(y == 0, jnp.concatenate([x_exp, y_exp], 1), jnp.concatenate([y_exp, x_exp], 1))
        second, x_exp = lax.optimization_barrier((second, x_exp))
        k0, s0, db0, red0, sg0 = local.feed(second, branch, [expand_weight], [reduce_weight], b_exp[0])
        e1 = [x_exp, swap(x_exp, "core", 2)]
        r1 = [x_red, swap(x_red, "core", 2)]
        k1, s1, db1, red1, mg, ag, v2 = local.feed(second, branch, e1, r1, b_exp[1], (live, middle, cotc, vecs, [sg0]))
        def split(keep, got):
            h = keep.shape[1] // 2
            return [plus(keep[:, i * h : (i + 1) * h], got[:, i * h : (i + 1) * h]) for i in range(2)]

        def first_leg(own, peer):
            return swap(peer[0], "tensor", nt), swap(jnp.stack([own[1][1], peer[1][1]]), "y", 2)

        def second_leg(own, peer, gx, gy):
            low = plus(own[0][1], gx[1])
            up = plus(own[0][0], gx[0])
            peer_b = plus(peer[1][0], gy[1])
            own_b = plus(own[1][0], gy[0])
            return up, swap(low, "y", 2), own_b, swap(peer_b, "tensor", nt)

        def z_first(up, gy, own_b, gx):
            a, b = plus(up, gy), plus(own_b, gx)
            return jnp.where(z % 2 == 0, a, b), jnp.where(z % 2 == 0, b, a)

        def z_second(keep, got):
            hi = z // 2
            total = lambda i: plus(pick_half(keep, i), pick_half(got, i))
            return total(hi), total(1 - hi)

        ff_peer = split(k1, swap(s1, "core", 2))
        ff_own = split(k0, swap(s0, "core", 2))
        ag, *ff = lax.optimization_barrier((ag, *ff_own, *ff_peer))
        ff_own, ff_peer = ff[:2], ff[2:]
        fx, fy = first_leg(ff_own, ff_peer)
        dq1, gk1, gs1, dba1, drel1 = local.back(ag, *held[1], first, w_out[1])
        dq1, gs1, red0 = lax.optimization_barrier((dq1, gs1, red0))
        got1 = swap(gs1, "core", 2)
        result = local.result(idx, live, middle, vecs, patches, [red0, red1])
        fx, fy, dq1, result, ag = lax.optimization_barrier((fx, fy, dq1, result, ag))
        ff_up, fy, ff_b, fx = second_leg(ff_own, ff_peer, fx, fy)
        dq0, gk0, gs0, dba0, drel0 = local.back(ag, *held[0], first, w_out[0])
        got1, fx, fy, dq0, gs0 = lax.optimization_barrier((got1, fx, fy, dq0, gs0))
        got0 = swap(gs0, "core", 2)
        ff_keep, ff_send = z_first(ff_up, fy, ff_b, fx)
        ff_got = swap(ff_send, "z", nz, 1)
        got1, got0, ff_keep, ff_send = lax.optimization_barrier((got1, got0, ff_keep, ff_send))
        at_peer = split(gk1, got1)
        at_own = split(gk0, got0)
        ax, ay = first_leg(at_own, at_peer)
        mg, *at4, ff_keep, ff_send = lax.optimization_barrier((mg, *at_own, *at_peer, ff_keep, ff_send))
        hi, lo, v1 = local.ends(live, xc, cotc, mg, vecs, [dq0, dq1], w_att)
        ff_got, hi = lax.optimization_barrier((ff_got, hi))
        ff_keep, ff_send = z_second(ff_keep, ff_got)
        ff_got = swap(ff_send, "z", nz, 2)
        ax, ay, hi, ff_send = lax.optimization_barrier((ax, ay, hi, ff_send))
        up, ay, own_b, ax = second_leg(at_own, at_peer, ax, ay)
        v1, up, own_b, ff_keep, ff_send = lax.optimization_barrier((v1, up, own_b, ff_keep, ff_send))
        mine, other = pack(t.reshape(1).astype(jnp.int32), v1, v2, (db0, db1), (dba0, dba1), (drel0, drel1))
        ids = jnp.stack([c, y, z]).astype(jnp.int32)
        barrier = lambda *xs: lax.optimization_barrier(xs)
        ax, ay, mine, other = barrier(ax, ay, mine, other)
        keep, send = z_first(up, ay, own_b, ax)
        got = swap(send, "z", nz, 1)
        tiny_got = swap(other.astype(BF), "tensor", nt)
        ff_got, keep, send = barrier(ff_got, keep, send)
        ff = plus(ff_keep, ff_got)
        ff2 = swap(ff, "z", nz, 2)
        got, tiny_got, ff = barrier(got, tiny_got, ff)
        keep, send = z_second(keep, got)
        got = swap(send, "z", nz, 2)
        tiny = plus(mine, tiny_got)
        tiny_got = swap(tiny, "core", 2)
        ff2, send, tiny, tiny_got = barrier(ff2, send, tiny, tiny_got)
        ff = jnp.stack([ff, ff2])
        ff1 = swap(ff, "z", nz, 1)
        ffy, far = swap(ff, "y", 2), swap(ff, "core", 2)
        tiny = plus(tiny, tiny_got)
        tiny_got = swap(tiny, "y", 2)
        got, tiny, ff = barrier(got, tiny, ff)
        att = plus(keep, got)
        att_y = swap(att, "y", 2)
        att, att_y, tiny_got = barrier(att, att_y, tiny_got)
        att = jnp.stack([att, att_y])
        att2 = swap(att, "z", nz, 2)
        tiny = plus(tiny, tiny_got)
        tiny_got = swap(tiny, "z", nz, 1)
        att, hi = barrier(att, hi)
        input_grad = local.scatter(idx, hi, lo, cotangent)
        ff, ff1, ffy, far, tiny_got, input_grad, att2, att = barrier(ff, ff1, ffy, far, tiny_got, input_grad, att2, att)
        att = jnp.stack([att, att2])
        att1 = swap(att, "z", nz, 1)
        ffy1 = swap(ff1, "y", 2)
        tiny = plus(tiny, tiny_got)
        tiny_got = swap(tiny, "z", nz, 2)
        ff, ff1, att, tiny = barrier(ff, ff1, att, tiny)
        g_ff = place_feed(ids, ff, ff1, d, 4 * GW, 0, 0)
        ff1, ffy, att, tiny_got, *g_ff = barrier(ff1, ffy, att, tiny_got, *g_ff)
        far1, fary, att_far = swap(ff1, "core", 2), swap(ffy, "core", 2), swap(att, "core", 2)
        tiny = plus(tiny, tiny_got).astype(F32)
        gb_exp, gb_att = tiny[0], bias_grad(tiny[1, : 3 * GW])
        smalls = [tiny[2 + i, : d // 2] for i in range(6)]
        g_rel = tiny[8 : 8 + drel0.shape[0], :CODES]
        far, far1, gb_exp, gb_att, g_rel, g0, g1, *smalls = barrier(far, far1, gb_exp, gb_att, g_rel, *g_ff, *smalls)
        g_ff = place_feed(ids, far, far1, d, 4 * GW, 1, 0, (g0, g1))
        att_far, ffy1, fary, *g_ff = barrier(att_far, ffy1, fary, *g_ff)
        fary1 = swap(ffy1, "core", 2)
        g_at = place_attend(ids, att, att_far, d, 0)
        g_ff = place_feed(ids, ffy, ffy1, d, 4 * GW, 0, 1, g_ff)
        att1, fary1, g2, g3, *g_ff = barrier(att1, fary1, *g_at, *g_ff)
        att_far = swap(att1, "core", 2)
        g_exp, g_red = place_feed(ids, fary, fary1, d, 4 * GW, 1, 1, g_ff)
        g_att, g_out = place_attend(ids, att1, att_far, d, 1, (g2, g3))
        vectors = smalls
    else:
        *tiles, gb_exp, red, mg, ag, v2 = local.feed(second, branch, w_exp[0], w_red[0], b_exp[0], (live, middle, cotc, vecs, []))
        dq, ga, dba, drel = local.back(ag, *held[0], first, w_out[0])
        hi, lo, v1 = local.ends(live, xc, cotc, mg, vecs, [dq], w_att)
        result = local.result(idx, live, middle, vecs, patches, [red])
        input_grad = local.scatter(idx, hi, lo, cotangent)
        ff = jnp.concatenate(tiles, 0)
        g_exp = ff[:, 0:d].transpose(1, 0, 2).reshape(d, -1)
        g_red = ff[:, d:].transpose(0, 2, 1).reshape(-1, d)
        g_att = ga[0 : dq.shape[1] // GW, 0:d].transpose(1, 0, 2).reshape(d, -1)
        g_out = ga[dq.shape[1] // GW].reshape(2, d, d // 2).transpose(1, 0, 2).reshape(d, d)
        dp = ("z", "y", "core")

        def total(a, axis):
            a = lax.psum_scatter(a.astype(BF), "tensor", scatter_dimension=axis, tiled=True)
            return lax.psum(a, dp).astype(F32)

        vectors = total(jnp.stack([v1[0], v1[1], v2[2], v2[0], v2[1], v1[2]]), 1)
        gb_att, g_rel, gb_exp = total(bias_grad(dba), 0), total(drel[:, :CODES], 0), total(gb_exp[0], 0)
        g_exp, g_att, g_out, g_red = total(g_exp, 1), total(g_att, 1), total(g_out, 0), total(g_red, 0)

    return (
        result,
        input_grad,
        vectors[0],
        vectors[1],
        g_att,
        gb_att,
        g_rel,
        g_out,
        vectors[2],
        vectors[3],
        vectors[4],
        g_exp,
        gb_exp,
        g_red,
        vectors[5],
    )


def solution(mesh):
    nt = mesh.shape["tensor"]
    nz = mesh.shape["dp"] // 4
    grid = Mesh(mesh.devices.reshape(nz, 2, 2, nt), ("z", "y", "core", "tensor"))
    dp = ("z", "y", "core")
    rows = P(dp + ("tensor",), None)
    in_specs = (
        rows,
        P(),
        P(),
        P(None, "tensor"),
        P("tensor", None, None),
        P("tensor", None),
        P("tensor", None),
        P(),
        P(),
        P(),
        P(None, "tensor"),
        P("tensor"),
        P("tensor", None),
        P(),
        P(dp),
        rows,
    )
    out_specs = (
        rows,
        rows,
        P("tensor"),
        P("tensor"),
        P(None, "tensor"),
        P("tensor", None, None),
        P("tensor", None),
        P("tensor", None),
        P("tensor"),
        P("tensor"),
        P("tensor"),
        P(None, "tensor"),
        P("tensor"),
        P("tensor", None),
        P("tensor"),
    )
    return jax.shard_map(partial(on_device, nz, nt), mesh=grid, in_specs=in_specs, out_specs=out_specs, check_vma=False)
```

```python
from functools import partial

import jax
import jax.numpy as jnp
import numpy as np
from jax import lax
from jax.experimental import pallas as pl
from jax.experimental.pallas import tpu as pltpu
from jax.sharding import Mesh
from jax.sharding import PartitionSpec as P

HEAD_DIM = 32
EPSILON = 1e-05
MASKED = 30000.0
SIDE = 7
SLOTS = SIDE * SIDE
BLK = 128
GROUP = 4
GW = 3 * GROUP * HEAD_DIM
BF = jnp.bfloat16
F32 = jnp.float32
VMEM_LIMIT = 60 * 1024 * 1024


def dot(a, b):
    return jnp.dot(a, b, preferred_element_type=F32)


def dot_nt(a, b):
    return lax.dot_general(a, b, (((1,), (1,)), ((), ())), preferred_element_type=F32)


def dot_tn(a, b):
    return lax.dot_general(a, b, (((0,), (0,)), ((), ())), preferred_element_type=F32)


def kind_tables():
    slot = -np.ones((2, BLK), np.int64)
    owner = 100 + np.arange(BLK)[None].repeat(2, 0)
    nine = np.arange(9)
    nine = (nine // 3) * SIDE + nine % 3
    for w in range(2):
        slot[0, w * SLOTS : (w + 1) * SLOTS] = np.arange(SLOTS)
        owner[0, w * SLOTS : (w + 1) * SLOTS] = w
    for w in range(3):
        at = 2 * SLOTS + 9 * w
        slot[0, at : at + 9] = nine
        owner[0, at : at + 9] = 2 + w
    for w in range(14):
        slot[1, 9 * w : 9 * w + 9] = nine
        owner[1, 9 * w : 9 * w + 9] = w
    pick = (slot[:, :, None] == np.arange(64)[None, None, :]).astype(np.float32)
    same = owner[:, :, None] == owner[:, None, :]
    mask = np.where(same, 0.0, -1e30).astype(np.float32)
    return pick, mask


def stride_tables():
    slot, _ = kind_tables()
    s = np.where(slot.sum(2) > 0, slot.argmax(2), -1)
    place = np.where(s >= 0, 13 * (s // SIDE) + s % SIDE, -1)
    up = (place[:, :, None] == np.arange(BLK)).astype(np.float32)
    down = ((84 - place)[:, :, None] == np.arange(BLK)) & (place >= 0)[:, :, None]
    return up, down.astype(np.float32).transpose(0, 2, 1)


def group_perm():
    perm = np.zeros((GW, GW), np.float32)
    for h in range(GROUP):
        for p in range(3):
            for e in range(HEAD_DIM):
                perm[(h * 3 + p) * HEAD_DIM + e, (p * GROUP + h) * HEAD_DIM + e] = 1.0
    return perm


PLAN_HEAD = 8
G1, B1, G2, B2, OB, RB = (slice(i, i + 1) for i in range(6))
AT_C, AT_ME = 6, 7


def bound_kernel(w, bias, table, out):
    width = w.shape[1]
    q = jnp.zeros((1, BLK), F32)
    k = jnp.zeros((1, BLK), F32)
    for start in range(0, width, BLK):
        size = min(BLK, width - start)
        x = w[:, start : start + size]
        gram = dot_tn(x, x)
        a = lax.broadcasted_iota(jnp.int32, (size, size), 0) >> 5
        b = lax.broadcasted_iota(jnp.int32, (size, size), 1) >> 5
        sums = jnp.sum(jnp.where(a == b, gram * gram, 0.0), axis=0, keepdims=True)
        lane = lax.broadcasted_iota(jnp.int32, (1, size), 1) >> 5
        for i in range(size // HEAD_DIM):
            part = (start // HEAD_DIM + i) % 3
            top = jnp.max(jnp.where(lane == i, sums, 0.0), axis=1, keepdims=True)
            if part == 0:
                q = jnp.maximum(q, top)
            if part == 1:
                k = jnp.maximum(k, top)
    qb = bias[...].astype(F32)
    qb = jnp.max(jnp.sum(qb * qb, axis=2, keepdims=True), axis=0)
    qb = jnp.max(qb, axis=0, keepdims=True)
    top = jnp.max(jnp.max(jnp.abs(table[...].astype(F32)), axis=1, keepdims=True), axis=0, keepdims=True)
    out[...] = jnp.zeros_like(out)
    for i, v in enumerate((q, k, qb, top)):
        out[i : i + 1, :] = jnp.broadcast_to(v, (1, BLK))


def plan_kernel(windows, images, per_chunk, where, counts, bounds, vecs, out):
    d = vecs.shape[1]
    g1, b1 = vecs.at[G1], vecs.at[B1]
    big = bounds[...]

    def root4(v):
        return jnp.sqrt(jnp.sqrt(HEAD_DIM * v))

    reach = jnp.sqrt(float(d)) * jnp.max(jnp.abs(g1[...]), axis=1, keepdims=True)
    reach = 1.02 * (reach + jnp.sqrt(jnp.sum(b1[...] * b1[...], axis=1, keepdims=True)))
    q = 1.01 * (reach * root4(big[0:1, :]) + jnp.sqrt(big[2:3, :])) * HEAD_DIM**-0.5
    top = 1.01 * q * (reach * root4(big[1:2, :])) + big[3:4, :]
    safe = jnp.where(2.0 * top < MASKED - 500.0, 1, 0)
    bad = 1 - jnp.min(safe)
    first = where[0]
    nf = jnp.int32(0)
    nq = jnp.int32(0)
    for i in range(2 * windows + PLAN_HEAD, out.shape[0]):
        out[i] = 0
    for w in range(windows):
        place = first + w
        start = jnp.int32(0)
        offset = jnp.int32(-1)
        for i in range(images):
            total = counts[i] + 2
            inside = (place >= start) & (place < start + total)
            offset = jnp.where(inside, place - start, offset)
            start = start + total
        present = offset >= 0
        whole = present & (offset < 2)
        full = present & (whole | (bad > 0))
        part = present & (~whole) & (bad == 0)
        out[PLAN_HEAD + 2 * windows + w] = whole.astype(jnp.int32)

        @pl.when(full)
        def _():
            out[PLAN_HEAD + nf] = w

        @pl.when(part)
        def _():
            out[PLAN_HEAD + windows + nq] = w

        nf = nf + full.astype(jnp.int32)
        nq = nq + part.astype(jnp.int32)
    n0 = (nf + 1) >> 1
    left = jnp.maximum(nq - 3 * n0, 0)
    n1 = jnp.int32(0)
    for i in range(-(-windows // 14)):
        n1 = n1 + (left > 14 * i).astype(jnp.int32)
    nb = n0 + n1
    chunks = jnp.int32(1)
    for i in range(1, windows):
        chunks = chunks + (nb > per_chunk * i).astype(jnp.int32)
    for i, v in enumerate((nb, n0, chunks, bad, nf, nq, where[1], where[2])):
        out[i] = v


def norm_stats(x):
    mean = jnp.mean(x, axis=1, keepdims=True)
    c = x - mean
    scale = lax.rsqrt(jnp.mean(c * c, axis=1, keepdims=True) + EPSILON)
    return c * scale, scale


def norm_back(grad, normal, scale, gain):
    inner = grad * gain
    mean = jnp.mean(inner, axis=1, keepdims=True)
    proj = jnp.mean(inner * normal, axis=1, keepdims=True)
    return scale * (inner - mean - normal * proj)


def gather_kernel(windows, meta, slots, patches, cot, vecs, xc, cotc, branch, first, live, idx_row, idx, pick):
    rows = xc.shape[0]
    total = patches.shape[0]
    blocks = rows // BLK
    spots = lax.broadcasted_iota(jnp.int32, (BLK, total), 1)
    chunk = pl.program_id(0)
    n0 = meta[1]
    r = lax.broadcasted_iota(jnp.int32, (BLK, 1), 0)

    def listed(first_at, count, i):
        ok = (i >= 0) & (i < count)
        w = meta[first_at + jnp.where(ok, i, 0)]
        return jnp.where(ok, w, -1)

    def spread(ends, wins):
        base = jnp.full((BLK, 1), -1, jnp.int32)
        for end, w in reversed(list(zip(ends, wins))):
            base = jnp.where(r < end, w, base)
        return base

    def one(b, carry):
        at = pl.ds(pl.multiple_of(b * BLK, BLK), BLK)
        block = chunk * blocks + b
        kind0 = block < n0

        @pl.when(kind0)
        def _():
            wins = [listed(PLAN_HEAD, meta[4], 2 * block + i) for i in range(2)]
            wins += [listed(PLAN_HEAD + windows, meta[5], 3 * block + i) for i in range(3)]
            ends = [SLOTS, 2 * SLOTS] + [2 * SLOTS + 9 * (i + 1) for i in range(3)]
            base = spread(ends, wins)
            slot = slots[0]
            where_whole = [
                jnp.where(w >= 0, meta[PLAN_HEAD + 2 * windows + jnp.maximum(w, 0)], 0) for w in wins[:2]
            ] + [jnp.int32(1)] * 3
            sure = spread(ends, where_whole) > 0
            ok = base >= 0
            idx[...] = jnp.where(ok, base * SLOTS + slot, -1)
            live[at, :] = jnp.where(ok & (sure | (slots[2] > 0)), 1.0, 0.0)

        @pl.when(jnp.logical_not(kind0))
        def _():
            start = 3 * n0 + 14 * (block - n0)
            wins = [listed(PLAN_HEAD + windows, meta[5], start + i) for i in range(14)]
            base = spread([9 * (i + 1) for i in range(14)], wins)
            ok = base >= 0
            idx[...] = jnp.where(ok, base * SLOTS + slots[1], -1)
            live[at, :] = jnp.where(ok, 1.0, 0.0)

        here = idx[...]
        wide = jnp.broadcast_to(here.astype(F32), (BLK, BLK))
        idx_row[0, :, at] = wide.T[0:1, :].astype(jnp.int32)
        pick[at, :] = (spots == here).astype(F32).astype(BF)
        return carry

    lax.fori_loop(0, blocks, one, 0)
    x = dot(pick[...], patches[...])
    xc[...] = x.astype(BF)
    up = dot(pick[...], cot[...])
    cotc[...] = up.astype(BF)
    branch[...] = (up * live[...]).astype(BF)
    for b in range(blocks):
        at = slice(b * BLK, (b + 1) * BLK)
        n, _ = norm_stats(xc[at, :].astype(F32))
        first[at, :] = (n * vecs[G1] + vecs[B1]).astype(BF)


def lane_head(shape, axis):
    return lax.broadcasted_iota(jnp.int32, shape, axis) >> 5


def spread_rows(x):
    h = lane_head(x.shape, 1)
    zero = jnp.zeros_like(x)
    return jnp.concatenate([jnp.where(h == i, x, zero) for i in range(GROUP)], axis=0)


def spread_cols(xt):
    h = lane_head(xt.shape, 0)
    zero = jnp.zeros_like(xt)
    return jnp.concatenate([jnp.where(h == i, xt, zero) for i in range(GROUP)], axis=1)


def fold_rows(x):
    h = lane_head((BLK, BLK), 1)
    out = x[0:BLK]
    for i in range(1, GROUP):
        out = jnp.where(h == i, x[i * BLK : (i + 1) * BLK], out)
    return out


def run_copies(pairs, sem):
    copies = [pltpu.make_async_copy(x, y, sem.at[i]) for i, (x, y) in enumerate(pairs)]
    for x in copies:
        x.start()
    for x in copies:
        x.wait()


def attend_kernel(pieces, groups, tail, prior, meta, live, first, perm, pick, mask, bias, rel, *rest):
    w, rest = rest[:pieces], rest[pieces:]
    if tail:
        (xc, vecs), rest = rest[:2], rest[2:]
        before, rest = rest[:prior], rest[prior:]
        w_before, rest = rest[:prior], rest[prior:]
        w_out, rest = rest[:pieces], rest[pieces:]
    k = 3 + prior if tail else 2
    sources, rest = rest[:k], rest[k:]
    loaded = (live, first) + ((xc, *before) if tail else ())
    if tail:
        qkv_out, probs_out, mixed_out, middle_out, second_out, table, qkv, probs, mixed, in_sem, sem = rest[:11]
        middle, second, att = rest[11:]
    else:
        qkv_out, probs_out, mixed_out, table, qkv, probs, mixed, in_sem, sem = rest
    rows, d = first.shape
    blocks = rows // BLK
    step = pl.program_id(0)
    chunks = meta[2]
    c = meta[AT_C]
    n0 = meta[1]
    near = pl.ds(pl.multiple_of(c * (d // 2), BLK), d // 2)
    far = pl.ds(pl.multiple_of((1 - c) * (d // 2), BLK), d // 2)
    last = groups if tail else groups - 1

    def reload(chunk):
        @pl.when(chunks > 1)
        def _():
            at = pl.ds(pl.multiple_of(chunk * rows, rows), rows)
            run_copies([(x.at[at, :], y) for x, y in zip(sources, loaded)], in_sem)

    def stores(chunk, g):
        at = pl.ds(pl.multiple_of(chunk * rows, rows), rows)
        cols = pl.ds(pl.multiple_of(g * GW, BLK), GW)
        return (
            pltpu.make_async_copy(qkv, qkv_out.at[at, cols], sem.at[0]),
            pltpu.make_async_copy(probs, probs_out.at[pl.ds(chunk * blocks, blocks), g], sem.at[1]),
        )

    def group(i, carry):
        chunk = chunks - 1 - i
        reload(chunk)
        if pieces == 1:
            v = dot(first[...], w[0][...])
        else:
            v = dot(first[:, near], w[0][...]) + dot(first[:, far], w[1][...])
        v = v + bias[...]
        block = lax.broadcasted_iota(jnp.int32, (1, GW), 1) >> 5
        is_q = block == 0
        for j in range(3, 3 * GROUP, 3):
            is_q = is_q | (block == j)
        v = (v * jnp.where(is_q, HEAD_DIM**-0.5, 1.0)).astype(BF)

        @pl.when((step > 0) | (i > 0))
        def _():
            for x in stores(0, 0):
                x.wait()

        qkv[...] = dot(v, perm[...]).astype(BF)
        stores(chunk, step)[0].start()
        for b in range(blocks):
            at = slice(b * BLK, (b + 1) * BLK)
            kind = jnp.where(chunk * blocks + b < n0, 0, 1)
            q = qkv[at, 0:BLK]
            k = qkv[at, BLK : 2 * BLK]
            v = qkv[at, 2 * BLK : 3 * BLK]
            st = dot_nt(spread_rows(k), q) + table[kind].astype(F32)
            dead = (live[at, :] - 1.0) * MASKED
            st = st.reshape(GROUP, BLK, BLK) + jnp.where(meta[3] > 0, dead, 0.0)[None]
            peak = jnp.max(st, axis=1, keepdims=True)
            e = jnp.exp(st - peak)
            p = (e * (1.0 / jnp.sum(e, axis=1, keepdims=True))).astype(BF)
            p = p.reshape(GROUP * BLK, BLK)
            probs[b] = p
            vt = v.astype(F32).T.astype(BF)
            m = dot(spread_cols(vt), p).T.astype(BF)
            mixed[chunk, at, pl.ds(pl.multiple_of(step * BLK, BLK), BLK)] = m
        stores(chunk, step)[1].start()
        return carry

    @pl.when(step < groups)
    def _():
        places = []
        for h in range(GROUP):
            row = rel[pl.ds(step * GROUP + h, 1), :]
            row = pltpu.roll(jnp.broadcast_to(row, (BLK, 2 * BLK)), 2 * BLK - 88, 1, stride=1, stride_axis=0)
            places.append(row[:, 0:BLK].astype(BF))
        for kind in range(2):
            e = pick[kind]
            for h in range(GROUP):
                half = dot(e, places[h]).astype(BF)
                t = dot_nt(half, e) + mask[kind].astype(F32)
                table[kind, h * BLK : (h + 1) * BLK, :] = t.astype(BF)
        lax.fori_loop(0, chunks, group, 0)

    def project(i, carry):
        chunk = chunks - 1 - i
        reload(chunk)
        if pieces == 1:
            att[...] = dot(mixed[chunk], w_out[0][...])
        else:
            att[:, near] = dot(mixed[chunk], w_out[0][...])
            att[:, far] = dot(mixed[chunk], w_out[1][...])
        for m, v in zip(before, w_before):
            att[...] = att[...] + dot(m[...], v[...])
        for b in range(blocks):
            at = slice(b * BLK, (b + 1) * BLK)
            m = xc[at, :].astype(F32) + live[at, :] * (att[at, :] + vecs[OB])
            middle[at, :] = m
            nrm, _ = norm_stats(m)
            second[at, :] = (nrm * vecs[G2] + vecs[B2]).astype(BF)
        at = pl.ds(pl.multiple_of(chunk * rows, rows), rows)
        run_copies([(middle, middle_out.at[at, :]), (second, second_out.at[at, :])], in_sem)
        return carry

    def give(chunk):
        at = pl.ds(pl.multiple_of(chunk * rows, rows), rows)
        return pltpu.make_async_copy(mixed.at[chunk], mixed_out.at[at, :], sem.at[2])

    if tail:

        @pl.when(step == groups)
        def _():
            lax.fori_loop(0, chunks, project, 0)

    @pl.when(step == last)
    def _():
        for x in stores(0, 0):
            x.wait()

        def out(i, carry):
            give(i).start()
            give(i).wait()
            return carry

        lax.fori_loop(0, chunks, out, 0)


def feed_kernel(tiles, pieces, last, prior, meta, second, branch, *rest):
    we, wr, rest = rest[:pieces], rest[pieces : 2 * pieces], rest[2 * pieces :]
    be, rest = rest[0], rest[1:]
    if last:
        (live, middle, cotc, vecs), rest = rest[:4], rest[4:]
        sg_in, rest = rest[:prior], rest[prior:]
    grads, rest = rest[:tiles], rest[tiles:]
    dbe, red = rest[:2]
    if last:
        (mg, ag, vec), rest = rest[2:5], rest[5:]
    else:
        (sg,), rest = rest[2:3], rest[3:]
    sec, br, e_buf, r_buf, gbuf, ra, sa, half, sem, w_sem, g_sem = rest[:11]
    if last:
        mid_buf, cot_buf, live_buf, sg_buf = rest[11:]
    ch, d = sec.shape
    wide = e_buf.shape[2]
    c0, me = meta[AT_C], meta[AT_ME]
    y = me & 1
    chunks = meta[2]

    def move(a, b, i):
        return pltpu.make_async_copy(a, b, sem.at[i])

    def loads(c):
        rows = pl.ds(pl.multiple_of(c * ch, ch), ch)
        return [move(second.at[rows, :], sec, 0), move(branch.at[rows, :], br, 1)]

    def weights(i):
        if pieces == 1:
            at = pl.ds(pl.multiple_of((i ^ c0) * wide, BLK), wide)
            a, b = we[0].at[:, at], wr[0].at[at, :]
        else:
            a, b = we[i], wr[i]
        return [
            pltpu.make_async_copy(a, e_buf.at[i], w_sem.at[2 * i]),
            pltpu.make_async_copy(b, r_buf.at[i], w_sem.at[2 * i + 1]),
        ]

    def extras(c):
        rows = pl.ds(pl.multiple_of(c * ch, ch), ch)
        out = [
            move(middle.at[rows, :], mid_buf, 2),
            move(cotc.at[rows, :], cot_buf, 3),
            move(live.at[rows, :], live_buf, 4),
        ]
        return out + [move(x.at[rows, :], sg_buf, 5) for x in sg_in]

    def store(i):
        return pltpu.make_async_copy(gbuf.at[i], grads[i], g_sem.at[i])

    if last:
        vec[...] = jnp.zeros_like(vec)

    def chunk(c, carry):
        rows = pl.ds(pl.multiple_of(c * ch, ch), ch)
        for x in loads(c):
            x.start()

        @pl.when(c == 0)
        def _():
            for i in range(tiles):
                for x in weights(i):
                    x.start()

        if last:
            for x in extras(c):
                x.start()
        for x in loads(c):
            x.wait()

        def tile(t, carry):
            for i in range(tiles):

                @pl.when((t == i) & (c == 0))
                def _():
                    for x in weights(i):
                        x.wait()

            at = pl.ds(pl.multiple_of((t ^ c0) * wide, BLK), wide)
            e, r = e_buf[t], r_buf[t]
            u = dot(sec[...], e) + be[:, at]
            cdf = 0.5 * (1.0 + lax.erf(u * 0.7071067811865476))
            h = (u * cdf).astype(BF)
            slope = cdf + u * (jnp.exp(-0.5 * u * u) * 0.3989422804014327)
            pg = (dot_nt(br[...], r) * slope).astype(BF)
            grad_b = jnp.sum(pg.astype(F32), axis=0, keepdims=True)

            def put(low, g):
                n = wide // 2
                for i in range(2):
                    ref = gbuf.at[t, i ^ y, low : low + d, :]
                    part = g[:, i * n : (i + 1) * n]

                    @pl.when(c == 0)
                    def _():
                        ref[...] = part.astype(BF)

                    @pl.when(c > 0)
                    def _():
                        ref[...] = (ref[...].astype(F32) + part).astype(BF)

            put(0, dot_tn(sec[...], pg))
            put(d, dot_tn(br[...], h))

            @pl.when(c == 0)
            def _():
                dbe[:, at] = grad_b

            @pl.when(c > 0)
            def _():
                dbe[:, at] = dbe[:, at] + grad_b

            red_t = dot(h, r)
            sg_t = dot_nt(pg, e)

            @pl.when(t == 0)
            def _():
                ra[...] = red_t
                sa[...] = sg_t

            @pl.when(t > 0)
            def _():
                ra[...] = ra[...] + red_t
                sa[...] = sa[...] + sg_t

            for i in range(tiles):

                @pl.when((t == i) & (c == chunks - 1))
                def _():
                    store(i).start()

            return carry

        lax.fori_loop(0, tiles, tile, 0)
        half[0] = ra[...].astype(BF)
        outs = [move(half.at[0], red.at[rows, :], 0)]
        outs[0].start()
        if not last:
            half[1] = sa[...].astype(BF)
            outs.append(move(half.at[1], sg.at[rows, :], 1))
            outs[1].start()
        else:
            for x in extras(c):
                x.wait()
            for b in range(ch // BLK):
                at = slice(b * BLK, (b + 1) * BLK)
                nrm, scale = norm_stats(mid_buf[at, :])
                g = sa[at, :]
                if prior:
                    g = g + sg_buf[at, :].astype(F32)
                m = cot_buf[at, :].astype(F32) + norm_back(g, nrm, scale, vecs[G2])
                ra[at, :] = m
                kept = m * live_buf[at, :]
                half[1, at, :] = kept.astype(BF)
                vec[0:1, :] = vec[0:1, :] + jnp.sum(g * nrm, axis=0, keepdims=True)
                vec[1:2, :] = vec[1:2, :] + jnp.sum(g, axis=0, keepdims=True)
                vec[2:3, :] = vec[2:3, :] + jnp.sum(kept, axis=0, keepdims=True)
            outs += [move(half.at[1], ag.at[rows, :], 1), move(ra, mg.at[rows, :], 2)]
            for x in outs[1:]:
                x.start()
        for x in outs:
            x.wait()
        return carry

    lax.fori_loop(0, chunks, chunk, 0)
    for i in range(tiles):
        store(i).wait()


def back_kernel(pieces, groups, split, meta, ag, perm, pick, pick_t, qkv, probs, mixed, first, *rest):
    w_out, rest = rest[:pieces], rest[pieces:]
    sources, rest = rest[:5], rest[5:]
    dqkv, rest = rest[0], rest[1:]
    grads, rest = rest[: 2 if split else 1], rest[2 if split else 1 :]
    dba, drel, dperm, dmix, table, out, in_sem, sem = rest
    rows, d = ag.shape
    blocks = rows // BLK
    step = pl.program_id(0)
    chunks = meta[2]
    n0 = meta[1]
    c, me = meta[AT_C], meta[AT_ME]
    half = d // 2
    stays = (step >> 1) == (me >> 1)

    def reload(chunk):
        @pl.when(chunks > 1)
        def _():
            at = pl.ds(pl.multiple_of(chunk * rows, rows), rows)
            g = jnp.minimum(step, groups - 1)
            cols = pl.ds(pl.multiple_of(g * GW, BLK), GW)
            ag_h, qkv_h, probs_h, mixed_h, first_h = sources
            pairs = [(ag_h.at[at, :], ag), (qkv_h.at[at, cols], qkv), (mixed_h.at[at, :], mixed), (first_h.at[at, :], first)]
            pairs += [(probs_h.at[pl.ds(chunk * blocks, blocks), g], probs.at[:, 0])]
            run_copies(pairs, in_sem)

    def store(chunk, g):
        at = pl.ds(pl.multiple_of(chunk * rows, rows), rows)
        cols = pl.ds(pl.multiple_of(g * GW, BLK), GW)
        return pltpu.make_async_copy(out, dqkv.at[at, cols], sem.at[0])

    def put(i, ref, value):
        @pl.when(i == 0)
        def _():
            ref[...] = value.astype(ref.dtype)

        @pl.when(i > 0)
        def _():
            ref[...] = (ref[...].astype(F32) + value).astype(ref.dtype)

    def put_grad(i, low, high, value):
        if not split:
            put(i, grads[0].at[0, low:high, :], value)
            return

        @pl.when(stays)
        def _():
            put(i, grads[0].at[0, low:high, :], value)

        @pl.when(jnp.logical_not(stays))
        def _():
            put(i, grads[1].at[0, low:high, :], value)

    def weights(i, carry):
        reload(chunks - 1 - i)
        wide = groups * BLK
        for j in range(2):
            put_grad(i, j * wide, (j + 1) * wide, dot_tn(mixed[...], ag[:, j * half : (j + 1) * half]))
        return carry

    def heads(i, carry):
        chunk = chunks - 1 - i
        reload(chunk)
        if pieces == 1:
            dmix[...] = dot_nt(ag[...], w_out[0][...]).astype(BF)
        else:
            near = pl.ds(pl.multiple_of(c * half, BLK), half)
            far = pl.ds(pl.multiple_of((1 - c) * half, BLK), half)
            dmix[...] = (dot_nt(ag[:, near], w_out[0][...]) + dot_nt(ag[:, far], w_out[1][...])).astype(BF)
        for b in range(blocks):
            at = slice(b * BLK, (b + 1) * BLK)
            kind = jnp.where(chunk * blocks + b < n0, 0, 1)
            q = qkv[at, 0:BLK]
            k = qkv[at, BLK : 2 * BLK]
            v = qkv[at, 2 * BLK : 3 * BLK]
            do = dmix[at, :]
            p = probs[b, 0]
            dp = dot_nt(spread_rows(v), do).reshape(GROUP, BLK, BLK)
            pf = p.astype(F32).reshape(GROUP, BLK, BLK)
            x = pf * dp
            ds = x - pf * jnp.sum(x, axis=1, keepdims=True)
            ds = ds.astype(BF).reshape(GROUP * BLK, BLK)
            table[kind] = table[kind] + ds.astype(F32)
            dv = fold_rows(dot(p, do))
            dk = fold_rows(dot(ds, q))
            kt = k.astype(F32).T.astype(BF)
            dq = (dot(spread_cols(kt), ds) * HEAD_DIM**-0.5).T
            dperm[at, 0:BLK] = dq.astype(BF)
            dperm[at, BLK : 2 * BLK] = dk.astype(BF)
            dperm[at, 2 * BLK : 3 * BLK] = dv.astype(BF)
        x = dot_nt(dperm[...], perm[...]).astype(BF)

        @pl.when((step > 0) | (i > 0))
        def _():
            store(0, 0).wait()

        out[...] = x
        store(chunk, step).start()
        put_grad(i, 0, d, dot_tn(first[...], x))
        put(i, dba, jnp.sum(x.astype(F32), axis=0, keepdims=True))
        return carry

    @pl.when(step == groups)
    def _():
        lax.fori_loop(0, chunks, weights, 0)
        store(0, 0).wait()

    @pl.when(step < groups)
    def _():
        table[...] = jnp.zeros_like(table)
        lax.fori_loop(0, chunks, heads, 0)
        for h in range(GROUP):
            total = jnp.zeros((BLK, BLK), F32)
            for kind in range(2):
                a = table[kind, h * BLK : (h + 1) * BLK, :]
                a = dot(a.astype(BF), pick[kind]).astype(BF)
                total = total + dot(pick_t[kind], a)
            wide = jnp.concatenate([total, jnp.zeros_like(total)], axis=1)
            wide = pltpu.roll(wide, 0, 1, stride=1, stride_axis=0)
            drel[pl.ds(step * GROUP + h, 1), :] = jnp.sum(wide, axis=0, keepdims=True)


def row_tiles(rows, size=384):
    return [(a, min(size, rows - a)) for a in range(0, rows, size)]


def ends_kernel(pieces, meta, live, xc, cotc, mg, vecs, *rest):
    n = len(pieces)
    dqkv, rest = rest[:n], rest[n:]
    w = []
    for k in pieces:
        w.append(rest[:k])
        rest = rest[k:]
    hi, lo, vec, fg = rest
    rows, d = xc.shape
    blocks = rows // BLK
    chunk = pl.program_id(0)
    c = meta[AT_C]
    half = d // 2

    @pl.when(chunk == 0)
    def _():
        vec[...] = jnp.zeros_like(vec)

    for s in range(n):
        if len(w[s]) == 1:
            v = dot_nt(dqkv[s][...], w[s][0][...])
            fg[...] = v if s == 0 else fg[...] + v
        else:
            for i in range(2):
                cols = pl.ds(pl.multiple_of((c if i == 0 else 1 - c) * half, BLK), half)
                fg[:, cols] = fg[:, cols] + dot_nt(dqkv[s][...], w[s][i][...])

    for b in range(blocks):
        at = slice(b * BLK, (b + 1) * BLK)
        keep = live[at, :]
        nrm, scale = norm_stats(xc[at, :].astype(F32))
        g = fg[at, :]
        up = cotc[at, :].astype(F32)
        delta = mg[at, :] - up + norm_back(g, nrm, scale, vecs[G1])
        top = delta.astype(BF)
        hi[at, :] = top
        lo[at, :] = (delta - top.astype(F32)).astype(BF)
        vec[0:1, :] = vec[0:1, :] + jnp.sum(g * nrm, axis=0, keepdims=True)
        vec[1:2, :] = vec[1:2, :] + jnp.sum(g, axis=0, keepdims=True)
        vec[2:3, :] = vec[2:3, :] + jnp.sum(up * keep, axis=0, keepdims=True)


def result_kernel(prior, meta, idx, live, middle, vecs, patches, *rest):
    red, (result, res) = rest[:prior], rest[prior:]
    rows = middle.shape[0]
    chunk = pl.program_id(0)
    for b in range(rows // BLK):
        at = slice(b * BLK, (b + 1) * BLK)
        reduced = vecs[RB]
        for x in red:
            reduced = reduced + x[at, :].astype(F32)
        res[at, :] = (middle[at, :] + live[at, :] * reduced).astype(BF)
    for start, size in row_tiles(patches.shape[0]):
        at = slice(start, start + size)
        spots = start + lax.broadcasted_iota(jnp.int32, (size, rows), 0)
        hit = (spots == idx[0]).astype(F32)
        here = jnp.sum(hit, axis=1, keepdims=True) > 0.0
        new = dot(hit.astype(BF), res[...])

        @pl.when(chunk == 0)
        def _():
            result[at, :] = jnp.where(here, new, patches[at, :].astype(F32)).astype(BF)

        @pl.when(chunk > 0)
        def _():
            result[at, :] = jnp.where(here, new, result[at, :].astype(F32)).astype(BF)


def scatter_kernel(meta, idx, hi, lo, cot, input_grad):
    rows = hi.shape[0]
    chunk = pl.program_id(0)
    for start, size in row_tiles(cot.shape[0]):
        at = slice(start, start + size)
        spots = start + lax.broadcasted_iota(jnp.int32, (size, rows), 0)
        put = (spots == idx[0]).astype(F32).astype(BF)
        grad = dot(put, hi[...]) + dot(put, lo[...])

        @pl.when(chunk == 0)
        def _():
            input_grad[at, :] = cot[at, :].astype(F32) + grad

        @pl.when(chunk > 0)
        def _():
            input_grad[at, :] = input_grad[at, :] + grad


SMEM = pl.BlockSpec(memory_space=pltpu.SMEM)
ANY = pl.BlockSpec(memory_space=pl.ANY)
SHORT = pl.CostEstimate(flops=1000, bytes_accessed=1000, transcendentals=0)
PACK = 24


def pack_kernel(where, v1, v2, *refs):
    n = 2
    db, dba, drel = (refs[i * n : (i + 1) * n] for i in range(3))
    outs = refs[3 * n :]
    d = v1.shape[1]
    half = d // 2
    for s in range(n):
        t = where[0] if s == 0 else 1 - where[0]
        cols = pl.ds(pl.multiple_of(t * half, BLK), half)
        out = outs[s]
        out[...] = jnp.zeros_like(out)
        out[0:1, :] = db[s][...].astype(BF).astype(F32)
        out[1:2, 0 : dba[s].shape[1]] = dba[s][...]
        for i, (v, r) in enumerate(((v1, 0), (v1, 1), (v2, 2), (v2, 0), (v2, 1), (v1, 2))):
            out[2 + i : 3 + i, 0:half] = v[r : r + 1, cols]
        k = drel[s].shape[0]
        out[8 : 8 + k, 0 : drel[s].shape[1]] = drel[s][...]


def pack(t, v1, v2, db, dba, drel):
    v = pl.BlockSpec(memory_space=pltpu.VMEM)
    shape = sds((PACK, db[0].shape[1]), F32)
    return pl.pallas_call(
        pack_kernel,
        in_specs=[SMEM] + [v] * 8,
        out_specs=[v, v],
        out_shape=[shape, shape],
        cost_estimate=SHORT,
        name="pack",
    )(t, v1, v2, *db, *dba, *drel)


def unpack_kernel(a, b, *outs):
    x = a[...].astype(F32) + b[...].astype(F32)
    x = x.astype(BF).astype(F32)
    vectors, (exp, att, rel) = outs[:6], outs[6:]
    for i, v in enumerate(vectors):
        v[...] = x[2 + i, 0 : v.shape[0]]
    exp[...] = x[0]
    att[...] = x[1:2, 0 : att.shape[1]]
    rel[...] = x[8 : 8 + rel.shape[0], 0 : rel.shape[1]]


def unpack(a, b, half, hidden, width, heads):
    v = pl.BlockSpec(memory_space=pltpu.VMEM)
    shapes = [(half,)] * 6 + [(hidden,), (1, width), (heads, CODES)]
    return pl.pallas_call(
        unpack_kernel,
        in_specs=[v, v],
        out_specs=[v] * len(shapes),
        out_shape=[sds(x, F32) for x in shapes],
        cost_estimate=SHORT,
        name="unpack",
    )(a, b)


def place_feed_kernel(ids, e0, e1, r0, r1, *rest):
    exp, red = rest[-2:]
    low = ids[2] & 1
    exp[...] = jnp.where(low == 0, e0[0], e1[0]).astype(F32)
    red[...] = jnp.where(low == 1, r0[0], r1[0]).astype(F32).T


def place_feed(ids, near, far, d, hidden, other_core, other_y, onto=()):
    spec = pl.BlockSpec((1, GW, GW), lambda j, ids: (j ^ (ids[2] >> 1), 0, 0))
    tile = lambda ids: (ids[0] ^ other_core) * 2 + (ids[1] ^ other_y)
    return pl.pallas_call(
        place_feed_kernel,
        grid_spec=pltpu.PrefetchScalarGridSpec(
            num_scalar_prefetch=1,
            grid=(2,),
            in_specs=[spec] * 4 + [ANY] * len(onto),
            out_specs=[
                pl.BlockSpec((GW, GW), lambda j, ids: (j, tile(ids))),
                pl.BlockSpec((GW, GW), lambda j, ids: (tile(ids), j)),
            ],
        ),
        out_shape=[sds((d, hidden), F32), sds((hidden, d), F32)],
        input_output_aliases={5: 0, 6: 1} if onto else {},
        cost_estimate=SHORT,
        name="place_feed",
    )(ids, near, far, near, far, *onto)


def place_attend_kernel(ids, *refs):
    att, out = refs[-2:]
    for i in range(4):
        near, far = refs[i], refs[4 + i]
        x = jnp.where((i >> 1) == ids[0], near[0, 0], far[0, 0]).astype(F32)
        if i < 3:
            att[:, i * GW : (i + 1) * GW] = x
        else:
            out[...] = x


def place_attend(ids, near, far, d, other, onto=()):
    r = near.shape[2]
    ins = [
        pl.BlockSpec((1, 1, r, GW), lambda j, ids, i=i: (j ^ (ids[2] >> 1), (i & 1) ^ ids[1], 0, 0))
        for i in range(4)
    ]
    half = lambda ids: (ids[2] & 1) ^ other
    return pl.pallas_call(
        place_attend_kernel,
        grid_spec=pltpu.PrefetchScalarGridSpec(
            num_scalar_prefetch=1,
            grid=(2,),
            in_specs=ins + ins + [ANY] * len(onto),
            out_specs=[
                pl.BlockSpec((r, 3 * GW), lambda j, ids: (2 * half(ids) + j, 0)),
                pl.BlockSpec((r, GW), lambda j, ids: (j, half(ids))),
            ],
        ),
        out_shape=[sds((d, 3 * GW), F32), sds((GW, d), F32)],
        input_output_aliases={9: 0, 10: 1} if onto else {},
        cost_estimate=SHORT,
        name="place_attend",
    )(ids, near, near, near, near, far, far, far, far, *onto)


def guarded(body, axis):
    def run(meta, *refs):
        @pl.when(pl.program_id(axis) < meta[2])
        def _():
            body(meta, *refs)

    return run


def clamp(i, meta):
    return jnp.minimum(i, meta[2] - 1)


def whole_spec(shape):
    zeros = (0,) * len(shape)
    return pl.BlockSpec(shape, lambda *_: zeros, pipeline_mode=pl.Buffered(1))


def chunk_spec(shape):
    zeros = (0,) * (len(shape) - 1)
    return pl.BlockSpec(shape, lambda i, meta: (clamp(i, meta),) + zeros)


def sds(shape, dtype):
    return jax.ShapeDtypeStruct(shape, dtype)


def w_(a):
    return (a, whole_spec(a.shape))


def o_(shape, dtype):
    return (sds(shape, dtype), whole_spec(shape))


class Local:
    def __init__(self, rows):
        self.rows = rows
        self.windows = rows // SLOTS
        worst = (self.windows + 1) // 2
        self.per_chunk = min(5, max(worst, 1))
        self.chunks = -(-worst // self.per_chunk)
        self.ch = self.per_chunk * BLK
        self.all = self.ch * self.chunks
        pick, mask = kind_tables()
        self.mask = jnp.asarray(mask, BF)
        self.perm = jnp.asarray(group_perm(), BF)
        up, down_t = stride_tables()
        self.up, self.down_t = jnp.asarray(up, BF), jnp.asarray(down_t, BF)
        slot = np.where(pick.sum(2) > 0, pick.argmax(2), 0)
        corner = (slot[0] // SIDE < 3) & (slot[0] % SIDE < 3)
        self.slots = jnp.asarray(np.stack([slot[0], slot[1], corner])[:, :, None], jnp.int32)

    def row(self, k, dt):
        return (sds((self.all, k), dt), chunk_spec((self.ch, k)))

    def c(self, a):
        return (a, chunk_spec((self.ch,) + a.shape[1:]))

    def call(self, body, name, ins, outs, scratch=(), grid=None, axis=0, flops=0, size=0, limit=VMEM_LIMIT):
        f = pl.pallas_call(
            body if axis is None else guarded(body, axis),
            out_shape=[o for o, _ in outs],
            grid_spec=pltpu.PrefetchScalarGridSpec(
                num_scalar_prefetch=1,
                grid=(self.chunks,) if grid is None else grid,
                in_specs=[s for _, s in ins],
                out_specs=[s for _, s in outs],
                scratch_shapes=list(scratch),
            ),
            compiler_params=pltpu.CompilerParams(vmem_limit_bytes=limit),
            cost_estimate=pl.CostEstimate(flops=int(flops), bytes_accessed=int(size), transcendentals=0),
            name=name,
        )
        return f(self.meta, *[a for a, _ in ins])

    def bound(self, w, bias, table):
        ins = [w, bias, table]
        return pl.pallas_call(
            bound_kernel,
            out_shape=sds((8, BLK), F32),
            compiler_params=pltpu.CompilerParams(vmem_limit_bytes=VMEM_LIMIT),
            name="bound",
        )(*ins)

    def plan(self, place, counts, bounds, vecs):
        v = pl.BlockSpec(memory_space=pltpu.VMEM)
        self.meta = pl.pallas_call(
            partial(plan_kernel, self.windows, counts.shape[0], self.per_chunk),
            out_shape=sds((PLAN_HEAD + 3 * self.windows,), jnp.int32),
            in_specs=[SMEM, SMEM, v, v],
            out_specs=SMEM,
            name="plan",
        )(place, counts, bounds, vecs)

    def gather(self, patches, cot, vecs):
        ch, d = self.ch, patches.shape[1]
        idx = (sds((self.chunks, 1, ch), jnp.int32), pl.BlockSpec((1, 1, ch), lambda i, meta: (clamp(i, meta), 0, 0)))
        return self.call(
            partial(gather_kernel, self.windows),
            "gather_rows",
            [w_(self.slots), w_(patches), w_(cot), w_(vecs)],
            [self.row(d, BF)] * 4 + [self.row(1, F32), idx],
            [pltpu.VMEM((BLK, 1), jnp.int32), pltpu.VMEM((ch, self.rows), BF)],
            flops=4 * ch * self.rows * d,
            size=8 * self.rows * d,
        )

    def attend(self, live, first, bias, rel, w, tail=None, before=()):
        ch, d = self.ch, first.shape[1]
        width = w[0].shape[1]
        groups = width // GW
        clip = lambda g: jnp.minimum(g, groups - 1)
        block = lambda a: (a, pl.BlockSpec((ch,) + a.shape[1:], lambda g, meta: (0, 0), pipeline_mode=pl.Buffered(1)))
        cols = lambda a, k: (a, pl.BlockSpec((a.shape[0], k), lambda g, meta: (0, clip(g))))
        full = lambda k, dt: (sds((self.all, k), dt), ANY)
        pshape = (self.per_chunk * self.chunks, groups, GROUP * BLK, BLK)
        ins = [block(live), block(first), w_(self.perm), w_(self.up), w_(self.mask), cols(bias, GW), w_(rel)]
        ins += [cols(a, GW) for a in w]
        outs = [full(width, BF), (sds(pshape, BF), ANY), full(groups * BLK, BF)]
        v, dma = pltpu.VMEM, pltpu.SemaphoreType.DMA
        scratch = [v((2, GROUP * BLK, BLK), BF), v((ch, GW), BF), v((self.per_chunk, GROUP * BLK, BLK), BF)]
        scratch += [v((self.chunks, ch, groups * BLK), BF), dma((4,)), dma((3,))]
        steps = groups
        again = [live, first]
        if tail is not None:
            steps += 1
            xc, vecs, wo = tail
            ins += [block(xc), w_(vecs)]
            ins += [block(m) for m, _ in before] + [w_(a) for _, a in before] + [w_(a) for a in wo]
            again += [xc] + [m for m, _ in before]
            outs += [full(d, F32), full(d, BF)]
            scratch += [v((ch, d), F32), v((ch, d), BF), v((ch, d), F32)]
        ins += [(a, ANY) for a in again]
        return self.call(
            partial(attend_kernel, len(w), groups, tail is not None, len(before)),
            "attend",
            ins,
            outs,
            scratch,
            grid=(steps,),
            axis=None,
            flops=0.16 * ch * d * width,
            size=0.4 * ch * d,
        )

    def feed(self, second, branch, we, wr, be, last=None):
        ch, d = self.ch, second.shape[1]
        hidden = be.shape[1]
        pieces = len(we)
        wide = 2 * GW
        tiles = hidden // wide
        any_ = lambda a: (a, ANY)
        full = lambda dt: (sds((self.all, d), dt), ANY)
        ins = [any_(a) for a in (second, branch, *we, *wr)] + [w_(be)]
        outs = [(sds((2, 2 * d, GW), BF), ANY)] * tiles + [o_((1, hidden), F32), full(BF)]
        v = pltpu.VMEM
        scratch = [v((ch, d), BF)] * 2 + [v((tiles, d, wide), BF), v((tiles, wide, d), BF)]
        scratch += [v((tiles, 2, 2 * d, GW), BF), v((ch, d), F32), v((ch, d), F32), v((2, ch, d), BF)]
        dma = pltpu.SemaphoreType.DMA
        scratch += [dma((6,)), dma((2 * tiles,)), dma((tiles,))]
        prior = 0
        if last is None:
            outs += [full(BF)]
        else:
            live, middle, cotc, vecs, sums = last
            prior = len(sums)
            ins += [any_(live), any_(middle), any_(cotc), w_(vecs)] + [any_(a) for a in sums]
            outs += [full(F32), full(BF), o_((8, d), F32)]
            scratch += [v((ch, d), F32), v((ch, d), BF), v((ch, 1), F32), v((ch, d), BF)]
        return self.call(
            partial(feed_kernel, tiles, pieces, last is not None, prior),
            "feed",
            ins,
            outs,
            scratch,
            grid=(1,),
            axis=None,
            flops=12 * ch * d * hidden,
            size=8 * d * hidden,
        )

    def back(self, ag, qkv, probs, mixed, first, wo):
        ch, d = self.ch, first.shape[1]
        width = qkv.shape[1]
        groups = width // GW
        split = groups == 3
        clip = lambda g: jnp.minimum(g, groups - 1)
        block = lambda a: (a, pl.BlockSpec((ch,) + a.shape[1:], lambda g, meta: (0, 0), pipeline_mode=pl.Buffered(1)))
        cols = pl.BlockSpec((ch, GW), lambda g, meta: (0, clip(g)))
        pspec = pl.BlockSpec((self.per_chunk, 1) + probs.shape[2:], lambda g, meta: (0, clip(g), 0, 0))
        one = (1, 2 * groups * BLK, GW)
        if split:

            def tile(start):
                return lambda g, meta: (
                    (jnp.clip(g - start(meta[AT_ME] >> 1), 0, 1) ^ meta[AT_ME]) & 1,
                    0,
                    0,
                )

            shape = sds((2,) + one[1:], BF)
            grads = [(shape, pl.BlockSpec(one, tile(lambda h: 2 * h))), (shape, pl.BlockSpec(one, tile(lambda h: 2 - 2 * h)))]
        else:
            grads = [(sds((groups + 1,) + one[1:], BF), pl.BlockSpec(one, lambda g, meta: (g, 0, 0)))]
        v, dma = pltpu.VMEM, pltpu.SemaphoreType.DMA
        return self.call(
            partial(back_kernel, len(wo), groups, split),
            "back",
            [block(ag), w_(self.perm), w_(self.up), w_(self.down_t), (qkv, cols), (probs, pspec)]
            + [block(mixed), block(first)]
            + [(a, pl.BlockSpec((BLK, a.shape[1]), lambda g, meta: (clip(g), 0))) for a in wo]
            + [(a, ANY) for a in (ag, qkv, probs, mixed, first)],
            [(sds((self.all, width), BF), ANY), *grads]
            + [(sds((1, width), F32), pl.BlockSpec((1, GW), lambda g, meta: (0, clip(g))))]
            + [o_((groups * GROUP, 2 * BLK), F32)],
            [v((ch, GW), BF), v((ch, BLK), BF), v((2, GROUP * BLK, BLK), F32), v((ch, GW), BF), dma((5,)), dma((1,))],
            grid=(groups + 1,),
            axis=None,
            flops=14 * ch * d * width,
            size=30 * ch * d,
        )

    def ends(self, live, xc, cotc, mg, vecs, dqkv, ws):
        ch, d = self.ch, xc.shape[1]
        c = self.c
        return self.call(
            partial(ends_kernel, [len(a) for a in ws]),
            "ends",
            [c(live), c(xc), c(cotc), c(mg), w_(vecs)] + [c(a) for a in dqkv] + [w_(a) for s in ws for a in s],
            [self.row(d, BF)] * 2 + [o_((8, d), F32)],
            [pltpu.VMEM((ch, d), F32)],
            flops=6 * ch * d * d,
            size=30 * ch * d,
        )

    def by_row(self, idx):
        return (idx, pl.BlockSpec((1, 1, self.ch), lambda i, meta: (clamp(i, meta), 0, 0)))

    def result(self, idx, live, middle, vecs, patches, red):
        ch, d = self.ch, patches.shape[1]
        c = self.c
        (out,) = self.call(
            partial(result_kernel, len(red)),
            "result",
            [self.by_row(idx), c(live), c(middle), w_(vecs), w_(patches)] + [c(a) for a in red],
            [o_(patches.shape, BF)],
            [pltpu.VMEM((ch, d), BF)],
            flops=2 * ch * self.rows * d,
            size=12 * self.rows * d,
        )
        return out

    def scatter(self, idx, hi, lo, cot):
        ch, d = self.ch, cot.shape[1]
        (out,) = self.call(
            scatter_kernel,
            "scatter",
            [self.by_row(idx), self.c(hi), self.c(lo), w_(cot)],
            [o_(cot.shape, F32)],
            flops=4 * ch * self.rows * d,
            size=12 * self.rows * d,
        )
        return out


CODES = 169


def pad_table(table):
    return jnp.pad(table.astype(F32), ((0, 0), (4, 2 * BLK - CODES - 4)))


def bias_row(bias):
    b = bias.astype(F32)
    return jnp.stack([b[:, 0], jnp.zeros_like(b[:, 0]), b[:, 1]], axis=1).reshape(1, -1)


def pick_half(a, bit, axis=0):
    n = a.shape[axis] // 2
    return lax.dynamic_slice_in_dim(a, bit * n, n, axis)


def swap(a, axis, n, step=1):
    return lax.ppermute(a, axis, [(i, i ^ step) for i in range(n)])


def plus(*xs):
    total = xs[0].astype(F32)
    for x in xs[1:]:
        total = total + x.astype(F32)
    return total.astype(BF)


def after(x, *deps):
    return lax.optimization_barrier((x, *deps))[0]


def on_device(
    nz,
    nt,
    patches,
    gain_first,
    shift_first,
    attend_weight,
    attend_bias,
    offset_table,
    output_weight,
    output_bias,
    gain_second,
    shift_second,
    expand_weight,
    expand_bias,
    reduce_weight,
    reduce_bias,
    crop_counts,
    cotangent,
):
    fast = nt == 2 and nz == 4
    t, c, y, z = (lax.axis_index(a) for a in ("tensor", "core", "y", "z"))
    rows, d = patches.shape
    local = Local(rows)
    vec = lambda a: a.astype(F32).reshape(1, -1)
    vecs = jnp.stack([gain_first, shift_first, gain_second, shift_second, output_bias, reduce_bias]).astype(F32)
    bound = local.bound(attend_weight, attend_bias, offset_table)
    if fast:
        got, w_att_in, w_out_in = lax.optimization_barrier(
            (swap(bound, "tensor", nt), attend_weight, output_weight)
        )
        bound = jnp.maximum(bound, got)
        x_att = swap(pick_half(pick_half(w_att_in, c), y), "tensor", nt)
        x_out = swap(pick_half(w_out_in, c, 1), "tensor", nt)
        small = lambda a: [a, swap(a, "tensor", nt)]
        me = c * 2 + y
    else:
        w_att = [[lax.all_gather(attend_weight, "tensor", axis=1, tiled=True)]]
        w_out = [[lax.all_gather(output_weight, "tensor", axis=0, tiled=True)]]
        w_exp = [[lax.all_gather(expand_weight, "tensor", axis=1, tiled=True)]]
        w_red = [[lax.all_gather(reduce_weight, "tensor", axis=0, tiled=True)]]
        bound = lax.pmax(bound, "tensor")
        small = lambda a: [lax.all_gather(a, "tensor", axis=0, tiled=True)]
        me = c = 0 * c
    place = jnp.stack([t * local.windows, c, me]).astype(jnp.int32)
    local.plan(place, crop_counts, bound, vecs)
    bias, rel, b_exp = small(attend_bias), small(pad_table(offset_table)), small(expand_bias)
    xc, cotc, branch, first, live, idx = local.gather(patches, cotangent, vecs)

    if fast:
        xc, first, x_att, bias, rel, b_exp = lax.optimization_barrier((xc, first, x_att, bias, rel, b_exp))
    bias, b_exp = [bias_row(b) for b in bias], [vec(a) for a in b_exp]
    if fast:
        s_exp = after(pick_half(pick_half(expand_weight, c, 1), y, 1), x_att)
        first, s_exp = lax.optimization_barrier((first, s_exp))
        x_exp = swap(s_exp, "tensor", nt)
        y_att = swap(x_att, "y", 2)
        w_out = [[output_weight], [x_out, swap(x_out, "core", 2)]]
        qkv0, probs0, mixed0 = local.attend(live, first, bias[0], rel[0], [attend_weight])
        y_att, x_exp, x_out, mixed0 = lax.optimization_barrier((y_att, x_exp, x_out, mixed0))
        x_att = jnp.where(y == 0, jnp.concatenate([x_att, y_att], 0), jnp.concatenate([y_att, x_att], 0))
        w_att = [[attend_weight], [x_att, swap(x_att, "core", 2)]]
        y_exp = swap(x_exp, "y", 2)
        first, s_red = lax.optimization_barrier((first, after(pick_half(reduce_weight, c, 0), w_att[1][0])))
        x_red = swap(s_red, "tensor", nt)
        held = [(qkv0, probs0, mixed0)]
        before = [(mixed0, output_weight)]
    else:
        held, before = [], []
    qkv1, probs1, mixed1, middle, second = local.attend(
        live, first, bias[-1], rel[-1], w_att[-1], (xc, vecs, w_out[-1]), before
    )
    held.append((qkv1, probs1, mixed1))
    n = len(w_att)

    def bias_grad(a):
        a = a.reshape(-1, 3, HEAD_DIM)
        return jnp.stack([a[:, 0], a[:, 2]], axis=1)

    if fast:
        y_exp, x_red, second = lax.optimization_barrier((y_exp, x_red, second))
        x_exp = jnp.where(y == 0, jnp.concatenate([x_exp, y_exp], 1), jnp.concatenate([y_exp, x_exp], 1))
        second, x_exp = lax.optimization_barrier((second, x_exp))
        k0, s0, db0, red0, sg0 = local.feed(second, branch, [expand_weight], [reduce_weight], b_exp[0])
        e1 = [x_exp, swap(x_exp, "core", 2)]
        r1 = [x_red, swap(x_red, "core", 2)]
        k1, s1, db1, red1, mg, ag, v2 = local.feed(second, branch, e1, r1, b_exp[1], (live, middle, cotc, vecs, [sg0]))
        def split(keep, got):
            h = keep.shape[1] // 2
            return [plus(keep[:, i * h : (i + 1) * h], got[:, i * h : (i + 1) * h]) for i in range(2)]

        def first_leg(own, peer):
            return swap(peer[0], "tensor", nt), swap(jnp.stack([own[1][1], peer[1][1]]), "y", 2)

        def second_leg(own, peer, gx, gy):
            low = plus(own[0][1], gx[1])
            up = plus(own[0][0], gx[0])
            peer_b = plus(peer[1][0], gy[1])
            own_b = plus(own[1][0], gy[0])
            return up, swap(low, "y", 2), own_b, swap(peer_b, "tensor", nt)

        def z_first(up, gy, own_b, gx):
            a, b = plus(up, gy), plus(own_b, gx)
            return jnp.where(z % 2 == 0, a, b), jnp.where(z % 2 == 0, b, a)

        def z_second(keep, got):
            hi = z // 2
            total = lambda i: plus(pick_half(keep, i), pick_half(got, i))
            return total(hi), total(1 - hi)

        ff_peer = split(k1, swap(s1, "core", 2))
        ff_own = split(k0, swap(s0, "core", 2))
        ag, *ff = lax.optimization_barrier((ag, *ff_own, *ff_peer))
        ff_own, ff_peer = ff[:2], ff[2:]
        fx, fy = first_leg(ff_own, ff_peer)
        dq1, gk1, gs1, dba1, drel1 = local.back(ag, *held[1], first, w_out[1])
        dq1, gs1, red0 = lax.optimization_barrier((dq1, gs1, red0))
        got1 = swap(gs1, "core", 2)
        result = local.result(idx, live, middle, vecs, patches, [red0, red1])
        fx, fy, dq1, result, ag = lax.optimization_barrier((fx, fy, dq1, result, ag))
        ff_up, fy, ff_b, fx = second_leg(ff_own, ff_peer, fx, fy)
        dq0, gk0, gs0, dba0, drel0 = local.back(ag, *held[0], first, w_out[0])
        got1, fx, fy, dq0, gs0 = lax.optimization_barrier((got1, fx, fy, dq0, gs0))
        got0 = swap(gs0, "core", 2)
        ff_keep, ff_send = z_first(ff_up, fy, ff_b, fx)
        ff_got = swap(ff_send, "z", nz, 1)
        got1, got0, ff_keep, ff_send = lax.optimization_barrier((got1, got0, ff_keep, ff_send))
        at_peer = split(gk1, got1)
        at_own = split(gk0, got0)
        ax, ay = first_leg(at_own, at_peer)
        mg, *at4, ff_keep, ff_send = lax.optimization_barrier((mg, *at_own, *at_peer, ff_keep, ff_send))
        hi, lo, v1 = local.ends(live, xc, cotc, mg, vecs, [dq0, dq1], w_att)
        ff_got, hi = lax.optimization_barrier((ff_got, hi))
        ff_keep, ff_send = z_second(ff_keep, ff_got)
        ff_got = swap(ff_send, "z", nz, 2)
        ax, ay, hi, ff_send = lax.optimization_barrier((ax, ay, hi, ff_send))
        up, ay, own_b, ax = second_leg(at_own, at_peer, ax, ay)
        v1, up, own_b, ff_keep, ff_send = lax.optimization_barrier((v1, up, own_b, ff_keep, ff_send))
        mine, other = pack(t.reshape(1).astype(jnp.int32), v1, v2, (db0, db1), (dba0, dba1), (drel0, drel1))
        ids = jnp.stack([c, y, z]).astype(jnp.int32)
        barrier = lambda *xs: lax.optimization_barrier(xs)
        ax, ay, mine, other = barrier(ax, ay, mine, other)
        keep, send = z_first(up, ay, own_b, ax)
        got = swap(send, "z", nz, 1)
        tiny_got = swap(other.astype(BF), "tensor", nt)
        ff_got, keep, send = barrier(ff_got, keep, send)
        ff = plus(ff_keep, ff_got)
        ff2 = swap(ff, "z", nz, 2)
        got, tiny_got, ff = barrier(got, tiny_got, ff)
        keep, send = z_second(keep, got)
        got = swap(send, "z", nz, 2)
        tiny = plus(mine, tiny_got)
        tiny_got = swap(tiny, "core", 2)
        ff2, send, tiny, tiny_got = barrier(ff2, send, tiny, tiny_got)
        ff = jnp.stack([ff, ff2])
        ff1 = swap(ff, "z", nz, 1)
        ffy, far = swap(ff, "y", 2), swap(ff, "core", 2)
        tiny = plus(tiny, tiny_got)
        tiny_got = swap(tiny, "y", 2)
        got, tiny, ff = barrier(got, tiny, ff)
        att = plus(keep, got)
        att_y = swap(att, "y", 2)
        att, att_y, tiny_got = barrier(att, att_y, tiny_got)
        att = jnp.stack([att, att_y])
        att2 = swap(att, "z", nz, 2)
        tiny = plus(tiny, tiny_got)
        tiny_got = swap(tiny, "z", nz, 1)
        att, hi = barrier(att, hi)
        input_grad = local.scatter(idx, hi, lo, cotangent)
        ff, ff1, ffy, far, tiny_got, input_grad, att2, att = barrier(ff, ff1, ffy, far, tiny_got, input_grad, att2, att)
        att = jnp.stack([att, att2])
        att1 = swap(att, "z", nz, 1)
        ffy1 = swap(ff1, "y", 2)
        tiny = plus(tiny, tiny_got)
        tiny_got = swap(tiny, "z", nz, 2)
        ff, ff1, att, tiny = barrier(ff, ff1, att, tiny)
        g_ff = place_feed(ids, ff, ff1, d, 4 * GW, 0, 0)
        ff1, ffy, att, tiny_got, *g_ff = barrier(ff1, ffy, att, tiny_got, *g_ff)
        far1, fary, att_far = swap(ff1, "core", 2), swap(ffy, "core", 2), swap(att, "core", 2)
        *smalls, gb_exp, gb_att, g_rel = unpack(tiny, tiny_got, d // 2, 4 * GW, 3 * GW, drel0.shape[0])
        gb_att = bias_grad(gb_att)
        far, far1, ffy1, gb_exp, gb_att, g_rel, g0, g1, *smalls = barrier(
            far, far1, ffy1, gb_exp, gb_att, g_rel, *g_ff, *smalls
        )
        g_ff = place_feed(ids, far, far1, d, 4 * GW, 1, 0, (g0, g1))
        att_far, ffy1, fary, *g_ff = barrier(att_far, ffy1, fary, *g_ff)
        fary1 = swap(ffy1, "core", 2)
        g_at = place_attend(ids, att, att_far, d, 0)
        g_ff = place_feed(ids, ffy, ffy1, d, 4 * GW, 0, 1, g_ff)
        att1, fary1, g2, g3, *g_ff = barrier(att1, fary1, *g_at, *g_ff)
        att_far = swap(att1, "core", 2)
        g_exp, g_red = place_feed(ids, fary, fary1, d, 4 * GW, 1, 1, g_ff)
        g_att, g_out = place_attend(ids, att1, att_far, d, 1, (g2, g3))
        vectors = smalls
    else:
        *tiles, gb_exp, red, mg, ag, v2 = local.feed(second, branch, w_exp[0], w_red[0], b_exp[0], (live, middle, cotc, vecs, []))
        dq, ga, dba, drel = local.back(ag, *held[0], first, w_out[0])
        hi, lo, v1 = local.ends(live, xc, cotc, mg, vecs, [dq], w_att)
        result = local.result(idx, live, middle, vecs, patches, [red])
        input_grad = local.scatter(idx, hi, lo, cotangent)
        ff = jnp.concatenate(tiles, 0)
        g_exp = ff[:, 0:d].transpose(1, 0, 2).reshape(d, -1)
        g_red = ff[:, d:].transpose(0, 2, 1).reshape(-1, d)
        g_att = ga[0 : dq.shape[1] // GW, 0:d].transpose(1, 0, 2).reshape(d, -1)
        g_out = ga[dq.shape[1] // GW].reshape(2, d, d // 2).transpose(1, 0, 2).reshape(d, d)
        dp = ("z", "y", "core")

        def total(a, axis):
            a = lax.psum_scatter(a.astype(BF), "tensor", scatter_dimension=axis, tiled=True)
            return lax.psum(a, dp).astype(F32)

        vectors = total(jnp.stack([v1[0], v1[1], v2[2], v2[0], v2[1], v1[2]]), 1)
        gb_att, g_rel, gb_exp = total(bias_grad(dba), 0), total(drel[:, :CODES], 0), total(gb_exp[0], 0)
        g_exp, g_att, g_out, g_red = total(g_exp, 1), total(g_att, 1), total(g_out, 0), total(g_red, 0)

    return (
        result,
        input_grad,
        vectors[0],
        vectors[1],
        g_att,
        gb_att,
        g_rel,
        g_out,
        vectors[2],
        vectors[3],
        vectors[4],
        g_exp,
        gb_exp,
        g_red,
        vectors[5],
    )


def solution(mesh):
    nt = mesh.shape["tensor"]
    nz = mesh.shape["dp"] // 4
    grid = Mesh(mesh.devices.reshape(nz, 2, 2, nt), ("z", "y", "core", "tensor"))
    dp = ("z", "y", "core")
    rows = P(dp + ("tensor",), None)
    in_specs = (
        rows,
        P(),
        P(),
        P(None, "tensor"),
        P("tensor", None, None),
        P("tensor", None),
        P("tensor", None),
        P(),
        P(),
        P(),
        P(None, "tensor"),
        P("tensor"),
        P("tensor", None),
        P(),
        P(dp),
        rows,
    )
    out_specs = (
        rows,
        rows,
        P("tensor"),
        P("tensor"),
        P(None, "tensor"),
        P("tensor", None, None),
        P("tensor", None),
        P("tensor", None),
        P("tensor"),
        P("tensor"),
        P("tensor"),
        P(None, "tensor"),
        P("tensor"),
        P("tensor", None),
        P("tensor"),
    )
    return jax.shard_map(partial(on_device, nz, nt), mesh=grid, in_specs=in_specs, out_specs=out_specs, check_vma=False)
```
